32 devices in a mesh: cuts: 2 (over core), lx: 2 (over x), ly: 8 (over z, y).
Axes of the slice: x: 2, y: 2, z: 4, core: 2. Of those that a mesh axis runs over, the one named last changes fastest.
Arguments:
- disorder: int32 [16, 16, 128], P('lx', 'ly'), may hold values from 0 to 255
- slice_bounds: float32 [12, 2], P('cuts'), may hold values from -1.5 to 1.5
- start: float32 [12, 32, 16, 16, 128], P('cuts', None, 'lx', 'ly'), may hold values from -36 to 36
- ritz: float32 [12, 8, 16, 16, 128], P('cuts', None, 'lx', 'ly'), may hold values from -4 to 4
Outputs:
- block: float32 [12, 32, 16, 16, 128], P('cuts', None, 'lx', 'ly')
- correlations: float32 [12, 16, 32], P('cuts')
The draws below stay inside these ranges and needn't reach their ends.
All inputs are finite; a program needn't handle non-finite values.
Results may differ from the reference program's by a relative error of at most 0.000096.
Values sent between devices are 32-bit elements; how exact they have to be, the bound alone decides.
A program may use at most 64 MiB of HBM per device.

```python
import jax
import jax.numpy as jnp
from jax import lax

NV = 32
RITZ = 8
DEG = 2
LEVELS = 256
NZ = 128
SLICES = 12
NX = 16
NY = 16


def ritz_field(key):
    shape = (SLICES, RITZ, NX, NY, NZ)
    values = jnp.clip(jax.random.normal(jax.random.fold_in(key, 7), shape, jnp.float32), -4.0, 4.0)
    return values


def draw_ritz(key, part):
    return ritz_field(key)


def draw_start(key, part):
    ritz_all = ritz_field(key)
    empty = jnp.zeros((1, RITZ, NX, NY, NZ), jnp.float32)
    lower = jnp.concatenate([empty, ritz_all[:-1]], 0)
    upper = jnp.concatenate([ritz_all[1:], empty], 0)
    window = jnp.concatenate([lower, upper], 1)
    shape = (SLICES, NV, NX, NY, NZ)
    noise = jnp.clip(jax.random.normal(jax.random.fold_in(key, 11), shape, jnp.float32), -4.0, 4.0)
    weights = jax.random.uniform(jax.random.fold_in(key, 13), (SLICES, NV, 2 * RITZ), jnp.float32, -1.0, 1.0)

    def drawn_slice(items):
        window_one = items[0]
        weight_one = items[1]
        planted = jnp.zeros((NV, NX, NY, NZ), jnp.float32)
        for column in range(2 * RITZ):
            planted = planted + weight_one[:, column][:, None, None, None] * window_one[column][None]
        return planted
    planted_all = lax.map(drawn_slice, (window, weights))
    return noise + 0.5 * planted_all


def set_ends(entries, rng, low, largest):
    shape = entries.shape
    spot = [jax.random.randint(jax.random.fold_in(rng, axis), (), 0, shape[axis]) for axis in range(len(shape))]
    entries = entries.at[tuple(spot)].set(low)
    longest = shape.index(max(shape))
    spot[longest] = (spot[longest] + 1) % shape[longest]
    return entries.at[tuple(spot)].set(largest)


def steps_of(stream_key, extent, shards, least, top_value):
    def one(axis_at, blocks):
        draws = jax.random.uniform(jax.random.fold_in(jax.random.fold_in(stream_key, 6), axis_at), (blocks,), jnp.float32, least / len(shards), top_value / len(shards))
        return jnp.repeat(jnp.exp(draws), extent[axis_at] // blocks).reshape((-1,) + (1,) * (len(extent) - axis_at - 1))

    level = one(*shards[0])
    for cut in shards[1:]:
        level = level * one(*cut)
    return level


def setup_inputs(seed: int = 0) -> dict:
    streams_of = jax.random.split(jax.random.key(seed), 5)
    return {
        "disorder": set_ends(jax.random.randint(streams_of[0], (NX, NY, NZ), 0, LEVELS), jax.random.fold_in(streams_of[0], 1), 0, LEVELS - 1).astype(jnp.int32),
        "slice_bounds": jnp.clip(jax.random.uniform(streams_of[1], (SLICES, 2), jnp.float32, -1.5, 1.5) * steps_of(streams_of[1], (SLICES, 2), ((0, 2),), -0.4, 0.0), -1.5, 1.5),
        "start": draw_start(jax.random.fold_in(streams_of[4], 71), 0),
        "ritz": draw_ritz(jax.random.fold_in(streams_of[4], 71), 0),
    }


def scaled_operator(field, onsite, centre):
    beside = jnp.roll(field, 1, 1) + jnp.roll(field, -1, 1)
    beside = beside + jnp.roll(field, 1, 2) + jnp.roll(field, -1, 2)
    beside = beside + jnp.roll(field, 1, 3) + jnp.roll(field, -1, 3)
    return ((onsite[None] - centre) * field - beside) / 16.0

def one_slice(onsite, bounds, vectors, lower, upper):
    centre = (bounds[0] + bounds[1]) / 2.0
    previous = vectors
    current = scaled_operator(vectors, onsite, centre)
    for step in range(DEG - 1):
        previous, current = (current, 2.0 * scaled_operator(current, onsite, centre) - previous)
    cells = NX * NY * NZ
    hp = lax.Precision.HIGHEST
    filtered = current.reshape(NV, cells)
    window = jnp.concatenate([lower, upper], 0).reshape(2 * RITZ, cells)
    correlation = jnp.einsum('rc,vc->rv', window, filtered, precision=hp) / jnp.float32(cells)
    cleaned = filtered - jnp.einsum('rv,rc->vc', correlation, window, precision=hp)
    gram = jnp.einsum('ac,bc->ab', cleaned, cleaned, precision=hp) / jnp.float32(cells)
    factor = jnp.linalg.cholesky(gram)
    result = jax.scipy.linalg.solve_triangular(factor, cleaned, lower=True)
    return (result.reshape(NV, NX, NY, NZ), correlation)

def reference(disorder, slice_bounds, start, ritz):
    onsite = 16.5 * (disorder.astype(jnp.float32) / jnp.float32(LEVELS - 1) - 0.5)
    empty = jnp.zeros((1, RITZ, NX, NY, NZ), jnp.float32)
    lower = jnp.concatenate([empty, ritz[:-1]], 0)
    upper = jnp.concatenate([ritz[1:], empty], 0)

    def run(items):
        return one_slice(onsite, items[0], items[1], items[2], items[3])
    block, correlations = lax.map(run, (slice_bounds, start, lower, upper))
    return (block, correlations)
```

```python
import functools

import jax
import jax.numpy as jnp
from jax import lax
from jax.experimental import pallas as pl
from jax.experimental.pallas import tpu as pltpu
from jax.sharding import PartitionSpec as P

LEVELS = 256
MESH = pl.DeviceIdType.MESH
HP = lax.Precision.HIGHEST
H = 2
BF = jnp.bfloat16
F32 = jnp.float32
NT = (((1,), (1,)), ((), ()))
NN = (((1,), (0,)), ((), ()))
TN = (((0,), (0,)), ((), ()))


def sem_counts(nx, K, S):
    groups = 2
    one = 4 + S * 13 + 2 + (S + 2) + S
    return one + groups * (nx + K)


def split(z):
    hi = z.astype(BF)
    return hi, (z - hi.astype(F32)).astype(BF)


def kernel(dims, dis_h, bnd, start_h, ritz_h, out, cor, dis, start, ritz, ls, E, T, O, U, FA, FT, RA, RQ,
           PK, RX, SM, RZ, LM, LP, LR, ss, rs):
    nc, nx, ny, count, NV, NR, X, Y, NZ = dims
    S = count // 2
    R = 2 * Y
    J = X * Y
    K = ny // 2
    total = float(J * NZ * nx * ny)
    NW = 2 * NR
    NB = NV + NW
    cut, mx, my = lax.axis_index("cuts"), lax.axis_index("lx"), lax.axis_index("ly")
    p = lax.rem(my, 2)
    q = 1 - p
    kz = my // 2
    yp = (cut, mx, kz * 2 + q)
    zup = (cut, mx, lax.rem(kz + 1, K) * 2 + p)
    zdown = (cut, mx, lax.rem(kz + K - 1, K) * 2 + p)
    xup = (cut, lax.rem(mx + 1, nx), my)
    xdown = (cut, lax.rem(mx + nx - 1, nx), my)
    cup = (lax.rem(cut + 1, nc), mx, my)
    cdown = (lax.rem(cut + nc - 1, nc), mx, my)

    def load(src, dst, i):
        copy = pltpu.make_async_copy(src, dst, ls.at[i])
        copy.start()
        return copy

    level_load = load(dis_h, dis, 2 * S)
    away, kept = [], []
    for c in range(S):
        away.append(load(start_h.at[q * S + c], start.at[c], c))
        kept.append(load(start_h.at[p * S + c], start.at[S + c], S + c))
    ritz_load = load(ritz_h, ritz, 2 * S + 1)
    barrier = pltpu.get_barrier_semaphore()

    def greet(dev):
        pl.semaphore_signal(barrier, inc=1, device_id=dev, device_id_type=MESH)

    greet(yp)
    for o in range(1, nx):
        greet((cut, lax.rem(mx + o, nx), my))
    for o in range(1, K):
        greet((cut, mx, lax.rem(kz + o, K) * 2 + p))
    greet(cup)
    greet(cdown)

    lo = H + Y * p
    lq = H + Y * q
    xi = pl.ds(H, X)
    level_load.wait()
    for x in range(X):
        for r in range(Y):
            row = dis[pl.ds(x * Y + r, 1), :].astype(F32)
            O[H + x, lo + r] = 16.5 * (row / F32(LEVELS - 1) - 0.5)

    def stage_away(c):
        away[c].wait()
        for x in range(X):
            for r in range(Y):
                T[c, x, r] = start[c, pl.ds(x * Y + r, NV, stride=J), :]

    def stage_kept(c):
        kept[c].wait()
        for x in range(X):
            for r in range(Y):
                E[c, H + x, lo + r] = start[S + c, pl.ds(x * Y + r, NV, stride=J), :]

    pending = []
    used = [0]

    def slots(n=1):
        i = used[0]
        used[0] += n
        return i

    def send(src, dst, i, j, dev):
        copy = pltpu.make_async_remote_copy(
            src_ref=src, dst_ref=dst, send_sem=ss.at[i], recv_sem=rs.at[j], device_id=dev, device_id_type=MESH)
        copy.start()
        pending.append(copy)

    def arrived(dst, j):
        pltpu.make_async_remote_copy(
            src_ref=dst, dst_ref=dst, send_sem=rs.at[j], recv_sem=rs.at[j],
            device_id=yp, device_id_type=MESH).wait_recv()

    def rows(at):
        return pl.ds(at, Y)

    o_y, o_z, o_x = slots(), slots(2), slots(2)
    y_at = [slots() for _ in range(S)]
    z_at = [slots(2) for _ in range(S)]
    xo_at = [slots(2) for _ in range(S)]
    xp_at = [slots(2) for _ in range(S)]
    k_at = [slots(4) for _ in range(S)]
    f_at = [slots() for _ in range(S)]
    l_at = [slots() for _ in range(S)]
    c_at = slots(2)
    r_at = slots(S + 2)
    groups = [list(range(S - 1)), [S - 1]]
    ax_at = [slots(nx) for _ in groups]
    az_at = [slots(K) for _ in groups]

    def send_y(c):
        send(T.at[c], E.at[c, xi, rows(lo)], y_at[c], y_at[c], yp)

    def send_z(c, half):
        side = 1 - half
        dev = (cut, mx, jnp.where(half == 1, zup[2], zdown[2]))
        dst = jnp.where(half == 1, 0, H + R)
        send(E.at[c, xi, rows(H + Y * half)], E.at[c, xi, rows(dst)], z_at[c] + side, z_at[c] + side, dev)

    def send_x(c, base, at):
        send(E.at[c, pl.ds(X, H), rows(at)], E.at[c, pl.ds(0, H), rows(at)], base, base, xup)
        send(E.at[c, pl.ds(H, H), rows(at)], E.at[c, pl.ds(H + X, H), rows(at)], base + 1, base + 1, xdown)

    def got_x(c, base, at):
        arrived(E.at[c, pl.ds(0, H), rows(at)], base)
        arrived(E.at[c, pl.ds(H + X, H), rows(at)], base + 1)

    def send_o(half):
        side = 1 - half
        dev = (cut, mx, jnp.where(half == 1, zup[2], zdown[2]))
        src = jnp.where(half == 1, H + R - 1, H)
        dst = jnp.where(half == 1, 1, H + R)
        send(O.at[xi, src], O.at[xi, dst], o_z + side, o_z + side, dev)

    stage_away(0)
    stage_kept(0)
    pl.semaphore_wait(barrier, nx + K + 1)
    send(O.at[xi, rows(lo)], O.at[xi, rows(lo)], o_y, o_y, yp)
    send_y(0)
    send_o(p)
    send_z(0, p)
    send_x(0, xo_at[0], lo)
    for c in range(1, S):
        stage_away(c)
        send_y(c)
        stage_kept(c)
        if c < S - 1:
            send_z(c, p)
        send_x(c, xo_at[c], lo)
    ritz_load.wait()
    for s in range(count):
        for x in range(X):
            for r in range(Y):
                RA[s + 1, x, r] = ritz[s, pl.ds(x * Y + r, NR, stride=J), :]
    send(RA.at[count], RA.at[0], c_at, c_at, cup)
    send(RA.at[1], RA.at[count + 1], c_at + 1, c_at + 1, cdown)

    own = pl.ds(H, R)
    arrived(O.at[xi, rows(lq)], o_y)
    send_o(q)
    send(O.at[H + X - 1, own], O.at[H - 1, own], o_x, o_x, xup)
    send(O.at[H, own], O.at[H + X, own], o_x + 1, o_x + 1, xdown)

    arrived(RA.at[0], c_at)
    arrived(RA.at[count + 1], c_at + 1)

    @pl.when(cut == 0)
    def _():
        RA[0] = jnp.zeros((X, Y, NR, NZ), F32)

    @pl.when(cut == nc - 1)
    def _():
        RA[count + 1] = jnp.zeros((X, Y, NR, NZ), F32)

    order = []
    for c in range(S):
        for j in (c, c + 2):
            if j not in order:
                order.append(j)
    for j in order:
        send(RA.at[q * S + j], RQ.at[j], r_at + j, r_at + j, yp)

    for c in range(S):
        arrived(E.at[c, xi, rows(lq)], y_at[c])
        send_z(c, q)
        send_x(c, xp_at[c], lq)
        if c == 0:
            send_z(S - 1, p)

    arrived(O.at[xi, H - 1], o_z)
    arrived(O.at[xi, H + R], o_z + 1)
    arrived(O.at[H - 1, own], o_x)
    arrived(O.at[H + X, own], o_x + 1)

    def point(src, x, r, centre):
        v = src(x, r)
        beside = src(x + 1, r) + src(x - 1, r)
        beside = beside + src(x, r + 1) + src(x, r - 1)
        beside = beside + pltpu.roll(v, 1, 1) + pltpu.roll(v, NZ - 1, 1)
        level = jnp.broadcast_to(O[x, r] - centre, (NV, NZ))
        return (level * v - beside) * 0.0625

    def apply(c):
        s = p * S + c
        centre = (bnd[0, s] + bnd[1, s]) / 2.0
        got_x(c, xo_at[c], lo)
        got_x(c, xp_at[c], lq)
        for early in (1, 0):
            side = q if early else p
            row = jnp.where(side == 1, H + R, H - 1)
            arrived(E.at[c, xi, rows(jnp.where(side == 1, H + R, 0))], z_at[c] + side)
            k = k_at[c] + 2 * side
            send(E.at[c, H + X - 1, row], E.at[c, H - 1, row], k, k, xup)
            send(E.at[c, H, row], E.at[c, H + X, row], k + 1, k + 1, xdown)

        def from_e(x, r):
            return E[c, x, r]

        def from_u(x, r):
            return U[x, r]

        def first(i, carry):
            for r in range(H - 1, H + R + 1):
                U[H + 1 + i, r] = point(from_e, H + 1 + i, r, centre)
            return carry

        lax.fori_loop(0, X - 2, first, 0)
        for x in (H, H + X - 1):
            for r in range(H, H + R):
                U[x, r] = point(from_e, x, r, centre)
        for x in (H - 1, H + X):
            for r in range(H + 1, H + R - 1):
                U[x, r] = point(from_e, x, r, centre)
        for side, row in ((0, H - 1), (1, H + R)):
            arrived(E.at[c, H - 1, row], k_at[c] + 2 * side)
            arrived(E.at[c, H + X, row], k_at[c] + 2 * side + 1)
        for x in (H, H + X - 1):
            for r in (H - 1, H + R):
                U[x, r] = point(from_e, x, r, centre)
        for x in (H - 1, H + X):
            for r in (H, H + R - 1):
                U[x, r] = point(from_e, x, r, centre)

        def second(i, carry):
            for r in range(Y):
                FT[c, i, r] = 2.0 * point(from_u, H + i, lq + r, centre) - E[c, H + i, lq + r]
                FA[s, i, r] = 2.0 * point(from_u, H + i, lo + r, centre) - E[c, H + i, lo + r]
            return carry

        lax.fori_loop(0, X, second, 0)
        send(FT.at[c], FA.at[s], f_at[c], f_at[c], yp)

    def gram(c):
        s = p * S + c
        arrived(RQ.at[c], r_at + c) if c < 2 else None
        arrived(RQ.at[c + 2], r_at + c + 2)

        def body(i, carry):
            a, b = carry
            for k in range(2):
                if k == 0:
                    z = [jnp.concatenate([FA[s, i, r], RA[s, i, r], RA[s + 2, i, r]], 0) for r in range(Y)]
                else:
                    z = [jnp.concatenate([FT[c, i, r], RQ[c, i, r], RQ[c + 2, i, r]], 0) for r in range(Y)]
                hi, lw = split(jnp.concatenate(z, 1))
                both = jnp.concatenate([hi, lw], 0)
                a = a + lax.dot_general(both, hi, NT, preferred_element_type=F32)
                b = b + lax.dot_general(both, lw, NT, preferred_element_type=F32)
            return a, b

        zero = jnp.zeros((2 * NB, NB), F32)
        a, b = lax.fori_loop(0, X, body, (zero, zero))
        g = (a[:NB] + b[NB:]) + (a[NB:] + b[:NB])
        g = jnp.concatenate([g, jnp.zeros((NB, 128 - NB), F32)], 1)
        lane = lax.broadcasted_iota(jnp.int32, (8, 128), 1)
        t0 = jnp.zeros((8, 128), F32)
        for b_ in range(NV // 8):
            piece = jnp.where(lane < NV, g[b_ * 8:b_ * 8 + 8], 0.0)
            t0 = t0 + (pltpu.roll(piece, b_ * NV, 1) if b_ else piece)
        t1 = g[NV:NV + 8] + pltpu.roll(g[NV + 8:NV + 16], 64, 1)
        PK[c, 0] = t0
        PK[c, 1] = t1

    def sum_x_start(k):
        cs = groups[k]
        part = pl.ds(cs[0], len(cs))
        for c in cs:
            RX[mx, c] = PK[c]
        for o in range(1, nx):
            send(PK.at[part], RX.at[mx, part], ax_at[k] + o, ax_at[k] + mx, (cut, lax.rem(mx + o, nx), my))

    def sum_x_end(k):
        cs = groups[k]
        part = pl.ds(cs[0], len(cs))
        for o in range(1, nx):
            t = lax.rem(mx + o, nx)
            arrived(RX.at[t, part], ax_at[k] + t)
        for c in cs:
            acc = RX[0, c]
            for t in range(1, nx):
                acc = acc + RX[t, c]
            SM[c] = acc
            RZ[kz, c] = acc
        for o in range(1, K):
            t = lax.rem(kz + o, K)
            send(SM.at[part], RZ.at[kz, part], az_at[k] + o, az_at[k] + kz, (cut, mx, t * 2 + p))

    e16r = lax.broadcasted_iota(jnp.int32, (NW, NW), 0)
    e16l = lax.broadcasted_iota(jnp.int32, (NW, NW), 1)
    l32 = lax.broadcasted_iota(jnp.int32, (NV, 128), 1)
    r32 = lax.broadcasted_iota(jnp.int32, (NV, 128), 0)
    eye = jnp.where(l32 == r32 + NV, 1.0, 0.0)
    ident = jnp.where(l32 == r32, 1.0, 0.0)[:, :NV]

    def factor(k):
        cs = groups[k]
        part = pl.ds(cs[0], len(cs))
        for o in range(1, K):
            t = lax.rem(kz + o, K)
            arrived(RZ.at[t, part], az_at[k] + t)
        corrs, mats = [], []
        for c in cs:
            acc = RZ[0, c]
            for t in range(1, K):
                acc = acc + RZ[t, c]
            acc = acc * (1.0 / total)
            t0, t1 = acc[0], acc[1]
            ff = jnp.concatenate([pltpu.roll(t0, 128 - b * NV, 1) if b else t0 for b in range(NV // 8)], 0)
            w = jnp.concatenate([t1, pltpu.roll(t1, 64, 1)], 0)
            corr = w[:, :NV]
            b = jnp.where(e16r == e16l, 2.0, 0.0) - pltpu.roll(w, 128 - NV, 1)[:, :NW]
            bc = lax.dot_general(b, corr, NN, precision=HP, preferred_element_type=F32)
            sub = lax.dot_general(corr, bc, TN, precision=HP, preferred_element_type=F32)
            sub = jnp.concatenate([sub, jnp.zeros((NV, 128 - NV), F32)], 1)
            corrs.append(corr)
            mats.append(jnp.where(l32 < NV, ff - sub, eye)[None])
        M = jnp.concatenate(mats, 0)
        line = lax.broadcasted_iota(jnp.int32, (1, NV, 1), 1)
        for j in range(NV):
            pivot = M[:, j:j + 1, :]
            inv = 1.0 / pivot[:, :, j:j + 1]
            f = jnp.where(line > j, M[:, :, j:j + 1] * inv, 0.0)
            M = M - f * pivot
        diag = jnp.sum(jnp.where(l32[None] == r32[None], M, 0.0), axis=2, keepdims=True)
        M = M * (1.0 / jnp.sqrt(diag))
        for i, c in enumerate(cs):
            s = p * S + c
            linv = pltpu.roll(M[i], 128 - NV, 1)[:, :NV]
            full = jnp.concatenate([ident, -corrs[i]], 0)
            lm = lax.dot_general(linv, full, NT, precision=HP, preferred_element_type=F32)
            LM[s] = lm
            cor[s] = corrs[i]
            wide = jnp.concatenate([corrs[i], jnp.zeros((NV - NW, NV), F32)], 0)
            wide = jnp.concatenate([lm, jnp.zeros((NV, 64 - NB), F32), wide, jnp.zeros((NV, 64 - NV), F32)], 1)
            LP[c] = wide
            send(LP.at[c], LR.at[c], l_at[c], l_at[c], yp)

    def take(c):
        s = q * S + c
        arrived(LR.at[c], l_at[c])
        wide = LR[c]
        LM[s] = wide[:, :NB]
        cor[s] = pltpu.roll(wide, 64, 1)[:NW, :NV]
        arrived(FA.at[s], f_at[c])

    def finish(s):
        hi, lw = split(LM[s])
        left = jnp.concatenate([hi, hi, lw], 1)

        def body(x, carry):
            z = [jnp.concatenate([FA[s, x, r], RA[s, x, r], RA[s + 2, x, r]], 0) for r in range(Y)]
            zh, zl = split(jnp.concatenate(z, 1))
            o = lax.dot_general(left, jnp.concatenate([zh, zl, zh], 0), NN, preferred_element_type=F32)
            for r in range(Y):
                out[s, pl.ds(x * Y + r, NV, stride=J), :] = o[:, r * NZ:(r + 1) * NZ]
            return carry

        lax.fori_loop(0, X, body, 0)

    for c in range(S - 1):
        apply(c)
        gram(c)
    sum_x_start(0)
    sum_x_end(0)
    apply(S - 1)
    gram(S - 1)
    sum_x_start(1)
    sum_x_end(1)
    factor(0)
    for c in groups[0]:
        finish(p * S + c)
    factor(1)
    for c in groups[0]:
        take(c)
        finish(q * S + c)
    finish(p * S + S - 1)
    take(S - 1)
    finish(q * S + S - 1)
    for copy in pending:
        copy.wait_send()


def on_device(disorder, slice_bounds, start, ritz):
    nc, nx, ny = (lax.axis_size(a) for a in ("cuts", "lx", "ly"))
    count, NV, X, Y, NZ = start.shape
    NR = ritz.shape[1]
    J = X * Y
    S, R, K = count // 2, 2 * Y, ny // 2
    V = pltpu.VMEM
    D = pltpu.SemaphoreType.DMA
    dims = (nc, nx, ny, count, NV, NR, X, Y, NZ)
    vm = pl.BlockSpec(memory_space=pltpu.VMEM)
    hbm = pl.BlockSpec(memory_space=pl.ANY)
    sems = sem_counts(nx, K, S)
    block, corr = pl.pallas_call(
        functools.partial(kernel, dims),
        out_shape=(jax.ShapeDtypeStruct((count, NV * J, NZ), F32),
                   jax.ShapeDtypeStruct((count, 2 * NR, NV), F32)),
        in_specs=[hbm, pl.BlockSpec(memory_space=pltpu.SMEM), hbm, hbm],
        out_specs=(vm, vm),
        scratch_shapes=[
            V((J, NZ), jnp.int32),
            V((count, NV * J, NZ), F32),
            V((count, NR * J, NZ), F32),
            D((2 * S + 2,)),
            V((S, X + 2 * H, R + 2 * H, NV, NZ), F32),
            V((S, X, Y, NV, NZ), F32),
            V((X + 2 * H, R + 2 * H, 1, NZ), F32),
            V((X + 2 * H, R + 2 * H, NV, NZ), F32),
            V((count, X, Y, NV, NZ), F32),
            V((S, X, Y, NV, NZ), F32),
            V((count + 2, X, Y, NR, NZ), F32),
            V((S + 2, X, Y, NR, NZ), F32),
            V((S, 2, 8, 128), F32),
            V((nx, S, 2, 8, 128), F32),
            V((S, 2, 8, 128), F32),
            V((K, S, 2, 8, 128), F32),
            V((count, NV, NV + 2 * NR), F32),
            V((S, NV, 128), F32),
            V((S, NV, 128), F32),
            D((sems,)), D((sems,)),
        ],
        compiler_params=pltpu.CompilerParams(collective_id=0, has_side_effects=True, vmem_limit_bytes=67043328),
    )(disorder.reshape(J, NZ), slice_bounds.T, start.reshape(count, NV * J, NZ), ritz.reshape(count, NR * J, NZ))
    return (block.reshape(start.shape), corr)


def solution(mesh):
    in_specs = (
        P("lx", "ly", None),
        P("cuts", None),
        P("cuts", None, "lx", "ly", None),
        P("cuts", None, "lx", "ly", None),
    )
    out_specs = (P("cuts", None, "lx", "ly", None), P("cuts", None, None))
    return jax.shard_map(
        on_device, mesh=mesh, in_specs=in_specs, out_specs=out_specs, check_vma=False
    )
```

```python
import functools

import jax
import jax.numpy as jnp
from jax import lax
from jax.experimental import pallas as pl
from jax.experimental.pallas import tpu as pltpu
from jax.sharding import PartitionSpec as P

LEVELS = 256
MESH = pl.DeviceIdType.MESH
HP = lax.Precision.HIGHEST
H = 2
BF = jnp.bfloat16
F32 = jnp.float32
NT = (((1,), (1,)), ((), ()))
NN = (((1,), (0,)), ((), ()))
TN = (((0,), (0,)), ((), ()))


def sem_counts(nx, K, S):
    return 5 + S * (14 + nx + K) + 2 + (S + 2)


def split(z):
    hi = z.astype(BF)
    return hi, (z - hi.astype(F32)).astype(BF)


def loop(n, unroll, body):
    def step(i, carry):
        for k in range(unroll):
            body(i * unroll + k)
        return carry

    if n % unroll:
        unroll = 1
    lax.fori_loop(0, n // unroll, step, 0)


def kernel(dims, dis_h, bnd_h, start_h, ritz_h, out_h, cor_h, out, cor, bnd, dis, start, ritz, ls, E, T, O, U, FA, FT,
           RA, RQ, GS, PK, RX, SM, RZ, LM, LP, LR, ss, rs):
    nc, nx, ny, count, NV, NR, X, Y, NZ = dims
    S = count // 2
    R = 2 * Y
    J = X * Y
    K = ny // 2
    total = float(J * NZ * nx * ny)
    NW = 2 * NR
    NB = NV + NW
    cut, mx, my = lax.axis_index("cuts"), lax.axis_index("lx"), lax.axis_index("ly")
    p = lax.rem(my, 2)
    q = 1 - p
    kz = my // 2
    yp = (cut, mx, kz * 2 + q)
    zup = (cut, mx, lax.rem(kz + 1, K) * 2 + p)
    zdown = (cut, mx, lax.rem(kz + K - 1, K) * 2 + p)
    xup = (cut, lax.rem(mx + 1, nx), my)
    xdown = (cut, lax.rem(mx + nx - 1, nx), my)
    cup = (lax.rem(cut + 1, nc), mx, my)
    cdown = (lax.rem(cut + nc - 1, nc), mx, my)

    def load(src, dst, i):
        copy = pltpu.make_async_copy(src, dst, ls.at[i])
        copy.start()
        return copy

    level_load = load(dis_h, dis, 2 * S)
    bound_load = load(bnd_h, bnd, 2 * S + 2)
    away, kept = [], []
    for c in range(S):
        away.append(load(start_h.at[q * S + c], start.at[c], c))
        kept.append(load(start_h.at[p * S + c], start.at[S + c], S + c))
    ritz_load = load(ritz_h, ritz, 2 * S + 1)
    barrier = pltpu.get_barrier_semaphore()

    def greet(dev):
        pl.semaphore_signal(barrier, inc=1, device_id=dev, device_id_type=MESH)

    greet(yp)
    for o in range(1, nx):
        greet((cut, lax.rem(mx + o, nx), my))
    for o in range(1, K):
        greet((cut, mx, lax.rem(kz + o, K) * 2 + p))
    greet(cup)
    greet(cdown)

    lo = H + Y * p
    lq = H + Y * q
    xi = pl.ds(H, X)
    level_load.wait()
    for x in range(X):
        for r in range(Y):
            row = dis[pl.ds(x * Y + r, 1), :].astype(F32)
            O[H + x, lo + r] = 16.5 * (row / F32(LEVELS - 1) - 0.5)

    def stage_away(c):
        away[c].wait()
        for x in range(X):
            for r in range(Y):
                T[c, x, r] = start[c, pl.ds(x * Y + r, NV, stride=J), :]

    def stage_kept(c):
        kept[c].wait()
        for x in range(X):
            for r in range(Y):
                E[c, H + x, lo + r] = start[S + c, pl.ds(x * Y + r, NV, stride=J), :]

    pending = []
    used = [0]

    def slots(n=1):
        i = used[0]
        used[0] += n
        return i

    def send(src, dst, i, j, dev):
        copy = pltpu.make_async_remote_copy(
            src_ref=src, dst_ref=dst, send_sem=ss.at[i], recv_sem=rs.at[j], device_id=dev, device_id_type=MESH)
        copy.start()
        pending.append(copy)

    def arrived(dst, j):
        pltpu.make_async_remote_copy(
            src_ref=dst, dst_ref=dst, send_sem=rs.at[j], recv_sem=rs.at[j],
            device_id=yp, device_id_type=MESH).wait_recv()

    def rows(at):
        return pl.ds(at, Y)

    o_y, o_z, o_x = slots(), slots(2), slots(2)
    y_at = [slots() for _ in range(S)]
    z_at = [slots(3) for _ in range(S)]
    xo_at = [slots(2) for _ in range(S)]
    xp_at = [slots(2) for _ in range(S)]
    k_at = [slots(4) for _ in range(S)]
    f_at = [slots() for _ in range(S)]
    l_at = [slots() for _ in range(S)]
    c_at = slots(2)
    r_at = slots(S + 2)
    ax_at = [slots(nx) for _ in range(S)]
    az_at = [slots(K) for _ in range(S)]

    def send_y(c):
        send(T.at[c], E.at[c, xi, rows(lo)], y_at[c], y_at[c], yp)

    def send_own_z(c):
        dev = (cut, mx, jnp.where(p == 1, zup[2], zdown[2]))
        dst = jnp.where(p == 1, 0, H + R)
        send(E.at[c, xi, rows(lo)], E.at[c, xi, rows(dst)], z_at[c], z_at[c], dev)

    def send_rest_z(c):
        dev = (cut, mx, jnp.where(q == 1, zup[2], zdown[2]))
        for k in range(2):
            src = jnp.where(q == 1, H + R - 1 - k, H + k)
            dst = jnp.where(q == 1, H - 1 - k, H + R + k)
            send(E.at[c, xi, src], E.at[c, xi, dst], z_at[c] + 1 + k, z_at[c] + 1 + k, dev)

    def send_x(c, base, at):
        send(E.at[c, pl.ds(X, H), rows(at)], E.at[c, pl.ds(0, H), rows(at)], base, base, xup)
        send(E.at[c, pl.ds(H, H), rows(at)], E.at[c, pl.ds(H + X, H), rows(at)], base + 1, base + 1, xdown)

    def got_x(c, base, at):
        arrived(E.at[c, pl.ds(0, H), rows(at)], base)
        arrived(E.at[c, pl.ds(H + X, H), rows(at)], base + 1)

    def send_o(half):
        side = 1 - half
        dev = (cut, mx, jnp.where(half == 1, zup[2], zdown[2]))
        src = jnp.where(half == 1, H + R - 1, H)
        dst = jnp.where(half == 1, 1, H + R)
        send(O.at[xi, src], O.at[xi, dst], o_z + side, o_z + side, dev)

    stage_away(0)
    stage_kept(0)
    pl.semaphore_wait(barrier, nx + K + 1)
    send(O.at[xi, rows(lo)], O.at[xi, rows(lo)], o_y, o_y, yp)
    send_y(0)
    send_o(p)
    send_own_z(0)
    send_x(0, xo_at[0], lo)
    for c in range(1, S):
        stage_away(c)
        send_y(c)
        stage_kept(c)
        if c < S - 1:
            send_own_z(c)
        send_x(c, xo_at[c], lo)
    bound_load.wait()
    ritz_load.wait()
    for s in range(count):
        for x in range(X):
            for r in range(Y):
                RA[s + 1, x, r] = ritz[s, pl.ds(x * Y + r, NR, stride=J), :]
    send(RA.at[count], RA.at[0], c_at, c_at, cup)
    send(RA.at[1], RA.at[count + 1], c_at + 1, c_at + 1, cdown)

    own = pl.ds(H, R)
    arrived(O.at[xi, rows(lq)], o_y)
    send_o(q)
    send(O.at[H + X - 1, own], O.at[H - 1, own], o_x, o_x, xup)
    send(O.at[H, own], O.at[H + X, own], o_x + 1, o_x + 1, xdown)

    arrived(RA.at[0], c_at)
    arrived(RA.at[count + 1], c_at + 1)

    @pl.when(cut == 0)
    def _():
        RA[0] = jnp.zeros((X, Y, NR, NZ), F32)

    @pl.when(cut == nc - 1)
    def _():
        RA[count + 1] = jnp.zeros((X, Y, NR, NZ), F32)

    order = []
    for c in range(S):
        for j in (c, c + 2):
            if j not in order:
                order.append(j)
    for j in order:
        send(RA.at[q * S + j], RQ.at[j], r_at + j, r_at + j, yp)

    for c in range(S):
        arrived(E.at[c, xi, rows(lq)], y_at[c])
        if c < S - 1:
            send_rest_z(c)
        send_x(c, xp_at[c], lq)
        if c == 0:
            send_own_z(S - 1)

    arrived(O.at[xi, H - 1], o_z)
    arrived(O.at[xi, H + R], o_z + 1)
    arrived(O.at[H - 1, own], o_x)
    arrived(O.at[H + X, own], o_x + 1)

    last = R + 2 * H - 1
    ra = [a + p * (last - 2 * a) for a in range(last + 1)]
    near, far = H - 1, H + R

    def point(src, x, a, centre):
        v = src(x, a)
        beside = src(x + 1, a) + src(x - 1, a)
        beside = beside + src(x, a + 1) + src(x, a - 1)
        beside = beside + pltpu.roll(v, 1, 1) + pltpu.roll(v, NZ - 1, 1)
        level = jnp.broadcast_to(O[x, ra[a]] - centre, (NV, NZ))
        return level * v - beside

    def refs(c):
        s = p * S + c
        centre = (bnd[0, s] + bnd[1, s]) / 2.0

        def from_e(x, a):
            return E[c, x, ra[a]]

        def from_u(x, a):
            return U[c, x, ra[a]]

        def one(x, a):
            U[c, x, ra[a]] = point(from_e, x, a, centre)

        def two(x, a):
            return point(from_u, x, a, centre) * (2.0 / 256.0) - from_e(x, a)

        return one, two

    def corners(c, a, k):
        send(E.at[c, H + X - 1, ra[a]], E.at[c, H - 1, ra[a]], k, k, xup)
        send(E.at[c, H, ra[a]], E.at[c, H + X, ra[a]], k + 1, k + 1, xdown)

    def got_corners(c, a, k):
        arrived(E.at[c, H - 1, ra[a]], k)
        arrived(E.at[c, H + X, ra[a]], k + 1)

    def early_corners(c):
        arrived(E.at[c, xi, rows(jnp.where(p == 1, 0, H + R))], z_at[c])
        corners(c, far, k_at[c])

    def early(c):
        one, two = refs(c)
        got_x(c, xo_at[c], lo)
        got_x(c, xp_at[c], lq)

        def inner(i):
            for a in range(H + 1, far + 1):
                one(H + 1 + i, a)

        loop(X - 2, 2, inner)
        for x in (H, H + X - 1):
            for a in range(H + 1, far):
                one(x, a)
        for x in (H - 1, H + X):
            for a in range(H + 1, far - 1):
                one(x, a)
        got_corners(c, far, k_at[c])
        for x in (H, H + X - 1):
            one(x, far)
        for x in (H - 1, H + X):
            one(x, far - 1)

        def outer(i):
            for a in range(H + Y, far):
                FT[c, i, ra[a] - lq] = two(H + i, a)

        loop(X, 2, outer)
        send(FT.at[c], FA.at[p * S + c], f_at[c], f_at[c], yp)

    def late(c):
        one, two = refs(c)
        arrived(E.at[c, xi, ra[near]], z_at[c] + 1)
        corners(c, near, k_at[c] + 2)
        arrived(E.at[c, xi, ra[near - 1]], z_at[c] + 2)

        def inner(i):
            for a in (near, H):
                one(H + 1 + i, a)

        loop(X - 2, 2, inner)
        for x in (H, H + X - 1):
            one(x, H)
        got_corners(c, near, k_at[c] + 2)
        for x in (H, H + X - 1):
            one(x, near)
        for x in (H - 1, H + X):
            one(x, H)

        def outer(i):
            for a in range(H, H + Y):
                FA[p * S + c, i, ra[a] - lo] = two(H + i, a)

        loop(X, 2, outer)

    def product(f, w0, w1):
        def body(i, acc):
            for k in range(2):
                z = [jnp.concatenate([f(2 * i + k, r), w0(2 * i + k, r), w1(2 * i + k, r)], 0) for r in range(Y)]
                hi, lw = split(jnp.concatenate(z, 1))
                acc = acc + lax.dot_general(jnp.concatenate([hi, lw], 0), hi, NT, preferred_element_type=F32)
            return acc

        return lax.fori_loop(0, X // 2, body, jnp.zeros((2 * NB, NB), F32))

    def gram_rest(c):
        for j in (c, c + 2):
            if j not in seen:
                arrived(RQ.at[j], r_at + j)
                seen.add(j)
        GS[c] = product(lambda x, r: FT[c, x, r], lambda x, r: RQ[c, x, r], lambda x, r: RQ[c + 2, x, r])

    def gram_own(c):
        s = p * S + c
        g = GS[c] + product(lambda x, r: FA[s, x, r], lambda x, r: RA[s, x, r], lambda x, r: RA[s + 2, x, r])
        g = jnp.concatenate([g, jnp.zeros((2 * NB, 128 - NB), F32)], 1)
        cross = jnp.concatenate([g[NB:], jnp.zeros((128 - NB, 128), F32)], 0)
        g = g[:NB] + (cross + cross.T)[:NB]
        lane = lax.broadcasted_iota(jnp.int32, (8, 128), 1)
        t0 = jnp.zeros((8, 128), F32)
        for b_ in range(NV // 8):
            piece = jnp.where(lane < NV, g[b_ * 8:b_ * 8 + 8], 0.0)
            t0 = t0 + (pltpu.roll(piece, b_ * NV, 1) if b_ else piece)
        t1 = g[NV:NV + 8] + pltpu.roll(g[NV + 8:NV + 16], 64, 1)
        PK[c, 0] = t0
        PK[c, 1] = t1

    seen = set()

    def sum_x_start(c):
        RX[mx, c] = PK[c]
        for o in range(1, nx):
            send(PK.at[c], RX.at[mx, c], ax_at[c] + o, ax_at[c] + mx, (cut, lax.rem(mx + o, nx), my))

    def sum_x_end(c):
        for o in range(1, nx):
            t = lax.rem(mx + o, nx)
            arrived(RX.at[t, c], ax_at[c] + t)
        acc = RX[0, c]
        for t in range(1, nx):
            acc = acc + RX[t, c]
        SM[c] = acc
        RZ[kz, c] = acc
        for o in range(1, K):
            t = lax.rem(kz + o, K)
            send(SM.at[c], RZ.at[kz, c], az_at[c] + o, az_at[c] + kz, (cut, mx, t * 2 + p))

    e16r = lax.broadcasted_iota(jnp.int32, (NW, NW), 0)
    e16l = lax.broadcasted_iota(jnp.int32, (NW, NW), 1)
    l32 = lax.broadcasted_iota(jnp.int32, (NV, 128), 1)
    r32 = lax.broadcasted_iota(jnp.int32, (NV, 128), 0)
    eye = jnp.where(l32 == r32 + NV, 1.0, 0.0)
    ident = jnp.where(l32 == r32, 1.0, 0.0)[:, :NV]

    def factor(c):
        for o in range(1, K):
            t = lax.rem(kz + o, K)
            arrived(RZ.at[t, c], az_at[c] + t)
        acc = RZ[0, c]
        for t in range(1, K):
            acc = acc + RZ[t, c]
        acc = acc * (1.0 / total)
        t0, t1 = acc[0], acc[1]
        ff = jnp.concatenate([pltpu.roll(t0, 128 - b * NV, 1) if b else t0 for b in range(NV // 8)], 0)
        w = jnp.concatenate([t1, pltpu.roll(t1, 64, 1)], 0)
        corr = w[:, :NV]
        b = jnp.where(e16r == e16l, 2.0, 0.0) - pltpu.roll(w, 128 - NV, 1)[:, :NW]
        bc = lax.dot_general(b, corr, NN, precision=HP, preferred_element_type=F32)
        sub = lax.dot_general(corr, bc, TN, precision=HP, preferred_element_type=F32)
        sub = jnp.concatenate([sub, jnp.zeros((NV, 128 - NV), F32)], 1)
        M = jnp.where(l32 < NV, ff - sub, eye)
        line = lax.broadcasted_iota(jnp.int32, (NV, 1), 0)
        for j in range(0, NV, 2):
            r0, r1 = M[j:j + 1], M[j + 1:j + 2]
            c0, c1 = M[:, j:j + 1], M[:, j + 1:j + 2]
            p00, p01, p11 = c0[j:j + 1], c1[j:j + 1], c1[j + 1:j + 2]
            inv = 1.0 / (p00 * p11 - p01 * p01)
            keep = jnp.where(line > j + 1, inv, 0.0)
            f0 = (c0 * p11 - c1 * p01) * keep
            f1 = (c1 * p00 - c0 * p01) * keep
            M = M - f0 * r0 - f1 * r1
        odd = r32 % 2
        diag = jnp.sum(jnp.where(l32 == r32, M, 0.0), axis=1, keepdims=True)
        side = jnp.sum(jnp.where(l32 == r32 - odd, M, 0.0), axis=1, keepdims=True)
        above = pltpu.roll(M, 1, 0)
        ratio = side / pltpu.roll(jnp.broadcast_to(diag, (NV, 128)), 1, 0)
        M = jnp.where(odd == 1, M - ratio * above, M)
        diag = jnp.sum(jnp.where(l32 == r32, M, 0.0), axis=1, keepdims=True)
        M = M * (1.0 / jnp.sqrt(diag))
        s = p * S + c
        linv = pltpu.roll(M, 128 - NV, 1)[:, :NV]
        full = jnp.concatenate([ident, -corr], 0)
        lm = lax.dot_general(linv, full, NT, precision=HP, preferred_element_type=F32)
        wide = jnp.concatenate([corr, jnp.zeros((NV - NW, NV), F32)], 0)
        wide = jnp.concatenate([lm, jnp.zeros((NV, 64 - NB), F32), wide, jnp.zeros((NV, 64 - NV), F32)], 1)
        LP[c] = wide
        send(LP.at[c], LR.at[c], l_at[c], l_at[c], yp)
        LM[s] = lm
        cor[s] = corr

    def take(c):
        s = q * S + c
        arrived(LR.at[c], l_at[c])
        wide = LR[c]
        LM[s] = wide[:, :NB]
        cor[s] = pltpu.roll(wide, 64, 1)[:NW, :NV]
        arrived(FA.at[s], f_at[c])

    stored = []

    def store(src, dst, i):
        stored.append(load(src, dst, i))

    def finish(s, i):
        hi, lw = split(LM[s])
        left = jnp.concatenate([hi, lw], 0)
        left = jnp.concatenate([left, jnp.concatenate([hi, jnp.zeros((NV, NB), BF)], 0)], 1)

        def body(x):
            z = [jnp.concatenate([FA[s, x, r], RA[s, x, r], RA[s + 2, x, r]], 0) for r in range(Y)]
            zh, zl = split(jnp.concatenate(z, 1))
            o = lax.dot_general(left, jnp.concatenate([zh, zl], 0), NN, preferred_element_type=F32)
            o = o[:NV] + o[NV:]
            for r in range(Y):
                out[s, pl.ds(x * Y + r, NV, stride=J), :] = o[:, r * NZ:(r + 1) * NZ]

        loop(X, 2, body)
        store(out.at[s], out_h.at[s], i)

    def finish_own(c):
        finish(p * S + c, c)

    def finish_rest(c):
        take(c)
        finish(q * S + c, S + c)

    early_corners(0)
    early(0)
    late(0)
    gram_rest(0)
    gram_own(0)
    sum_x_start(0)
    for c in range(1, S):
        early_corners(c) if c < S - 1 else None
    for c in range(1, S):
        if c == S - 1:
            sum_x_end(0)
            send_rest_z(c)
            early_corners(c)
        early(c)
        gram_rest(c)
    for c in range(1, S - 1):
        late(c)
        gram_own(c)
        sum_x_start(c)
        factor(c - 1)
        finish_own(c - 1)
        sum_x_end(c)
        finish_rest(c - 1)
    late(S - 1)
    gram_own(S - 1)
    sum_x_start(S - 1)
    sum_x_end(S - 1)
    factor(S - 2)
    finish_own(S - 2)
    factor(S - 1)
    finish_rest(S - 2)
    finish_own(S - 1)
    take(S - 1)
    store(cor, cor_h, 2 * S)
    finish(q * S + S - 1, 2 * S - 1)
    for copy in stored:
        copy.wait()
    for copy in pending:
        copy.wait_send()


def on_device(disorder, slice_bounds, start, ritz):
    nc, nx, ny = (lax.axis_size(a) for a in ("cuts", "lx", "ly"))
    count, NV, X, Y, NZ = start.shape
    NR = ritz.shape[1]
    J = X * Y
    S, R, K = count // 2, 2 * Y, ny // 2
    V = pltpu.VMEM
    D = pltpu.SemaphoreType.DMA
    dims = (nc, nx, ny, count, NV, NR, X, Y, NZ)
    hbm = pl.BlockSpec(memory_space=pl.ANY)
    sems = sem_counts(nx, K, S)
    block, corr = pl.pallas_call(
        functools.partial(kernel, dims),
        out_shape=(jax.ShapeDtypeStruct((count, NV * J, NZ), F32),
                   jax.ShapeDtypeStruct((count, 2 * NR, NV), F32)),
        in_specs=[hbm] * 4,
        out_specs=(hbm, hbm),
        scratch_shapes=[
            V((count, NV * J, NZ), F32),
            V((count, 2 * NR, NV), F32),
            pltpu.SMEM((2, count), F32),
            V((J, NZ), jnp.int32),
            V((count, NV * J, NZ), F32),
            V((count, NR * J, NZ), F32),
            D((2 * S + 3,)),
            V((S, X + 2 * H, R + 2 * H, NV, NZ), F32),
            V((S, X, Y, NV, NZ), F32),
            V((X + 2 * H, R + 2 * H, 1, NZ), F32),
            V((S, X + 2 * H, R + 2 * H, NV, NZ), F32),
            V((count, X, Y, NV, NZ), F32),
            V((S, X, Y, NV, NZ), F32),
            V((count + 2, X, Y, NR, NZ), F32),
            V((S + 2, X, Y, NR, NZ), F32),
            V((S, 2 * (NV + 2 * NR), NV + 2 * NR), F32),
            V((S, 2, 8, 128), F32),
            V((nx, S, 2, 8, 128), F32),
            V((S, 2, 8, 128), F32),
            V((K, S, 2, 8, 128), F32),
            V((count, NV, NV + 2 * NR), F32),
            V((S, NV, 128), F32),
            V((S, NV, 128), F32),
            D((sems,)), D((sems,)),
        ],
        compiler_params=pltpu.CompilerParams(collective_id=0, has_side_effects=True, vmem_limit_bytes=48 << 20),
    )(*[pltpu.with_memory_space_constraint(a, pltpu.HBM) for a in (
        disorder.reshape(J, NZ), slice_bounds.T, start.reshape(count, NV * J, NZ), ritz.reshape(count, NR * J, NZ))])
    return (block.reshape(start.shape), corr)


def solution(mesh):
    in_specs = (
        P("lx", "ly", None),
        P("cuts", None),
        P("cuts", None, "lx", "ly", None),
        P("cuts", None, "lx", "ly", None),
    )
    out_specs = (P("cuts", None, "lx", "ly", None), P("cuts", None, None))
    return jax.shard_map(
        on_device, mesh=mesh, in_specs=in_specs, out_specs=out_specs, check_vma=False
    )
```

```python
import functools

import jax
import jax.numpy as jnp
from jax import lax
from jax.experimental import pallas as pl
from jax.experimental.pallas import tpu as pltpu
from jax.sharding import PartitionSpec as P

LEVELS = 256
MESH = pl.DeviceIdType.MESH
HP = lax.Precision.HIGHEST
H = 2
BF = jnp.bfloat16
F32 = jnp.float32
NT = (((1,), (1,)), ((), ()))
NN = (((1,), (0,)), ((), ()))
TN = (((0,), (0,)), ((), ()))


def sem_counts(nx, K, S):
    return 5 + S * (14 + nx + K) + 2 + (S + 2)


def split(z):
    hi = z.astype(BF)
    return hi, (z - hi.astype(F32)).astype(BF)


def loop(n, unroll, body):
    def step(i, carry):
        for k in range(unroll):
            body(i * unroll + k)
        return carry

    if n % unroll:
        unroll = 1
    lax.fori_loop(0, n // unroll, step, 0)


def kernel(dims, dis_h, bnd_h, start_h, ritz_h, out_h, cor_h, out, cor, bnd, dis, start, ritz, ls, E, T, O, U, FA, FT,
           RA, RQ, GS, PK, RX, SM, RZ, LM, LP, LR, ss, rs):
    nc, nx, ny, count, NV, NR, X, Y, NZ = dims
    S = count // 2
    R = 2 * Y
    J = X * Y
    K = ny // 2
    total = float(J * NZ * nx * ny)
    NW = 2 * NR
    NB = NV + NW
    cut, mx, my = lax.axis_index("cuts"), lax.axis_index("lx"), lax.axis_index("ly")
    p = lax.rem(my, 2)
    q = 1 - p
    kz = my // 2
    yp = (cut, mx, kz * 2 + q)
    zup = (cut, mx, lax.rem(kz + 1, K) * 2 + p)
    zdown = (cut, mx, lax.rem(kz + K - 1, K) * 2 + p)
    xup = (cut, lax.rem(mx + 1, nx), my)
    xdown = (cut, lax.rem(mx + nx - 1, nx), my)
    cup = (lax.rem(cut + 1, nc), mx, my)
    cdown = (lax.rem(cut + nc - 1, nc), mx, my)

    def load(src, dst, i):
        copy = pltpu.make_async_copy(src, dst, ls.at[i])
        copy.start()
        return copy

    barrier = pltpu.get_barrier_semaphore()

    def greet(dev):
        pl.semaphore_signal(barrier, inc=1, device_id=dev, device_id_type=MESH)

    greet(yp)
    for o in range(1, nx):
        greet((cut, lax.rem(mx + o, nx), my))
    for o in range(1, K):
        greet((cut, mx, lax.rem(kz + o, K) * 2 + p))
    greet(cup)
    greet(cdown)

    away, kept = [], []
    for c in range(S):
        away.append(load(start_h.at[q * S + c], start.at[c], c))
        kept.append(load(start_h.at[p * S + c], start.at[S + c], S + c))
        if c == 0:
            level_load = load(dis_h, dis, 2 * S)
    bound_load = load(bnd_h, bnd, 2 * S + 2)
    ritz_load = load(ritz_h, ritz, 2 * S + 1)

    lo = H + Y * p
    lq = H + Y * q
    xi = pl.ds(H, X)
    def stage_away(c):
        away[c].wait()
        for x in range(X):
            for r in range(Y):
                T[c, x, r] = start[c, pl.ds(x * Y + r, NV, stride=J), :]

    def stage_kept(c):
        kept[c].wait()
        for x in range(X):
            for r in range(Y):
                E[c, H + x, lo + r] = start[S + c, pl.ds(x * Y + r, NV, stride=J), :]

    pending = []
    used = [0]

    def slots(n=1):
        i = used[0]
        used[0] += n
        return i

    def send(src, dst, i, j, dev):
        copy = pltpu.make_async_remote_copy(
            src_ref=src, dst_ref=dst, send_sem=ss.at[i], recv_sem=rs.at[j], device_id=dev, device_id_type=MESH)
        copy.start()
        pending.append(copy)

    def arrived(dst, j):
        pltpu.make_async_remote_copy(
            src_ref=dst, dst_ref=dst, send_sem=rs.at[j], recv_sem=rs.at[j],
            device_id=yp, device_id_type=MESH).wait_recv()

    def rows(at):
        return pl.ds(at, Y)

    o_y, o_z, o_x = slots(), slots(2), slots(2)
    y_at = [slots() for _ in range(S)]
    z_at = [slots(3) for _ in range(S)]
    xo_at = [slots(2) for _ in range(S)]
    xp_at = [slots(2) for _ in range(S)]
    k_at = [slots(4) for _ in range(S)]
    f_at = [slots() for _ in range(S)]
    l_at = [slots() for _ in range(S)]
    c_at = slots(2)
    r_at = slots(S + 2)
    ax_at = [slots(nx) for _ in range(S)]
    az_at = [slots(K) for _ in range(S)]

    def send_y(c):
        send(T.at[c], E.at[c, xi, rows(lo)], y_at[c], y_at[c], yp)

    def send_own_z(c):
        dev = (cut, mx, jnp.where(p == 1, zup[2], zdown[2]))
        dst = jnp.where(p == 1, 0, H + R)
        send(E.at[c, xi, rows(lo)], E.at[c, xi, rows(dst)], z_at[c], z_at[c], dev)

    def send_rest_z(c):
        dev = (cut, mx, jnp.where(q == 1, zup[2], zdown[2]))
        for k in range(2):
            src = jnp.where(q == 1, H + R - 1 - k, H + k)
            dst = jnp.where(q == 1, H - 1 - k, H + R + k)
            send(E.at[c, xi, src], E.at[c, xi, dst], z_at[c] + 1 + k, z_at[c] + 1 + k, dev)

    def send_x(c, base, at):
        send(E.at[c, pl.ds(X, H), rows(at)], E.at[c, pl.ds(0, H), rows(at)], base, base, xup)
        send(E.at[c, pl.ds(H, H), rows(at)], E.at[c, pl.ds(H + X, H), rows(at)], base + 1, base + 1, xdown)

    def got_x(c, base, at):
        arrived(E.at[c, pl.ds(0, H), rows(at)], base)
        arrived(E.at[c, pl.ds(H + X, H), rows(at)], base + 1)

    def send_o(half):
        side = 1 - half
        dev = (cut, mx, jnp.where(half == 1, zup[2], zdown[2]))
        src = jnp.where(half == 1, H + R - 1, H)
        dst = jnp.where(half == 1, 1, H + R)
        send(O.at[xi, src], O.at[xi, dst], o_z + side, o_z + side, dev)

    stage_away(0)
    stage_kept(0)
    pl.semaphore_wait(barrier, nx + K + 1)
    send_y(0)
    send_own_z(0)
    send_x(0, xo_at[0], lo)
    level_load.wait()
    for x in range(X):
        for r in range(Y):
            row = dis[pl.ds(x * Y + r, 1), :].astype(F32)
            O[H + x, lo + r] = 16.5 * (row / F32(LEVELS - 1) - 0.5)
    send(O.at[xi, rows(lo)], O.at[xi, rows(lo)], o_y, o_y, yp)
    send_o(p)
    for c in range(1, S):
        stage_away(c)
        send_y(c)
        stage_kept(c)
        if c < S - 1:
            send_own_z(c)
        send_x(c, xo_at[c], lo)
    bound_load.wait()
    ritz_load.wait()
    for s in range(count):
        for x in range(X):
            for r in range(Y):
                RA[s + 1, x, r] = ritz[s, pl.ds(x * Y + r, NR, stride=J), :]
    send(RA.at[count], RA.at[0], c_at, c_at, cup)
    send(RA.at[1], RA.at[count + 1], c_at + 1, c_at + 1, cdown)

    arrived(RA.at[0], c_at)
    arrived(RA.at[count + 1], c_at + 1)

    @pl.when(cut == 0)
    def _():
        RA[0] = jnp.zeros((X, Y, NR, NZ), F32)

    @pl.when(cut == nc - 1)
    def _():
        RA[count + 1] = jnp.zeros((X, Y, NR, NZ), F32)

    order = []
    for c in range(S):
        for j in (c, c + 2):
            if j not in order:
                order.append(j)
    for j in order:
        send(RA.at[q * S + j], RQ.at[j], r_at + j, r_at + j, yp)

    own = pl.ds(H, R)

    def relay_o():
        arrived(O.at[xi, rows(lq)], o_y)
        send_o(q)
        send(O.at[H + X - 1, own], O.at[H - 1, own], o_x, o_x, xup)
        send(O.at[H, own], O.at[H + X, own], o_x + 1, o_x + 1, xdown)

    def got_y(c):
        arrived(E.at[c, xi, rows(lq)], y_at[c])

    last = R + 2 * H - 1
    ra = [a + p * (last - 2 * a) for a in range(last + 1)]
    near, far = H - 1, H + R

    def point(src, x, a, centre):
        v = src(x, a)
        beside = src(x + 1, a) + src(x - 1, a)
        beside = beside + src(x, a + 1) + src(x, a - 1)
        beside = beside + pltpu.roll(v, 1, 1) + pltpu.roll(v, NZ - 1, 1)
        level = jnp.broadcast_to(O[x, ra[a]] - centre, (NV, NZ))
        return level * v - beside

    def refs(c):
        s = p * S + c
        centre = (bnd[0, s] + bnd[1, s]) / 2.0

        def from_e(x, a):
            return E[c, x, ra[a]]

        def from_u(x, a):
            return U[c, x, ra[a]]

        def one(x, a):
            U[c, x, ra[a]] = point(from_e, x, a, centre)

        def two(x, a):
            return point(from_u, x, a, centre) * (2.0 / 256.0) - from_e(x, a)

        return one, two

    def corners(c, a, k):
        send(E.at[c, H + X - 1, ra[a]], E.at[c, H - 1, ra[a]], k, k, xup)
        send(E.at[c, H, ra[a]], E.at[c, H + X, ra[a]], k + 1, k + 1, xdown)

    def got_corners(c, a, k):
        arrived(E.at[c, H - 1, ra[a]], k)
        arrived(E.at[c, H + X, ra[a]], k + 1)

    def early_corners(c):
        arrived(E.at[c, xi, rows(jnp.where(p == 1, 0, H + R))], z_at[c])
        corners(c, far, k_at[c])

    def late_corners(c):
        arrived(E.at[c, xi, ra[near]], z_at[c] + 1)
        corners(c, near, k_at[c] + 2)

    def got_o():
        arrived(O.at[xi, H - 1], o_z)
        arrived(O.at[xi, H + R], o_z + 1)
        arrived(O.at[H - 1, own], o_x)
        arrived(O.at[H + X, own], o_x + 1)

    def early(c):
        one, two = refs(c)
        got_x(c, xo_at[c], lo)
        got_x(c, xp_at[c], lq)
        if c == 0:
            got_o()

        def inner(i):
            for a in range(H + 1, far + 1):
                one(H + 1 + i, a)

        loop(X - 2, 2, inner)
        for x in (H, H + X - 1):
            for a in range(H + 1, far):
                one(x, a)
        for x in (H - 1, H + X):
            for a in range(H + 1, far - 1):
                one(x, a)
        got_corners(c, far, k_at[c])
        for x in (H, H + X - 1):
            one(x, far)
        for x in (H - 1, H + X):
            one(x, far - 1)

        def outer(i):
            for a in range(H + Y, far):
                FT[c, i, ra[a] - lq] = two(H + i, a)

        loop(X, 2, outer)
        send(FT.at[c], FA.at[p * S + c], f_at[c], f_at[c], yp)

    def late(c):
        one, two = refs(c)
        arrived(E.at[c, xi, ra[near - 1]], z_at[c] + 2)

        def inner(i):
            for a in (near, H):
                one(H + 1 + i, a)

        loop(X - 2, 2, inner)
        for x in (H, H + X - 1):
            one(x, H)
        got_corners(c, near, k_at[c] + 2)
        for x in (H, H + X - 1):
            one(x, near)
        for x in (H - 1, H + X):
            one(x, H)

        def outer(i):
            for a in range(H, H + Y):
                FA[p * S + c, i, ra[a] - lo] = two(H + i, a)

        loop(X, 2, outer)

    def product(f, w0, w1):
        def body(i, acc):
            for k in range(2):
                z = [jnp.concatenate([f(2 * i + k, r), w0(2 * i + k, r), w1(2 * i + k, r)], 0) for r in range(Y)]
                hi, lw = split(jnp.concatenate(z, 1))
                acc = acc + lax.dot_general(jnp.concatenate([hi, lw], 0), hi, NT, preferred_element_type=F32)
            return acc

        return lax.fori_loop(0, X // 2, body, jnp.zeros((2 * NB, NB), F32))

    def gram_rest(c):
        for j in (c, c + 2):
            if j not in seen:
                arrived(RQ.at[j], r_at + j)
                seen.add(j)
        GS[c] = product(lambda x, r: FT[c, x, r], lambda x, r: RQ[c, x, r], lambda x, r: RQ[c + 2, x, r])

    def gram_own(c):
        s = p * S + c
        g = GS[c] + product(lambda x, r: FA[s, x, r], lambda x, r: RA[s, x, r], lambda x, r: RA[s + 2, x, r])
        g = jnp.concatenate([g, jnp.zeros((2 * NB, 128 - NB), F32)], 1)
        cross = jnp.concatenate([g[NB:], jnp.zeros((128 - NB, 128), F32)], 0)
        g = g[:NB] + (cross + cross.T)[:NB]
        lane = lax.broadcasted_iota(jnp.int32, (8, 128), 1)
        t0 = jnp.zeros((8, 128), F32)
        t1 = jnp.zeros((8, 128), F32)
        for b_ in range(NV // 8):
            block = g[b_ * 8:b_ * 8 + 8]
            ff = jnp.where(lane < NV, block, 0.0)
            fw = jnp.where(lane >= NV, block, 0.0)
            t0 = t0 + (pltpu.roll(ff, b_ * NV, 1) if b_ else ff)
            t1 = t1 + pltpu.roll(fw, (128 - NV + b_ * NW) % 128, 1)
        for b_ in range(NW // 8):
            ww = jnp.where(lane >= NV, g[NV + b_ * 8:NV + b_ * 8 + 8], 0.0)
            t1 = t1 + pltpu.roll(ww, (128 - NV + (NV // 8 + b_) * NW) % 128, 1)
        PK[c, 0] = t0
        PK[c, 1] = t1

    seen = set()

    def sum_x_start(c):
        RX[mx, c] = PK[c]
        for o in range(1, nx):
            send(PK.at[c], RX.at[mx, c], ax_at[c] + o, ax_at[c] + mx, (cut, lax.rem(mx + o, nx), my))

    def sum_x_end(c):
        for o in range(1, nx):
            t = lax.rem(mx + o, nx)
            arrived(RX.at[t, c], ax_at[c] + t)
        acc = RX[0, c]
        for t in range(1, nx):
            acc = acc + RX[t, c]
        SM[c] = acc
        RZ[kz, c] = acc
        for o in range(1, K):
            t = lax.rem(kz + o, K)
            send(SM.at[c], RZ.at[kz, c], az_at[c] + o, az_at[c] + kz, (cut, mx, t * 2 + p))

    e16r = lax.broadcasted_iota(jnp.int32, (NW, NW), 0)
    e16l = lax.broadcasted_iota(jnp.int32, (NW, NW), 1)
    l32 = lax.broadcasted_iota(jnp.int32, (NV, 128), 1)
    r32 = lax.broadcasted_iota(jnp.int32, (NV, 128), 0)
    eye = jnp.where(l32 == r32 + NV, 1.0, 0.0)

    def factor(c):
        for o in range(1, K):
            t = lax.rem(kz + o, K)
            arrived(RZ.at[t, c], az_at[c] + t)
        acc = RZ[0, c]
        for t in range(1, K):
            acc = acc + RZ[t, c]
        acc = acc * (1.0 / total)
        t0, t1 = acc[0], acc[1]

        def strip(t, at):
            return pltpu.roll(t, 128 - at, 1) if at else t

        ff = jnp.concatenate([strip(t0, b * NV) for b in range(NV // 8)], 0)
        fw = jnp.concatenate([strip(t1, b * NW) for b in range(NV // 8)], 0)
        ww = jnp.concatenate([strip(t1, NV // 8 * NW + b * NW) for b in range(NW // 8)], 0)
        b = jnp.where(e16r == e16l, 2.0, 0.0) - ww[:, :NW]
        fn = fw[:, :NW]
        fb = lax.dot_general(fn, b, NN, precision=HP, preferred_element_type=F32)
        sub = lax.dot_general(fb, fn, NT, precision=HP, preferred_element_type=F32)
        sub = jnp.concatenate([sub, jnp.zeros((NV, 128 - NV), F32)], 1)
        M = jnp.where(l32 < NV, ff - sub, eye)
        wide = jnp.where(l32 < NW, fw, 0.0)
        M = M - pltpu.roll(wide, 2 * NV, 1)
        line = lax.broadcasted_iota(jnp.int32, (NV, 1), 0)
        for j in range(0, NV, 2):
            r0, r1 = M[j:j + 1], M[j + 1:j + 2]
            c0 = jnp.broadcast_to(M[:, j:j + 1], (NV, 128))
            c1 = jnp.broadcast_to(M[:, j + 1:j + 2], (NV, 128))
            p00, p01, p11 = c0[j:j + 1], c1[j:j + 1], c1[j + 1:j + 2]
            inv = 1.0 / (p00 * p11 - p01 * p01)
            g0 = (p11 * r0 - p01 * r1) * inv
            g1 = (p00 * r1 - p01 * r0) * inv
            M = jnp.where(line > j + 1, M - c0 * g0 - c1 * g1, M)
        odd = r32 % 2
        diag = jnp.sum(jnp.where(l32 == r32, M, 0.0), axis=1, keepdims=True)
        side = jnp.sum(jnp.where(l32 == r32 - odd, M, 0.0), axis=1, keepdims=True)
        above = pltpu.roll(M, 1, 0)
        ratio = side / pltpu.roll(jnp.broadcast_to(diag, (NV, 128)), 1, 0)
        M = jnp.where(odd == 1, M - ratio * above, M)
        diag = jnp.sum(jnp.where(l32 == r32, M, 0.0), axis=1, keepdims=True)
        M = M * (1.0 / jnp.sqrt(diag))
        s = p * S + c
        M = pltpu.roll(M, 128 - NV, 1)
        LP[c] = jnp.where(l32 < NB, M, pltpu.roll(wide, 2 * NV, 1))
        send(LP.at[c], LR.at[c], l_at[c], l_at[c], yp)
        LM[s] = M[:, :NB]
        keep_corr(s, wide)

    def keep_corr(s, wide):
        cor[s] = jnp.concatenate([wide, jnp.zeros((128 - NV, 128), F32)], 0).T[:NW, :NV]

    def take(c):
        s = q * S + c
        arrived(LR.at[c], l_at[c])
        wide = LR[c]
        LM[s] = wide[:, :NB]
        keep_corr(s, pltpu.roll(wide, 128 - 2 * NV, 1))
        arrived(FA.at[s], f_at[c])

    stored = []

    def store(src, dst, i):
        stored.append(load(src, dst, i))

    def finish(s, i):
        hi, lw = split(LM[s])
        left = jnp.concatenate([hi, lw], 0)
        left = jnp.concatenate([left, jnp.concatenate([hi, jnp.zeros((NV, NB), BF)], 0)], 1)

        def body(x):
            z = [jnp.concatenate([FA[s, x, r], RA[s, x, r], RA[s + 2, x, r]], 0) for r in range(Y)]
            zh, zl = split(jnp.concatenate(z, 1))
            o = lax.dot_general(left, jnp.concatenate([zh, zl], 0), NN, preferred_element_type=F32)
            o = o[:NV] + o[NV:]
            for r in range(Y):
                out[s, pl.ds(x * Y + r, NV, stride=J), :] = o[:, r * NZ:(r + 1) * NZ]

        loop(X, 2, body)
        store(out.at[s], out_h.at[s], i)

    def finish_own(c):
        finish(p * S + c, c)

    def finish_rest(c):
        take(c)
        finish(q * S + c, S + c)

    end = S - 1
    for c in range(S):
        got_y(c)
        if c < end:
            send_rest_z(c)
        send_x(c, xp_at[c], lq)
        if c == 0:
            send_own_z(end)
            relay_o()
            early_corners(0)
        if c == 1:
            early(0)
            early_corners(1) if c < end else None
    for c in range(1, end):
        early(c)
    late_corners(0)
    gram_rest(0)
    late(0)
    gram_own(0)
    sum_x_start(0)
    for c in range(1, end):
        gram_rest(c)
    early_corners(end)
    sum_x_end(0)
    send_rest_z(end)
    early(end)
    gram_rest(end)
    for c in range(1, end):
        late_corners(c)
        late(c)
        gram_own(c)
        sum_x_start(c)
        factor(c - 1)
        finish_own(c - 1)
        sum_x_end(c)
    late_corners(end)
    late(end)
    gram_own(end)
    sum_x_start(end)
    sum_x_end(end)
    factor(end - 1)
    finish_own(end - 1)
    factor(end)
    for c in range(end - 1):
        finish_rest(c)
    finish_own(end)
    finish_rest(end - 1)
    take(S - 1)
    store(cor, cor_h, 2 * S)
    finish(q * S + S - 1, 2 * S - 1)
    for copy in stored:
        copy.wait()
    for copy in pending:
        copy.wait_send()


def on_device(disorder, slice_bounds, start, ritz):
    nc, nx, ny = (lax.axis_size(a) for a in ("cuts", "lx", "ly"))
    count, NV, X, Y, NZ = start.shape
    NR = ritz.shape[1]
    J = X * Y
    S, R, K = count // 2, 2 * Y, ny // 2
    V = pltpu.VMEM
    D = pltpu.SemaphoreType.DMA
    dims = (nc, nx, ny, count, NV, NR, X, Y, NZ)
    hbm = pl.BlockSpec(memory_space=pl.ANY)
    sems = sem_counts(nx, K, S)
    block, corr = pl.pallas_call(
        functools.partial(kernel, dims),
        out_shape=(jax.ShapeDtypeStruct((count, NV * J, NZ), F32),
                   jax.ShapeDtypeStruct((count, 2 * NR, NV), F32)),
        in_specs=[hbm] * 4,
        out_specs=(hbm, hbm),
        scratch_shapes=[
            V((count, NV * J, NZ), F32),
            V((count, 2 * NR, NV), F32),
            pltpu.SMEM((2, count), F32),
            V((J, NZ), jnp.int32),
            V((count, NV * J, NZ), F32),
            V((count, NR * J, NZ), F32),
            D((2 * S + 3,)),
            V((S, X + 2 * H, R + 2 * H, NV, NZ), F32),
            V((S, X, Y, NV, NZ), F32),
            V((X + 2 * H, R + 2 * H, 1, NZ), F32),
            V((S, X + 2 * H, R + 2 * H, NV, NZ), F32),
            V((count, X, Y, NV, NZ), F32),
            V((S, X, Y, NV, NZ), F32),
            V((count + 2, X, Y, NR, NZ), F32),
            V((S + 2, X, Y, NR, NZ), F32),
            V((S, 2 * (NV + 2 * NR), NV + 2 * NR), F32),
            V((S, 2, 8, 128), F32),
            V((nx, S, 2, 8, 128), F32),
            V((S, 2, 8, 128), F32),
            V((K, S, 2, 8, 128), F32),
            V((count, NV, NV + 2 * NR), F32),
            V((S, NV, 128), F32),
            V((S, NV, 128), F32),
            D((sems,)), D((sems,)),
        ],
        compiler_params=pltpu.CompilerParams(collective_id=0, has_side_effects=True, vmem_limit_bytes=48 << 20),
    )(*[pltpu.with_memory_space_constraint(a, pltpu.HBM) for a in (
        disorder.reshape(J, NZ), slice_bounds.T, start.reshape(count, NV * J, NZ), ritz.reshape(count, NR * J, NZ))])
    return (block.reshape(start.shape), corr)


def solution(mesh):
    in_specs = (
        P("lx", "ly", None),
        P("cuts", None),
        P("cuts", None, "lx", "ly", None),
        P("cuts", None, "lx", "ly", None),
    )
    out_specs = (P("cuts", None, "lx", "ly", None), P("cuts", None, None))
    return jax.shard_map(
        on_device, mesh=mesh, in_specs=in_specs, out_specs=out_specs, check_vma=False
    )
```

```python
import functools

import jax
import jax.numpy as jnp
from jax import lax
from jax.experimental import pallas as pl
from jax.experimental.pallas import tpu as pltpu
from jax.sharding import PartitionSpec as P

LEVELS = 256
MESH = pl.DeviceIdType.MESH
HP = lax.Precision.HIGHEST
H = 2
BF = jnp.bfloat16
F32 = jnp.float32
NT = (((1,), (1,)), ((), ()))
NN = (((1,), (0,)), ((), ()))
TN = (((0,), (0,)), ((), ()))


def sem_counts(nx, K, S):
    return 5 + S * (14 + nx + K) + 2 + (S + 2)


def split(z):
    hi = z.astype(BF)
    return hi, (z - hi.astype(F32)).astype(BF)


def loop(n, unroll, body):
    def step(i, carry):
        for k in range(unroll):
            body(i * unroll + k)
        return carry

    if n % unroll:
        unroll = 1
    lax.fori_loop(0, n // unroll, step, 0)


def kernel(dims, dis_h, bnd_h, start_h, ritz_h, out_h, cor_h, out, cor, bnd, dis, start, ritz, ls, E, T, O, U, FA, FT,
           RA, RQ, GS, PK, RX, SM, RZ, LM, LP, LR, ss, rs):
    nc, nx, ny, count, NV, NR, X, Y, NZ = dims
    S = count // 2
    R = 2 * Y
    J = X * Y
    K = ny // 2
    total = float(J * NZ * nx * ny)
    NW = 2 * NR
    NB = NV + NW
    cut, mx, my = lax.axis_index("cuts"), lax.axis_index("lx"), lax.axis_index("ly")
    p = lax.rem(my, 2)
    q = 1 - p
    kz = my // 2
    yp = (cut, mx, kz * 2 + q)
    zup = (cut, mx, lax.rem(kz + 1, K) * 2 + p)
    zdown = (cut, mx, lax.rem(kz + K - 1, K) * 2 + p)
    xup = (cut, lax.rem(mx + 1, nx), my)
    xdown = (cut, lax.rem(mx + nx - 1, nx), my)
    cup = (lax.rem(cut + 1, nc), mx, my)
    cdown = (lax.rem(cut + nc - 1, nc), mx, my)

    def load(src, dst, i):
        copy = pltpu.make_async_copy(src, dst, ls.at[i])
        copy.start()
        return copy

    barrier = pltpu.get_barrier_semaphore()

    def greet(dev):
        pl.semaphore_signal(barrier, inc=1, device_id=dev, device_id_type=MESH)

    greet(yp)
    for o in range(1, nx):
        greet((cut, lax.rem(mx + o, nx), my))
    for o in range(1, K):
        greet((cut, mx, lax.rem(kz + o, K) * 2 + p))
    greet(cup)
    greet(cdown)

    level_load = load(dis_h, dis, 2 * S)
    away, kept = [], []
    for c in range(S):
        away.append(load(start_h.at[q * S + c], start.at[c], c))
        kept.append(load(start_h.at[p * S + c], start.at[S + c], S + c))
    bound_load = load(bnd_h, bnd, 2 * S + 2)
    ritz_load = load(ritz_h, ritz, 2 * S + 1)

    lo = H + Y * p
    lq = H + Y * q
    xi = pl.ds(H, X)
    def stage_away(c):
        away[c].wait()
        for x in range(X):
            for r in range(Y):
                T[c, x, r] = start[c, pl.ds(x * Y + r, NV, stride=J), :]

    def stage_kept(c):
        kept[c].wait()
        for x in range(X):
            for r in range(Y):
                E[c, H + x, lo + r] = start[S + c, pl.ds(x * Y + r, NV, stride=J), :]

    pending = []
    used = [0]

    def slots(n=1):
        i = used[0]
        used[0] += n
        return i

    def send(src, dst, i, j, dev):
        copy = pltpu.make_async_remote_copy(
            src_ref=src, dst_ref=dst, send_sem=ss.at[i], recv_sem=rs.at[j], device_id=dev, device_id_type=MESH)
        copy.start()
        pending.append(copy)

    def arrived(dst, j):
        pltpu.make_async_remote_copy(
            src_ref=dst, dst_ref=dst, send_sem=rs.at[j], recv_sem=rs.at[j],
            device_id=yp, device_id_type=MESH).wait_recv()

    def rows(at):
        return pl.ds(at, Y)

    o_y, o_z, o_x = slots(), slots(2), slots(2)
    y_at = [slots() for _ in range(S)]
    z_at = [slots(3) for _ in range(S)]
    xo_at = [slots(2) for _ in range(S)]
    xp_at = [slots(2) for _ in range(S)]
    k_at = [slots(4) for _ in range(S)]
    f_at = [slots() for _ in range(S)]
    l_at = [slots() for _ in range(S)]
    c_at = slots(2)
    r_at = slots(S + 2)
    ax_at = [slots(nx) for _ in range(S)]
    az_at = [slots(K) for _ in range(S)]

    def send_y(c):
        send(T.at[c], E.at[c, xi, rows(lo)], y_at[c], y_at[c], yp)

    def send_own_z(c):
        dev = (cut, mx, jnp.where(p == 1, zup[2], zdown[2]))
        dst = jnp.where(p == 1, 0, H + R)
        send(E.at[c, xi, rows(lo)], E.at[c, xi, rows(dst)], z_at[c], z_at[c], dev)

    def send_rest_z(c):
        dev = (cut, mx, jnp.where(q == 1, zup[2], zdown[2]))
        for k in range(2):
            src = jnp.where(q == 1, H + R - 1 - k, H + k)
            dst = jnp.where(q == 1, H - 1 - k, H + R + k)
            send(E.at[c, xi, src], E.at[c, xi, dst], z_at[c] + 1 + k, z_at[c] + 1 + k, dev)

    def send_x(c, base, at):
        send(E.at[c, pl.ds(X, H), rows(at)], E.at[c, pl.ds(0, H), rows(at)], base, base, xup)
        send(E.at[c, pl.ds(H, H), rows(at)], E.at[c, pl.ds(H + X, H), rows(at)], base + 1, base + 1, xdown)

    def got_x(c, base, at):
        arrived(E.at[c, pl.ds(0, H), rows(at)], base)
        arrived(E.at[c, pl.ds(H + X, H), rows(at)], base + 1)

    def send_o(half):
        side = 1 - half
        dev = (cut, mx, jnp.where(half == 1, zup[2], zdown[2]))
        src = jnp.where(half == 1, H + R - 1, H)
        dst = jnp.where(half == 1, 1, H + R)
        send(O.at[xi, src], O.at[xi, dst], o_z + side, o_z + side, dev)

    own = pl.ds(H, R)

    def relay_o():
        arrived(O.at[xi, rows(lq)], o_y)
        send_o(q)
        send(O.at[H + X - 1, own], O.at[H - 1, own], o_x, o_x, xup)
        send(O.at[H, own], O.at[H + X, own], o_x + 1, o_x + 1, xdown)

    level_load.wait()
    for x in range(X):
        for r in range(Y):
            row = dis[pl.ds(x * Y + r, 1), :].astype(F32)
            O[H + x, lo + r] = 16.5 * (row / F32(LEVELS - 1) - 0.5)
    stage_away(0)
    stage_kept(0)
    pl.semaphore_wait(barrier, nx + K + 1)
    send(O.at[xi, rows(lo)], O.at[xi, rows(lo)], o_y, o_y, yp)
    send_y(0)
    send_o(p)
    send_own_z(0)
    send_x(0, xo_at[0], lo)
    for c in range(1, S):
        stage_away(c)
        send_y(c)
        stage_kept(c)
        if c == 1:
            relay_o()
        if c < S - 1:
            send_own_z(c)
        send_x(c, xo_at[c], lo)
    bound_load.wait()
    ritz_load.wait()
    for s in range(count):
        for x in range(X):
            for r in range(Y):
                RA[s + 1, x, r] = ritz[s, pl.ds(x * Y + r, NR, stride=J), :]
    send(RA.at[count], RA.at[0], c_at, c_at, cup)
    send(RA.at[1], RA.at[count + 1], c_at + 1, c_at + 1, cdown)

    arrived(RA.at[0], c_at)
    arrived(RA.at[count + 1], c_at + 1)

    @pl.when(cut == 0)
    def _():
        RA[0] = jnp.zeros((X, Y, NR, NZ), F32)

    @pl.when(cut == nc - 1)
    def _():
        RA[count + 1] = jnp.zeros((X, Y, NR, NZ), F32)

    order = []
    for c in range(S):
        for j in (c, c + 2):
            if j not in order:
                order.append(j)
    for j in order:
        send(RA.at[q * S + j], RQ.at[j], r_at + j, r_at + j, yp)

    def got_y(c):
        arrived(E.at[c, xi, rows(lq)], y_at[c])

    last = R + 2 * H - 1
    ra = [a + p * (last - 2 * a) for a in range(last + 1)]
    near, far = H - 1, H + R

    def point(src, x, a, centre):
        v = src(x, a)
        beside = src(x + 1, a) + src(x - 1, a)
        beside = beside + src(x, a + 1) + src(x, a - 1)
        beside = beside + pltpu.roll(v, 1, 1) + pltpu.roll(v, NZ - 1, 1)
        level = jnp.broadcast_to(O[x, ra[a]] - centre, (NV, NZ))
        return level * v - beside

    def refs(c):
        s = p * S + c
        centre = (bnd[0, s] + bnd[1, s]) / 2.0

        def from_e(x, a):
            return E[c, x, ra[a]]

        def from_u(x, a):
            return U[c, x, ra[a]]

        def one(x, a):
            U[c, x, ra[a]] = point(from_e, x, a, centre)

        def two(x, a):
            return point(from_u, x, a, centre) * (2.0 / 256.0) - from_e(x, a)

        return one, two

    def corners(c, a, k):
        send(E.at[c, H + X - 1, ra[a]], E.at[c, H - 1, ra[a]], k, k, xup)
        send(E.at[c, H, ra[a]], E.at[c, H + X, ra[a]], k + 1, k + 1, xdown)

    def got_corners(c, a, k):
        arrived(E.at[c, H - 1, ra[a]], k)
        arrived(E.at[c, H + X, ra[a]], k + 1)

    def early_corners(c):
        arrived(E.at[c, xi, rows(jnp.where(p == 1, 0, H + R))], z_at[c])
        corners(c, far, k_at[c])

    def late_corners(c):
        arrived(E.at[c, xi, ra[near]], z_at[c] + 1)
        corners(c, near, k_at[c] + 2)

    def got_o():
        arrived(O.at[xi, H - 1], o_z)
        arrived(O.at[xi, H + R], o_z + 1)
        arrived(O.at[H - 1, own], o_x)
        arrived(O.at[H + X, own], o_x + 1)

    def early(c):
        one, two = refs(c)
        got_x(c, xo_at[c], lo)
        got_x(c, xp_at[c], lq)
        if c == 0:
            got_o()

        def inner(i):
            for a in range(H + 1, far + 1):
                one(H + 1 + i, a)

        loop(X - 2, 2, inner)
        for x in (H, H + X - 1):
            for a in range(H + 1, far):
                one(x, a)
        for x in (H - 1, H + X):
            for a in range(H + 1, far - 1):
                one(x, a)
        got_corners(c, far, k_at[c])
        for x in (H, H + X - 1):
            one(x, far)
        for x in (H - 1, H + X):
            one(x, far - 1)

        def outer(i):
            for a in range(H + Y, far):
                FT[c, i, ra[a] - lq] = two(H + i, a)

        loop(X, 2, outer)
        send(FT.at[c], FA.at[p * S + c], f_at[c], f_at[c], yp)

    def late(c):
        one, two = refs(c)
        arrived(E.at[c, xi, ra[near - 1]], z_at[c] + 2)

        def inner(i):
            for a in (near, H):
                one(H + 1 + i, a)

        loop(X - 2, 2, inner)
        for x in (H, H + X - 1):
            one(x, H)
        got_corners(c, near, k_at[c] + 2)
        for x in (H, H + X - 1):
            one(x, near)
        for x in (H - 1, H + X):
            one(x, H)

        def outer(i):
            for a in range(H, H + Y):
                FA[p * S + c, i, ra[a] - lo] = two(H + i, a)

        loop(X, 2, outer)

    def product(f, w0, w1):
        def body(i, acc):
            for k in range(2):
                z = [jnp.concatenate([f(2 * i + k, r), w0(2 * i + k, r), w1(2 * i + k, r)], 0) for r in range(Y)]
                hi, lw = split(jnp.concatenate(z, 1))
                acc = acc + lax.dot_general(jnp.concatenate([hi, lw], 0), hi, NT, preferred_element_type=F32)
            return acc

        return lax.fori_loop(0, X // 2, body, jnp.zeros((2 * NB, NB), F32))

    def gram_rest(c):
        for j in (c, c + 2):
            if j not in seen:
                arrived(RQ.at[j], r_at + j)
                seen.add(j)
        GS[c] = product(lambda x, r: FT[c, x, r], lambda x, r: RQ[c, x, r], lambda x, r: RQ[c + 2, x, r])

    def gram_own(c):
        s = p * S + c
        g = GS[c] + product(lambda x, r: FA[s, x, r], lambda x, r: RA[s, x, r], lambda x, r: RA[s + 2, x, r])
        g = jnp.concatenate([g, jnp.zeros((2 * NB, 128 - NB), F32)], 1)
        cross = jnp.concatenate([g[NB:], jnp.zeros((128 - NB, 128), F32)], 0)
        g = g[:NB] + (cross + cross.T)[:NB]
        lane = lax.broadcasted_iota(jnp.int32, (8, 128), 1)
        t0 = jnp.zeros((8, 128), F32)
        t1 = jnp.zeros((8, 128), F32)
        for b_ in range(NV // 8):
            block = g[b_ * 8:b_ * 8 + 8]
            ff = jnp.where(lane < NV, block, 0.0)
            fw = jnp.where(lane >= NV, block, 0.0)
            t0 = t0 + (pltpu.roll(ff, b_ * NV, 1) if b_ else ff)
            t1 = t1 + pltpu.roll(fw, (128 - NV + b_ * NW) % 128, 1)
        for b_ in range(NW // 8):
            ww = jnp.where(lane >= NV, g[NV + b_ * 8:NV + b_ * 8 + 8], 0.0)
            t1 = t1 + pltpu.roll(ww, (128 - NV + (NV // 8 + b_) * NW) % 128, 1)
        PK[c, 0] = t0
        PK[c, 1] = t1

    seen = set()

    def sum_x_start(c):
        RX[mx, c] = PK[c]
        for o in range(1, nx):
            send(PK.at[c], RX.at[mx, c], ax_at[c] + o, ax_at[c] + mx, (cut, lax.rem(mx + o, nx), my))

    def sum_x_end(c):
        for o in range(1, nx):
            t = lax.rem(mx + o, nx)
            arrived(RX.at[t, c], ax_at[c] + t)
        acc = RX[0, c]
        for t in range(1, nx):
            acc = acc + RX[t, c]
        SM[c] = acc
        RZ[kz, c] = acc
        for o in range(1, K):
            t = lax.rem(kz + o, K)
            send(SM.at[c], RZ.at[kz, c], az_at[c] + o, az_at[c] + kz, (cut, mx, t * 2 + p))

    e16r = lax.broadcasted_iota(jnp.int32, (NW, NW), 0)
    e16l = lax.broadcasted_iota(jnp.int32, (NW, NW), 1)
    l32 = lax.broadcasted_iota(jnp.int32, (NV, 128), 1)
    r32 = lax.broadcasted_iota(jnp.int32, (NV, 128), 0)
    eye = jnp.where(l32 == r32 + NV, 1.0, 0.0)

    def factor(c):
        for o in range(1, K):
            t = lax.rem(kz + o, K)
            arrived(RZ.at[t, c], az_at[c] + t)
        acc = RZ[0, c]
        for t in range(1, K):
            acc = acc + RZ[t, c]
        acc = acc * (1.0 / total)
        t0, t1 = acc[0], acc[1]

        def strip(t, at):
            return pltpu.roll(t, 128 - at, 1) if at else t

        ff = jnp.concatenate([strip(t0, b * NV) for b in range(NV // 8)], 0)
        fw = jnp.concatenate([strip(t1, b * NW) for b in range(NV // 8)], 0)
        ww = jnp.concatenate([strip(t1, NV // 8 * NW + b * NW) for b in range(NW // 8)], 0)
        b = jnp.where(e16r == e16l, 2.0, 0.0) - ww[:, :NW]
        fn = fw[:, :NW]
        fb = lax.dot_general(fn, b, NN, precision=HP, preferred_element_type=F32)
        sub = lax.dot_general(fb, fn, NT, precision=HP, preferred_element_type=F32)
        sub = jnp.concatenate([sub, jnp.zeros((NV, 128 - NV), F32)], 1)
        M = jnp.where(l32 < NV, ff - sub, eye)
        wide = jnp.where(l32 < NW, fw, 0.0)
        M = M - pltpu.roll(wide, 2 * NV, 1)
        line = lax.broadcasted_iota(jnp.int32, (NV, 1), 0)
        for j in range(0, NV, 2):
            r0, r1 = M[j:j + 1], M[j + 1:j + 2]
            c0 = jnp.broadcast_to(M[:, j:j + 1], (NV, 128))
            c1 = jnp.broadcast_to(M[:, j + 1:j + 2], (NV, 128))
            p00, p01, p11 = c0[j:j + 1], c1[j:j + 1], c1[j + 1:j + 2]
            inv = 1.0 / (p00 * p11 - p01 * p01)
            g0 = (p11 * r0 - p01 * r1) * inv
            g1 = (p00 * r1 - p01 * r0) * inv
            M = jnp.where(line > j + 1, M - c0 * g0 - c1 * g1, M)
        odd = r32 % 2
        diag = jnp.sum(jnp.where(l32 == r32, M, 0.0), axis=1, keepdims=True)
        side = jnp.sum(jnp.where(l32 == r32 - odd, M, 0.0), axis=1, keepdims=True)
        above = pltpu.roll(M, 1, 0)
        ratio = side / pltpu.roll(jnp.broadcast_to(diag, (NV, 128)), 1, 0)
        M = jnp.where(odd == 1, M - ratio * above, M)
        diag = jnp.sum(jnp.where(l32 == r32, M, 0.0), axis=1, keepdims=True)
        M = M * (1.0 / jnp.sqrt(diag))
        s = p * S + c
        M = pltpu.roll(M, 128 - NV, 1)
        LP[c] = jnp.where(l32 < NB, M, pltpu.roll(wide, 2 * NV, 1))
        send(LP.at[c], LR.at[c], l_at[c], l_at[c], yp)
        LM[s] = M[:, :NB]
        keep_corr(s, wide)

    def keep_corr(s, wide):
        cor[s] = jnp.concatenate([wide, jnp.zeros((128 - NV, 128), F32)], 0).T[:NW, :NV]

    def take(c):
        s = q * S + c
        arrived(LR.at[c], l_at[c])
        wide = LR[c]
        LM[s] = wide[:, :NB]
        keep_corr(s, pltpu.roll(wide, 128 - 2 * NV, 1))
        arrived(FA.at[s], f_at[c])

    stored = []

    def store(src, dst, i):
        stored.append(load(src, dst, i))

    def finish(s, i):
        hi, lw = split(LM[s])
        left = jnp.concatenate([hi, lw], 0)
        left = jnp.concatenate([left, jnp.concatenate([hi, jnp.zeros((NV, NB), BF)], 0)], 1)

        def body(x):
            z = [jnp.concatenate([FA[s, x, r], RA[s, x, r], RA[s + 2, x, r]], 0) for r in range(Y)]
            zh, zl = split(jnp.concatenate(z, 1))
            o = lax.dot_general(left, jnp.concatenate([zh, zl], 0), NN, preferred_element_type=F32)
            o = o[:NV] + o[NV:]
            for r in range(Y):
                out[s, pl.ds(x * Y + r, NV, stride=J), :] = o[:, r * NZ:(r + 1) * NZ]

        loop(X, 2, body)
        store(out.at[s], out_h.at[s], i)

    def finish_own(c):
        finish(p * S + c, c)

    def finish_rest(c):
        take(c)
        finish(q * S + c, S + c)

    end = S - 1
    for c in range(S):
        got_y(c)
        if c < end:
            send_rest_z(c)
        send_x(c, xp_at[c], lq)
        if c == 0:
            send_own_z(end)
            early_corners(0)
        if c == 1:
            early_corners(1) if c < end else None
            early(0)
    for c in range(2, end):
        early_corners(c)
    late_corners(0)
    for c in range(1, end):
        early(c)
    gram_rest(0)
    late(0)
    gram_own(0)
    sum_x_start(0)
    for c in range(1, end):
        gram_rest(c)
    early_corners(end)
    sum_x_end(0)
    send_rest_z(end)
    early(end)
    for c in range(1, end):
        late_corners(c)
    gram_rest(end)
    for c in range(1, end):
        late(c)
        gram_own(c)
        sum_x_start(c)
        factor(c - 1)
        if c == end - 1:
            late_corners(end)
        finish_own(c - 1)
        sum_x_end(c)
    late(end)
    gram_own(end)
    sum_x_start(end)
    sum_x_end(end)
    factor(end - 1)
    finish_own(end - 1)
    factor(end)
    for c in range(end - 1):
        finish_rest(c)
    finish_own(end)
    finish_rest(end - 1)
    take(S - 1)
    store(cor, cor_h, 2 * S)
    finish(q * S + S - 1, 2 * S - 1)
    for copy in stored:
        copy.wait()
    for copy in pending:
        copy.wait_send()


def on_device(disorder, slice_bounds, start, ritz):
    nc, nx, ny = (lax.axis_size(a) for a in ("cuts", "lx", "ly"))
    count, NV, X, Y, NZ = start.shape
    NR = ritz.shape[1]
    J = X * Y
    S, R, K = count // 2, 2 * Y, ny // 2
    V = pltpu.VMEM
    D = pltpu.SemaphoreType.DMA
    dims = (nc, nx, ny, count, NV, NR, X, Y, NZ)
    hbm = pl.BlockSpec(memory_space=pl.ANY)
    sems = sem_counts(nx, K, S)
    block, corr = pl.pallas_call(
        functools.partial(kernel, dims),
        out_shape=(jax.ShapeDtypeStruct((count, NV * J, NZ), F32),
                   jax.ShapeDtypeStruct((count, 2 * NR, NV), F32)),
        in_specs=[hbm] * 4,
        out_specs=(hbm, hbm),
        scratch_shapes=[
            V((count, NV * J, NZ), F32),
            V((count, 2 * NR, NV), F32),
            pltpu.SMEM((2, count), F32),
            V((J, NZ), jnp.int32),
            V((count, NV * J, NZ), F32),
            V((count, NR * J, NZ), F32),
            D((2 * S + 3,)),
            V((S, X + 2 * H, R + 2 * H, NV, NZ), F32),
            V((S, X, Y, NV, NZ), F32),
            V((X + 2 * H, R + 2 * H, 1, NZ), F32),
            V((S, X + 2 * H, R + 2 * H, NV, NZ), F32),
            V((count, X, Y, NV, NZ), F32),
            V((S, X, Y, NV, NZ), F32),
            V((count + 2, X, Y, NR, NZ), F32),
            V((S + 2, X, Y, NR, NZ), F32),
            V((S, 2 * (NV + 2 * NR), NV + 2 * NR), F32),
            V((S, 2, 8, 128), F32),
            V((nx, S, 2, 8, 128), F32),
            V((S, 2, 8, 128), F32),
            V((K, S, 2, 8, 128), F32),
            V((count, NV, NV + 2 * NR), F32),
            V((S, NV, 128), F32),
            V((S, NV, 128), F32),
            D((sems,)), D((sems,)),
        ],
        compiler_params=pltpu.CompilerParams(collective_id=0, has_side_effects=True, vmem_limit_bytes=48 << 20),
    )(*[pltpu.with_memory_space_constraint(a, pltpu.HBM) for a in (
        disorder.reshape(J, NZ), slice_bounds.T, start.reshape(count, NV * J, NZ), ritz.reshape(count, NR * J, NZ))])
    return (block.reshape(start.shape), corr)


def solution(mesh):
    in_specs = (
        P("lx", "ly", None),
        P("cuts", None),
        P("cuts", None, "lx", "ly", None),
        P("cuts", None, "lx", "ly", None),
    )
    out_specs = (P("cuts", None, "lx", "ly", None), P("cuts", None, None))
    return jax.shard_map(
        on_device, mesh=mesh, in_specs=in_specs, out_specs=out_specs, check_vma=False
    )
```

```python
import functools

import jax
import jax.numpy as jnp
from jax import lax
from jax.experimental import pallas as pl
from jax.experimental.pallas import tpu as pltpu
from jax.sharding import PartitionSpec as P

LEVELS = 256
MESH = pl.DeviceIdType.MESH
HP = lax.Precision.HIGHEST
H = 2
BF = jnp.bfloat16
F32 = jnp.float32
NT = (((1,), (1,)), ((), ()))
NN = (((1,), (0,)), ((), ()))
TN = (((0,), (0,)), ((), ()))


def direct_sum(nx, K):
    return nx * K <= 16


def sem_counts(nx, K, S):
    return 5 + S * 14 + 2 + (S + 2) + 2 * (nx * K if direct_sum(nx, K) else nx + K)


def split(z):
    hi = z.astype(BF)
    return hi, (z - hi.astype(F32)).astype(BF)


def loop(n, unroll, body):
    def step(i, carry):
        for k in range(unroll):
            body(i * unroll + k)
        return carry

    if n % unroll:
        unroll = 1
    lax.fori_loop(0, n // unroll, step, 0)


def kernel(dims, dis_h, bnd_h, start_h, ritz_h, out_h, cor_h, out, cor, bnd, dis, start, ritz, ls, E, T, O, U, FA, FT,
           RA, RQ, GS, PK, RX, SM, RZ, LM, LP, LR, ss, rs):
    nc, nx, ny, count, NV, NR, X, Y, NZ = dims
    S = count // 2
    R = 2 * Y
    J = X * Y
    K = ny // 2
    total = float(J * NZ * nx * ny)
    NW = 2 * NR
    NB = NV + NW
    cut, mx, my = lax.axis_index("cuts"), lax.axis_index("lx"), lax.axis_index("ly")
    p = lax.rem(my, 2)
    q = 1 - p
    kz = my // 2
    yp = (cut, mx, kz * 2 + q)
    zup = (cut, mx, lax.rem(kz + 1, K) * 2 + p)
    zdown = (cut, mx, lax.rem(kz + K - 1, K) * 2 + p)
    xup = (cut, lax.rem(mx + 1, nx), my)
    xdown = (cut, lax.rem(mx + nx - 1, nx), my)
    cup = (lax.rem(cut + 1, nc), mx, my)
    cdown = (lax.rem(cut + nc - 1, nc), mx, my)

    def load(src, dst, i):
        copy = pltpu.make_async_copy(src, dst, ls.at[i])
        copy.start()
        return copy

    barrier = pltpu.get_barrier_semaphore()

    def greet(dev):
        pl.semaphore_signal(barrier, inc=1, device_id=dev, device_id_type=MESH)

    greet(yp)
    if direct_sum(nx, K):
        for o in range(1, nx * K):
            t = lax.rem(mx * K + kz + o, nx * K)
            greet((cut, t // K, lax.rem(t, K) * 2 + p))
        greeted = nx * K + 2
    else:
        for o in range(1, nx):
            greet((cut, lax.rem(mx + o, nx), my))
        for o in range(1, K):
            greet((cut, mx, lax.rem(kz + o, K) * 2 + p))
        greeted = nx + K + 1
    greet(cup)
    greet(cdown)

    level_load = load(dis_h, dis, 2 * S)
    away, kept = [], []
    for c in range(S):
        away.append(load(start_h.at[q * S + c], start.at[c], c))
        kept.append(load(start_h.at[p * S + c], start.at[S + c], S + c))
    bound_load = load(bnd_h, bnd, 2 * S + 2)
    ritz_load = load(ritz_h, ritz, 2 * S + 1)

    lo = H + Y * p
    lq = H + Y * q
    xi = pl.ds(H, X)
    def stage_away(c):
        away[c].wait()
        for x in range(X):
            for r in range(Y):
                T[c, x, r] = start[c, pl.ds(x * Y + r, NV, stride=J), :]

    def stage_kept(c):
        kept[c].wait()
        for x in range(X):
            for r in range(Y):
                E[c, H + x, lo + r] = start[S + c, pl.ds(x * Y + r, NV, stride=J), :]

    pending = []
    used = [0]

    def slots(n=1):
        i = used[0]
        used[0] += n
        return i

    def send(src, dst, i, j, dev):
        copy = pltpu.make_async_remote_copy(
            src_ref=src, dst_ref=dst, send_sem=ss.at[i], recv_sem=rs.at[j], device_id=dev, device_id_type=MESH)
        copy.start()
        pending.append(copy)

    def flush(n):
        for copy in pending[:n]:
            copy.wait_send()
        del pending[:n]

    def arrived(dst, j):
        pltpu.make_async_remote_copy(
            src_ref=dst, dst_ref=dst, send_sem=rs.at[j], recv_sem=rs.at[j],
            device_id=yp, device_id_type=MESH).wait_recv()

    def rows(at):
        return pl.ds(at, Y)

    o_y, o_z, o_x = slots(), slots(2), slots(2)
    y_at = [slots() for _ in range(S)]
    z_at = [slots(3) for _ in range(S)]
    xo_at = [slots(2) for _ in range(S)]
    xp_at = [slots(2) for _ in range(S)]
    k_at = [slots(4) for _ in range(S)]
    f_at = [slots() for _ in range(S)]
    l_at = [slots() for _ in range(S)]
    c_at = slots(2)
    r_at = slots(S + 2)
    groups = [list(range(S - 1)), [S - 1]]
    direct = direct_sum(nx, K)
    span = nx * K if direct else K
    me = mx * K + kz if direct else kz
    ax_at = [0 if direct else slots(nx) for _ in groups]
    az_at = [slots(span) for _ in groups]

    def send_y(c):
        send(T.at[c], E.at[c, xi, rows(lo)], y_at[c], y_at[c], yp)

    def send_own_z(c):
        dev = (cut, mx, jnp.where(p == 1, zup[2], zdown[2]))
        dst = jnp.where(p == 1, 0, H + R)
        send(E.at[c, xi, rows(lo)], E.at[c, xi, rows(dst)], z_at[c], z_at[c], dev)

    def send_rest_z(c):
        dev = (cut, mx, jnp.where(q == 1, zup[2], zdown[2]))
        for k in range(2):
            src = jnp.where(q == 1, H + R - 1 - k, H + k)
            dst = jnp.where(q == 1, H - 1 - k, H + R + k)
            send(E.at[c, xi, src], E.at[c, xi, dst], z_at[c] + 1 + k, z_at[c] + 1 + k, dev)

    def send_x(c, base, at):
        send(E.at[c, pl.ds(X, H), rows(at)], E.at[c, pl.ds(0, H), rows(at)], base, base, xup)
        send(E.at[c, pl.ds(H, H), rows(at)], E.at[c, pl.ds(H + X, H), rows(at)], base + 1, base + 1, xdown)

    def got_x(c, base, at):
        arrived(E.at[c, pl.ds(0, H), rows(at)], base)
        arrived(E.at[c, pl.ds(H + X, H), rows(at)], base + 1)

    def send_o(half):
        side = 1 - half
        dev = (cut, mx, jnp.where(half == 1, zup[2], zdown[2]))
        src = jnp.where(half == 1, H + R - 1, H)
        dst = jnp.where(half == 1, 1, H + R)
        send(O.at[xi, src], O.at[xi, dst], o_z + side, o_z + side, dev)

    own = pl.ds(H, R)

    def relay_o():
        arrived(O.at[xi, rows(lq)], o_y)
        send_o(q)
        send(O.at[H + X - 1, own], O.at[H - 1, own], o_x, o_x, xup)
        send(O.at[H, own], O.at[H + X, own], o_x + 1, o_x + 1, xdown)

    level_load.wait()
    for x in range(X):
        for r in range(Y):
            row = dis[pl.ds(x * Y + r, 1), :].astype(F32)
            O[H + x, lo + r] = 16.5 * (row / F32(LEVELS - 1) - 0.5)
    stage_away(0)
    stage_kept(0)
    pl.semaphore_wait(barrier, greeted)
    send(O.at[xi, rows(lo)], O.at[xi, rows(lo)], o_y, o_y, yp)
    send_y(0)
    send_o(p)
    send_own_z(0)
    send_x(0, xo_at[0], lo)
    for c in range(1, S):
        stage_away(c)
        send_y(c)
        stage_kept(c)
        if c == 1:
            relay_o()
        if c < S - 1:
            send_own_z(c)
        send_x(c, xo_at[c], lo)
    bound_load.wait()
    ritz_load.wait()
    for s in range(count):
        for x in range(X):
            for r in range(Y):
                RA[s + 1, x, r] = ritz[s, pl.ds(x * Y + r, NR, stride=J), :]
    send(RA.at[count], RA.at[0], c_at, c_at, cup)
    send(RA.at[1], RA.at[count + 1], c_at + 1, c_at + 1, cdown)

    arrived(RA.at[0], c_at)
    arrived(RA.at[count + 1], c_at + 1)

    @pl.when(cut == 0)
    def _():
        RA[0] = jnp.zeros((X, Y, NR, NZ), F32)

    @pl.when(cut == nc - 1)
    def _():
        RA[count + 1] = jnp.zeros((X, Y, NR, NZ), F32)

    order = []
    for c in range(S):
        for j in (c, c + 2):
            if j not in order:
                order.append(j)
    for j in order:
        send(RA.at[q * S + j], RQ.at[j], r_at + j, r_at + j, yp)

    def got_y(c):
        arrived(E.at[c, xi, rows(lq)], y_at[c])

    last = R + 2 * H - 1
    ra = [a + p * (last - 2 * a) for a in range(last + 1)]
    near, far = H - 1, H + R

    def point(src, x, a, centre):
        v = src(x, a)
        beside = src(x + 1, a) + src(x - 1, a)
        beside = beside + src(x, a + 1) + src(x, a - 1)
        beside = beside + pltpu.roll(v, 1, 1) + pltpu.roll(v, NZ - 1, 1)
        level = jnp.broadcast_to(O[x, ra[a]] - centre, (NV, NZ))
        return level * v - beside

    def refs(c):
        s = p * S + c
        centre = (bnd[0, s] + bnd[1, s]) / 2.0

        def from_e(x, a):
            return E[c, x, ra[a]]

        def from_u(x, a):
            return U[c, x, ra[a]]

        def one(x, a):
            U[c, x, ra[a]] = point(from_e, x, a, centre)

        def two(x, a):
            return point(from_u, x, a, centre) * (2.0 / 256.0) - from_e(x, a)

        return one, two

    def corners(c, a, k):
        send(E.at[c, H + X - 1, ra[a]], E.at[c, H - 1, ra[a]], k, k, xup)
        send(E.at[c, H, ra[a]], E.at[c, H + X, ra[a]], k + 1, k + 1, xdown)

    def got_corners(c, a, k):
        arrived(E.at[c, H - 1, ra[a]], k)
        arrived(E.at[c, H + X, ra[a]], k + 1)

    def early_corners(c):
        arrived(E.at[c, xi, rows(jnp.where(p == 1, 0, H + R))], z_at[c])
        corners(c, far, k_at[c])

    def late_corners(c):
        arrived(E.at[c, xi, ra[near]], z_at[c] + 1)
        corners(c, near, k_at[c] + 2)

    def got_o():
        arrived(O.at[xi, H - 1], o_z)
        arrived(O.at[xi, H + R], o_z + 1)
        arrived(O.at[H - 1, own], o_x)
        arrived(O.at[H + X, own], o_x + 1)

    def early(c):
        one, two = refs(c)
        got_x(c, xo_at[c], lo)
        got_x(c, xp_at[c], lq)
        if c == 0:
            got_o()

        def inner(i):
            for a in range(H + 1, far + 1):
                one(H + 1 + i, a)

        loop(X - 2, 2, inner)
        for x in (H, H + X - 1):
            for a in range(H + 1, far):
                one(x, a)
        for x in (H - 1, H + X):
            for a in range(H + 1, far - 1):
                one(x, a)
        got_corners(c, far, k_at[c])
        for x in (H, H + X - 1):
            one(x, far)
        for x in (H - 1, H + X):
            one(x, far - 1)

        def outer(i):
            for a in range(H + Y, far):
                FT[c, i, ra[a] - lq] = two(H + i, a)

        loop(X, 2, outer)
        send(FT.at[c], FA.at[p * S + c], f_at[c], f_at[c], yp)

    def late(c):
        one, two = refs(c)
        arrived(E.at[c, xi, ra[near - 1]], z_at[c] + 2)

        def inner(i):
            for a in (near, H):
                one(H + 1 + i, a)

        loop(X - 2, 2, inner)
        for x in (H, H + X - 1):
            one(x, H)
        got_corners(c, near, k_at[c] + 2)
        for x in (H, H + X - 1):
            one(x, near)
        for x in (H - 1, H + X):
            one(x, H)

        s = p * S + c

        def outer(i, acc):
            for k in range(2):
                x = 2 * i + k
                for a in range(H, H + Y):
                    FA[s, x, ra[a] - lo] = two(H + x, a)
                z = [jnp.concatenate([FA[s, x, r], RA[s, x, r], RA[s + 2, x, r]], 0) for r in range(Y)]
                acc = acc + square(z)
            return acc

        gram_pack(c, lax.fori_loop(0, X // 2, outer, GS[c]))

    def square(z):
        hi, lw = split(jnp.concatenate(z, 1))
        return lax.dot_general(jnp.concatenate([hi, lw], 0), hi, NT, preferred_element_type=F32)

    def product(f, w0, w1):
        def body(i, acc):
            for k in range(2):
                z = [jnp.concatenate([f(2 * i + k, r), w0(2 * i + k, r), w1(2 * i + k, r)], 0) for r in range(Y)]
                acc = acc + square(z)
            return acc

        return lax.fori_loop(0, X // 2, body, jnp.zeros((2 * NB, NB), F32))

    def gram_rest(c):
        for j in (c, c + 2):
            if j not in seen:
                arrived(RQ.at[j], r_at + j)
                seen.add(j)
        GS[c] = product(lambda x, r: FT[c, x, r], lambda x, r: RQ[c, x, r], lambda x, r: RQ[c + 2, x, r])

    def gram_pack(c, g):
        g = jnp.concatenate([g, jnp.zeros((2 * NB, 128 - NB), F32)], 1)
        cross = jnp.concatenate([g[NB:], jnp.zeros((128 - NB, 128), F32)], 0)
        g = g[:NB] + (cross + cross.T)[:NB]
        lane = lax.broadcasted_iota(jnp.int32, (8, 128), 1)
        t0 = jnp.zeros((8, 128), F32)
        t1 = jnp.zeros((8, 128), F32)
        for b_ in range(NV // 8):
            block = g[b_ * 8:b_ * 8 + 8]
            ff = jnp.where(lane < NV, block, 0.0)
            fw = jnp.where(lane >= NV, block, 0.0)
            t0 = t0 + (pltpu.roll(ff, b_ * NV, 1) if b_ else ff)
            t1 = t1 + pltpu.roll(fw, (128 - NV + b_ * NW) % 128, 1)
        for b_ in range(NW // 8):
            ww = jnp.where(lane >= NV, g[NV + b_ * 8:NV + b_ * 8 + 8], 0.0)
            t1 = t1 + pltpu.roll(ww, (128 - NV + (NV // 8 + b_) * NW) % 128, 1)
        PK[c, 0] = t0
        PK[c, 1] = t1

    seen = set()

    def spread(k, src):
        cs = groups[k]
        part = pl.ds(cs[0], len(cs))
        for o in range(1, span):
            t = lax.rem(me + o, span)
            x, z = (t // K, lax.rem(t, K)) if direct else (mx, t)
            send(src.at[part], RZ.at[me, part], az_at[k] + o, az_at[k] + me, (cut, x, z * 2 + p))

    def sum_start(k):
        cs = groups[k]
        part = pl.ds(cs[0], len(cs))
        for c in cs:
            if direct:
                RZ[me, c] = PK[c]
            else:
                RX[mx, c] = PK[c]
        if direct:
            spread(k, PK)
            return
        for o in range(1, nx):
            send(PK.at[part], RX.at[mx, part], ax_at[k] + o, ax_at[k] + mx, (cut, lax.rem(mx + o, nx), my))

    def sum_more(k):
        if direct:
            return
        cs = groups[k]
        part = pl.ds(cs[0], len(cs))
        for o in range(1, nx):
            t = lax.rem(mx + o, nx)
            arrived(RX.at[t, part], ax_at[k] + t)
        for c in cs:
            acc = RX[0, c]
            for t in range(1, nx):
                acc = acc + RX[t, c]
            SM[c] = acc
            RZ[kz, c] = acc
        spread(k, SM)

    e16r = lax.broadcasted_iota(jnp.int32, (NW, NW), 0)
    e16l = lax.broadcasted_iota(jnp.int32, (NW, NW), 1)
    l32 = lax.broadcasted_iota(jnp.int32, (NV, 128), 1)
    r32 = lax.broadcasted_iota(jnp.int32, (NV, 128), 0)
    eye = jnp.where(l32 == r32 + NV, 1.0, 0.0)

    line = lax.broadcasted_iota(jnp.int32, (NV, 1), 0)
    odd = r32 % 2

    def strip(t, at):
        return pltpu.roll(t, 128 - at, 1) if at else t

    def cleaned(c):
        acc = RZ[0, c]
        for t in range(1, span):
            acc = acc + RZ[t, c]
        acc = acc * (1.0 / total)
        t0, t1 = acc[0], acc[1]
        ff = jnp.concatenate([strip(t0, b * NV) for b in range(NV // 8)], 0)
        fw = jnp.concatenate([strip(t1, b * NW) for b in range(NV // 8)], 0)
        ww = jnp.concatenate([strip(t1, NV // 8 * NW + b * NW) for b in range(NW // 8)], 0)
        b = jnp.where(e16r == e16l, 2.0, 0.0) - ww[:, :NW]
        fn = fw[:, :NW]
        fb = lax.dot_general(fn, b, NN, precision=HP, preferred_element_type=F32)
        sub = lax.dot_general(fb, fn, NT, precision=HP, preferred_element_type=F32)
        sub = jnp.concatenate([sub, jnp.zeros((NV, 128 - NV), F32)], 1)
        wide = jnp.where(l32 < NW, fw, 0.0)
        return jnp.where(l32 < NV, ff - sub, eye) - pltpu.roll(wide, 2 * NV, 1), wide

    def eliminate(M, j):
        r0, r1 = M[j:j + 1], M[j + 1:j + 2]
        c0 = jnp.broadcast_to(M[:, j:j + 1], (NV, 128))
        c1 = jnp.broadcast_to(M[:, j + 1:j + 2], (NV, 128))
        p00, p01, p11 = c0[j:j + 1], c1[j:j + 1], c1[j + 1:j + 2]
        inv = 1.0 / (p00 * p11 - p01 * p01)
        g0 = (p11 * r0 - p01 * r1) * inv
        g1 = (p00 * r1 - p01 * r0) * inv
        return jnp.where(line > j + 1, M - c0 * g0 - c1 * g1, M)

    def scaled(M):
        diag = jnp.sum(jnp.where(l32 == r32, M, 0.0), axis=1, keepdims=True)
        side = jnp.sum(jnp.where(l32 == r32 - odd, M, 0.0), axis=1, keepdims=True)
        ratio = side / pltpu.roll(jnp.broadcast_to(diag, (NV, 128)), 1, 0)
        M = jnp.where(odd == 1, M - ratio * pltpu.roll(M, 1, 0), M)
        diag = jnp.sum(jnp.where(l32 == r32, M, 0.0), axis=1, keepdims=True)
        return pltpu.roll(M * (1.0 / jnp.sqrt(diag)), 128 - NV, 1)

    def factor(k):
        cs = groups[k]
        part = pl.ds(cs[0], len(cs))
        for o in range(1, span):
            t = lax.rem(me + o, span)
            arrived(RZ.at[t, part], az_at[k] + t)
        both = [cleaned(c) for c in cs]
        mats = [m for m, _ in both]
        for j in range(0, NV, 2):
            mats = [eliminate(m, j) for m in mats]
        mats = [scaled(m) for m in mats]
        for i, c in enumerate(cs):
            LP[c] = jnp.where(l32 < NB, mats[i], pltpu.roll(both[i][1], 2 * NV, 1))
            send(LP.at[c], LR.at[c], l_at[c], l_at[c], yp)
        for i, c in enumerate(cs):
            LM[p * S + c] = mats[i][:, :NB]
            keep_corr(p * S + c, both[i][1])

    def keep_corr(s, wide):
        cor[s] = jnp.concatenate([wide, jnp.zeros((128 - NV, 128), F32)], 0).T[:NW, :NV]

    def take(c):
        s = q * S + c
        arrived(LR.at[c], l_at[c])
        wide = LR[c]
        LM[s] = wide[:, :NB]
        keep_corr(s, pltpu.roll(wide, 128 - 2 * NV, 1))
        arrived(FA.at[s], f_at[c])

    stored = []

    def store(src, dst, i):
        stored.append(load(src, dst, i))

    def finish(s, i):
        hi, lw = split(LM[s])
        left = jnp.concatenate([hi, lw], 0)
        left = jnp.concatenate([left, jnp.concatenate([hi, jnp.zeros((NV, NB), BF)], 0)], 1)

        def body(x):
            z = [jnp.concatenate([FA[s, x, r], RA[s, x, r], RA[s + 2, x, r]], 0) for r in range(Y)]
            zh, zl = split(jnp.concatenate(z, 1))
            o = lax.dot_general(left, jnp.concatenate([zh, zl], 0), NN, preferred_element_type=F32)
            o = o[:NV] + o[NV:]
            for r in range(Y):
                out[s, pl.ds(x * Y + r, NV, stride=J), :] = o[:, r * NZ:(r + 1) * NZ]

        loop(X, 2, body)
        store(out.at[s], out_h.at[s], i)

    def finish_own(c):
        finish(p * S + c, c)

    def finish_rest(c):
        take(c)
        finish(q * S + c, S + c)

    end = S - 1
    for c in range(S):
        got_y(c)
        send_rest_z(c)
        send_x(c, xp_at[c], lq)
        if c == 0:
            send_own_z(end)
            early_corners(0)
        if c == 1:
            early_corners(1) if c < end else None
            early(0)
            mark = len(pending)
    for c in range(2, end):
        early_corners(c)
    late_corners(0)
    for c in range(1, end):
        early(c)
    gram_rest(0)
    late(0)
    early_corners(end)
    flush(mark // 2)
    for c in range(1, end):
        gram_rest(c)
    early(end)
    for c in range(1, end):
        late_corners(c)
    gram_rest(end)
    for c in range(1, end):
        late(c)
    sum_start(0)
    flush(mark - mark // 2)
    late_corners(end)
    sum_more(0)
    late(end)
    sum_start(1)
    sum_more(1)
    factor(0)
    for c in range(end):
        finish_own(c)
    factor(1)
    for c in range(end):
        finish_rest(c)
    finish_own(end)
    flush(len(pending) - 1)
    take(S - 1)
    store(cor, cor_h, 2 * S)
    finish(q * S + S - 1, 2 * S - 1)
    for copy in stored:
        copy.wait()
    flush(len(pending))


def on_device(disorder, slice_bounds, start, ritz):
    nc, nx, ny = (lax.axis_size(a) for a in ("cuts", "lx", "ly"))
    count, NV, X, Y, NZ = start.shape
    NR = ritz.shape[1]
    J = X * Y
    S, R, K = count // 2, 2 * Y, ny // 2
    V = pltpu.VMEM
    D = pltpu.SemaphoreType.DMA
    dims = (nc, nx, ny, count, NV, NR, X, Y, NZ)
    hbm = pl.BlockSpec(memory_space=pl.ANY)
    sems = sem_counts(nx, K, S)
    block, corr = pl.pallas_call(
        functools.partial(kernel, dims),
        out_shape=(jax.ShapeDtypeStruct((count, NV * J, NZ), F32),
                   jax.ShapeDtypeStruct((count, 2 * NR, NV), F32)),
        in_specs=[hbm] * 4,
        out_specs=(hbm, hbm),
        scratch_shapes=[
            V((count, NV * J, NZ), F32),
            V((count, 2 * NR, NV), F32),
            pltpu.SMEM((2, count), F32),
            V((J, NZ), jnp.int32),
            V((count, NV * J, NZ), F32),
            V((count, NR * J, NZ), F32),
            D((2 * S + 3,)),
            V((S, X + 2 * H, R + 2 * H, NV, NZ), F32),
            V((S, X, Y, NV, NZ), F32),
            V((X + 2 * H, R + 2 * H, 1, NZ), F32),
            V((S, X + 2 * H, R + 2 * H, NV, NZ), F32),
            V((count, X, Y, NV, NZ), F32),
            V((S, X, Y, NV, NZ), F32),
            V((count + 2, X, Y, NR, NZ), F32),
            V((S + 2, X, Y, NR, NZ), F32),
            V((S, 2 * (NV + 2 * NR), NV + 2 * NR), F32),
            V((S, 2, 8, 128), F32),
            V((nx, S, 2, 8, 128), F32),
            V((S, 2, 8, 128), F32),
            V((nx * K if direct_sum(nx, K) else K, S, 2, 8, 128), F32),
            V((count, NV, NV + 2 * NR), F32),
            V((S, NV, 128), F32),
            V((S, NV, 128), F32),
            D((sems,)), D((sems,)),
        ],
        compiler_params=pltpu.CompilerParams(collective_id=0, has_side_effects=True, vmem_limit_bytes=48 << 20),
    )(*[pltpu.with_memory_space_constraint(a, pltpu.HBM) for a in (
        disorder.reshape(J, NZ), slice_bounds.T, start.reshape(count, NV * J, NZ), ritz.reshape(count, NR * J, NZ))])
    return (block.reshape(start.shape), corr)


def solution(mesh):
    in_specs = (
        P("lx", "ly", None),
        P("cuts", None),
        P("cuts", None, "lx", "ly", None),
        P("cuts", None, "lx", "ly", None),
    )
    out_specs = (P("cuts", None, "lx", "ly", None), P("cuts", None, None))
    return jax.shard_map(
        on_device, mesh=mesh, in_specs=in_specs, out_specs=out_specs, check_vma=False
    )
```

```python
import functools

import jax
import jax.numpy as jnp
from jax import lax
from jax.experimental import pallas as pl
from jax.experimental.pallas import tpu as pltpu
from jax.sharding import PartitionSpec as P

LEVELS = 256
MESH = pl.DeviceIdType.MESH
HP = lax.Precision.HIGHEST
H = 2
BF = jnp.bfloat16
F32 = jnp.float32
NT = (((1,), (1,)), ((), ()))
NN = (((1,), (0,)), ((), ()))
TN = (((0,), (0,)), ((), ()))


def direct_sum(nx, K):
    return nx * K <= 16


def sem_counts(nx, K, S):
    more = 0 if direct_sum(nx, K) else 2
    return 12 + 3 * S + more, 9 + 11 * S + more


def split(z):
    hi = z.astype(BF)
    return hi, (z - hi.astype(F32)).astype(BF)


def loop(n, unroll, body):
    def step(i, carry):
        for k in range(unroll):
            body(i * unroll + k)
        return carry

    if n % unroll:
        unroll = 1
    lax.fori_loop(0, n // unroll, step, 0)


def kernel(dims, dis_h, bnd_h, start_h, ritz_h, out_h, cor_h, out, cor, bnd, dis, start, ritz, ls, E, T, O, U, FA, FT,
           RA, RQ, GS, PK, RX, SM, RZ, LM, LP, LR, ss, rs):
    nc, nx, ny, count, NV, NR, X, Y, NZ = dims
    S = count // 2
    R = 2 * Y
    J = X * Y
    K = ny // 2
    total = float(J * NZ * nx * ny)
    NW = 2 * NR
    NB = NV + NW
    cut, mx, my = lax.axis_index("cuts"), lax.axis_index("lx"), lax.axis_index("ly")
    p = lax.rem(my, 2)
    q = 1 - p
    kz = my // 2
    yp = (cut, mx, kz * 2 + q)
    zup = (cut, mx, lax.rem(kz + 1, K) * 2 + p)
    zdown = (cut, mx, lax.rem(kz + K - 1, K) * 2 + p)
    xup = (cut, lax.rem(mx + 1, nx), my)
    xdown = (cut, lax.rem(mx + nx - 1, nx), my)
    cup = (lax.rem(cut + 1, nc), mx, my)
    cdown = (lax.rem(cut + nc - 1, nc), mx, my)

    def load(src, dst, i):
        copy = pltpu.make_async_copy(src, dst, ls.at[i])
        copy.start()
        return copy

    barrier = pltpu.get_barrier_semaphore()

    def greet(dev):
        pl.semaphore_signal(barrier, inc=1, device_id=dev, device_id_type=MESH)

    greet(yp)
    if direct_sum(nx, K):
        for o in range(1, nx * K):
            t = lax.rem(mx * K + kz + o, nx * K)
            greet((cut, t // K, lax.rem(t, K) * 2 + p))
        greeted = nx * K + 2
    else:
        for o in range(1, nx):
            greet((cut, lax.rem(mx + o, nx), my))
        for o in range(1, K):
            greet((cut, mx, lax.rem(kz + o, K) * 2 + p))
        greeted = nx + K + 1
    greet(cup)
    greet(cdown)

    level_load = load(dis_h, dis, 2 * S)
    away, kept = [], []
    for c in range(S):
        away.append(load(start_h.at[q * S + c], start.at[c], c))
        kept.append(load(start_h.at[p * S + c], start.at[S + c], S + c))
    bound_load = load(bnd_h, bnd, 2 * S + 2)
    ritz_load = load(ritz_h, ritz, 2 * S + 1)

    lo = H + Y * p
    lq = H + Y * q
    xi = pl.ds(H, X)
    mid = pl.ds(H + 1, X - 2)
    def stage_away(c):
        away[c].wait()
        for x in range(X):
            for r in range(Y):
                T[c, x, r] = start[c, pl.ds(x * Y + r, NV, stride=J), :]

    def stage_kept(c):
        kept[c].wait()
        for x in range(X):
            for r in range(Y):
                E[c, H + x, lo + r] = start[S + c, pl.ds(x * Y + r, NV, stride=J), :]

    used = [0, 0]

    def take_slots(kind, n=1):
        i = used[kind]
        used[kind] += n
        return i

    def send(src, dst, i, j, dev):
        pltpu.make_async_remote_copy(
            src_ref=src, dst_ref=dst, send_sem=ss.at[i], recv_sem=rs.at[j], device_id=dev, device_id_type=MESH).start()

    def left(src, i):
        pltpu.make_async_remote_copy(
            src_ref=src, dst_ref=src, send_sem=ss.at[i], recv_sem=ss.at[i],
            device_id=yp, device_id_type=MESH).wait_send()

    def arrived(dst, j):
        pltpu.make_async_remote_copy(
            src_ref=dst, dst_ref=dst, send_sem=rs.at[j], recv_sem=rs.at[j],
            device_id=yp, device_id_type=MESH).wait_recv()

    def rows(at):
        return pl.ds(at, Y)

    so, sy, sf, sl, sr, sc = (take_slots(0, n) for n in (5, 1, 1, 1, 1, 1))
    sz, sx, sk, sa = (take_slots(0, n) for n in (S, S, S, 2))
    ro, ry, rf, rl, rx, rc, rr, ra_ = (take_slots(1, n) for n in (5, S, S, S, S, 2, S, 2))
    rz, rk = take_slots(1, 4 * S), take_slots(1, 2 * S)
    groups = [list(range(S - 1)), [S - 1]]
    direct = direct_sum(nx, K)
    span = nx * K if direct else K
    me = mx * K + kz if direct else kz
    sb, rb = (0, 0) if direct else (take_slots(0, 2), take_slots(1, 2))

    def send_y(c):
        send(T.at[c], E.at[c, xi, rows(lo)], sy, ry + c, yp)

    def z_dev(half):
        return (cut, mx, jnp.where(half == 1, zup[2], zdown[2]))

    def send_own_z(c):
        dst = jnp.where(p == 1, 0, H + R)
        send(E.at[c, xi, rows(lo)], E.at[c, xi, rows(dst)], sz + c, rz + 4 * c, z_dev(p))

    def send_rest_z(c):
        src = [jnp.where(q == 1, H + R - 1 - k, H + k) for k in range(2)]
        dst = [jnp.where(q == 1, H - 1 - k, H + R + k) for k in range(2)]
        for x in (H, H + X - 1):
            send(E.at[c, x, src[0]], E.at[c, x, dst[0]], sz + c, rz + 4 * c + 1, z_dev(q))
        send(E.at[c, mid, src[0]], E.at[c, mid, dst[0]], sz + c, rz + 4 * c + 2, z_dev(q))
        send(E.at[c, xi, src[1]], E.at[c, xi, dst[1]], sz + c, rz + 4 * c + 3, z_dev(q))

    def send_x(c, at):
        send(E.at[c, pl.ds(X, H), rows(at)], E.at[c, pl.ds(0, H), rows(at)], sx + c, rx + c, xup)
        send(E.at[c, pl.ds(H, H), rows(at)], E.at[c, pl.ds(H + X, H), rows(at)], sx + c, rx + c, xdown)

    def got_x(c):
        arrived(E.at[c, pl.ds(0, 4 * H), rows(0)], rx + c)

    def send_o(half):
        side = 1 - half
        src = jnp.where(half == 1, H + R - 1, H)
        dst = jnp.where(half == 1, 1, H + R)
        send(O.at[xi, src], O.at[xi, dst], so + 1 + side, ro + 1 + side, z_dev(half))

    own = pl.ds(H, R)

    def relay_o():
        arrived(O.at[xi, rows(lq)], ro)
        send_o(q)
        send(O.at[H + X - 1, own], O.at[H - 1, own], so + 3, ro + 3, xup)
        send(O.at[H, own], O.at[H + X, own], so + 4, ro + 4, xdown)

    level_load.wait()
    for x in range(X):
        for r in range(Y):
            row = dis[pl.ds(x * Y + r, 1), :].astype(F32)
            O[H + x, lo + r] = 16.5 * (row / F32(LEVELS - 1) - 0.5)
    stage_away(0)
    stage_kept(0)
    pl.semaphore_wait(barrier, greeted)
    send(O.at[xi, rows(lo)], O.at[xi, rows(lo)], so, ro, yp)
    send_y(0)
    send_o(p)
    send_own_z(0)
    send_x(0, lo)
    for c in range(1, S):
        stage_away(c)
        send_y(c)
        stage_kept(c)
        if c == 1:
            relay_o()
        if c < S - 1:
            send_own_z(c)
        send_x(c, lo)
    bound_load.wait()
    ritz_load.wait()
    for s in range(count):
        for x in range(X):
            for r in range(Y):
                RA[s + 1, x, r] = ritz[s, pl.ds(x * Y + r, NR, stride=J), :]
    send(RA.at[count], RA.at[0], sc, rc, cup)
    send(RA.at[1], RA.at[count + 1], sc, rc + 1, cdown)

    arrived(RA.at[0], rc)
    arrived(RA.at[count + 1], rc + 1)

    @pl.when(cut == 0)
    def _():
        RA[0] = jnp.zeros((X, Y, NR, NZ), F32)

    @pl.when(cut == nc - 1)
    def _():
        RA[count + 1] = jnp.zeros((X, Y, NR, NZ), F32)

    fresh = [[j for j in (c, c + 2) if j >= 2 or c < 2] for c in range(S)]
    fresh = [[j for j in js if j not in sum(fresh[:c], [])] for c, js in enumerate(fresh)]
    for c in range(S):
        for j in fresh[c]:
            send(RA.at[q * S + j], RQ.at[j], sr, rr + c, yp)

    def got_y(c):
        arrived(E.at[c, xi, rows(lq)], ry + c)

    last = R + 2 * H - 1
    ra = [a + p * (last - 2 * a) for a in range(last + 1)]
    near, far = H - 1, H + R

    def point(src, x, a, centre):
        v = src(x, a)
        beside = src(x + 1, a) + src(x - 1, a)
        beside = beside + src(x, a + 1) + src(x, a - 1)
        beside = beside + pltpu.roll(v, 1, 1) + pltpu.roll(v, NZ - 1, 1)
        level = jnp.broadcast_to(O[x, ra[a]] - centre, (NV, NZ))
        return level * v - beside

    def refs(c):
        s = p * S + c
        centre = (bnd[0, s] + bnd[1, s]) / 2.0

        def from_e(x, a):
            return E[c, x, ra[a]]

        def from_u(x, a):
            return U[c, x, ra[a]]

        def one(x, a):
            U[c, x, ra[a]] = point(from_e, x, a, centre)

        def two(x, a):
            return point(from_u, x, a, centre) * (2.0 / 256.0) - from_e(x, a)

        return one, two

    def corners(c, a, k):
        send(E.at[c, H + X - 1, ra[a]], E.at[c, H - 1, ra[a]], sk + c, rk + k, xup)
        send(E.at[c, H, ra[a]], E.at[c, H + X, ra[a]], sk + c, rk + k, xdown)

    def got_corners(c, k):
        arrived(E.at[c, pl.ds(0, 2), 0], rk + k)

    def early_corners(c):
        arrived(E.at[c, xi, rows(jnp.where(p == 1, 0, H + R))], rz + 4 * c)
        corners(c, far, 2 * c)

    def late_corners(c):
        arrived(E.at[c, pl.ds(0, 2), 0], rz + 4 * c + 1)
        corners(c, near, 2 * c + 1)

    def got_o():
        arrived(O.at[xi, H - 1], ro + 1)
        arrived(O.at[xi, H + R], ro + 2)
        arrived(O.at[H - 1, own], ro + 3)
        arrived(O.at[H + X, own], ro + 4)

    def early(c):
        one, two = refs(c)
        got_x(c)
        if c == 0:
            got_o()

        def inner(i):
            for a in range(H + 1, far + 1):
                one(H + 1 + i, a)

        loop(X - 2, 6, inner)
        for x in (H, H + X - 1):
            for a in range(H + 1, far):
                one(x, a)
        for x in (H - 1, H + X):
            for a in range(H + 1, far - 1):
                one(x, a)
        got_corners(c, 2 * c)
        for x in (H, H + X - 1):
            one(x, far)
        for x in (H - 1, H + X):
            one(x, far - 1)

        def outer(i):
            for a in range(H + Y, far):
                FT[c, i, ra[a] - lq] = two(H + i, a)

        loop(X, 8, outer)
        send(FT.at[c], FA.at[p * S + c], sf, rf + c, yp)

    def row_gram(c, a, two, acc):
        s, r = p * S + c, ra[a] - lo
        for i in range(0, X, 2):
            z = []
            for x in (i, i + 1):
                f = two(H + x, a)
                FA[s, x, r] = f
                z.append(jnp.concatenate([f, RA[s, x, r], RA[s + 2, x, r]], 0))
            acc = acc + square(z)
        return acc

    def late_near(c):
        one, two = refs(c)
        arrived(E.at[c, mid, ra[near]], rz + 4 * c + 2)
        for x in range(H, H + X):
            one(x, H)
        for a in range(H + 1, H + Y):
            GS[c] = row_gram(c, a, two, GS[c])

    def late_far(c):
        one, two = refs(c)
        arrived(E.at[c, xi, ra[near - 1]], rz + 4 * c + 3)
        for x in range(H + 1, H + X - 1):
            one(x, near)
        got_corners(c, 2 * c + 1)
        for x in (H, H + X - 1):
            one(x, near)
        for x in (H - 1, H + X):
            one(x, H)
        gram_pack(c, row_gram(c, H, two, GS[c]))

    def square(z):
        hi, lw = split(jnp.concatenate(z, 1))
        return lax.dot_general(jnp.concatenate([hi, lw], 0), hi, NT, preferred_element_type=F32)

    def product(f, w0, w1):
        def body(i, acc):
            for k in range(8):
                x = 8 * i + k
                z = [jnp.concatenate([f(x, r), w0(x, r), w1(x, r)], 0) for r in range(Y)]
                acc = acc + square(z)
            return acc

        return lax.fori_loop(0, X // 8, body, jnp.zeros((2 * NB, NB), F32))

    def gram_rest(c):
        arrived(RQ.at[pl.ds(0, len(fresh[c]))], rr + c)
        GS[c] = product(lambda x, r: FT[c, x, r], lambda x, r: RQ[c, x, r], lambda x, r: RQ[c + 2, x, r])

    def gram_pack(c, g):
        g = jnp.concatenate([g, jnp.zeros((2 * NB, 128 - NB), F32)], 1)
        cross = jnp.concatenate([g[NB:], jnp.zeros((128 - NB, 128), F32)], 0)
        g = g[:NB] + (cross + cross.T)[:NB]
        lane = lax.broadcasted_iota(jnp.int32, (8, 128), 1)
        t0 = jnp.zeros((8, 128), F32)
        t1 = jnp.zeros((8, 128), F32)
        for b_ in range(NV // 8):
            block = g[b_ * 8:b_ * 8 + 8]
            ff = jnp.where(lane < NV, block, 0.0)
            fw = jnp.where(lane >= NV, block, 0.0)
            t0 = t0 + (pltpu.roll(ff, b_ * NV, 1) if b_ else ff)
            t1 = t1 + pltpu.roll(fw, (128 - NV + b_ * NW) % 128, 1)
        for b_ in range(NW // 8):
            ww = jnp.where(lane >= NV, g[NV + b_ * 8:NV + b_ * 8 + 8], 0.0)
            t1 = t1 + pltpu.roll(ww, (128 - NV + (NV // 8 + b_) * NW) % 128, 1)
        PK[c, 0] = t0
        PK[c, 1] = t1

    def spread(k, src):
        cs = groups[k]
        part = pl.ds(cs[0], len(cs))
        for o in range(1, span):
            t = lax.rem(me + o, span)
            x, z = (t // K, lax.rem(t, K)) if direct else (mx, t)
            send(src.at[part], RZ.at[me, part], sa + k, ra_ + k, (cut, x, z * 2 + p))

    def sum_start(k):
        cs = groups[k]
        part = pl.ds(cs[0], len(cs))
        for c in cs:
            if direct:
                RZ[me, c] = PK[c]
            else:
                RX[mx, c] = PK[c]
        if direct:
            spread(k, PK)
            return
        for o in range(1, nx):
            send(PK.at[part], RX.at[mx, part], sb + k, rb + k, (cut, lax.rem(mx + o, nx), my))

    def sum_more(k):
        if direct:
            return
        cs = groups[k]
        part = pl.ds(cs[0], len(cs))
        arrived(RX.at[pl.ds(0, nx - 1), part], rb + k)
        for c in cs:
            acc = RX[0, c]
            for t in range(1, nx):
                acc = acc + RX[t, c]
            SM[c] = acc
            RZ[kz, c] = acc
        spread(k, SM)

    e16r = lax.broadcasted_iota(jnp.int32, (NW, NW), 0)
    e16l = lax.broadcasted_iota(jnp.int32, (NW, NW), 1)
    l32 = lax.broadcasted_iota(jnp.int32, (NV, 128), 1)
    r32 = lax.broadcasted_iota(jnp.int32, (NV, 128), 0)
    eye = jnp.where(l32 == r32 + NV, 1.0, 0.0)

    line = lax.broadcasted_iota(jnp.int32, (NV, 1), 0)
    odd = r32 % 2

    def strip(t, at):
        return pltpu.roll(t, 128 - at, 1) if at else t

    def cleaned(c):
        acc = RZ[0, c]
        for t in range(1, span):
            acc = acc + RZ[t, c]
        acc = acc * (1.0 / total)
        t0, t1 = acc[0], acc[1]
        ff = jnp.concatenate([strip(t0, b * NV) for b in range(NV // 8)], 0)
        fw = jnp.concatenate([strip(t1, b * NW) for b in range(NV // 8)], 0)
        ww = jnp.concatenate([strip(t1, NV // 8 * NW + b * NW) for b in range(NW // 8)], 0)
        b = jnp.where(e16r == e16l, 2.0, 0.0) - ww[:, :NW]
        fn = fw[:, :NW]
        fb = lax.dot_general(fn, b, NN, precision=HP, preferred_element_type=F32)
        sub = lax.dot_general(fb, fn, NT, precision=HP, preferred_element_type=F32)
        sub = jnp.concatenate([sub, jnp.zeros((NV, 128 - NV), F32)], 1)
        wide = jnp.where(l32 < NW, fw, 0.0)
        return jnp.where(l32 < NV, ff - sub, eye) - pltpu.roll(wide, 2 * NV, 1), wide

    def eliminate(M, j):
        r0, r1 = M[j:j + 1], M[j + 1:j + 2]
        c0 = jnp.broadcast_to(M[:, j:j + 1], (NV, 128))
        c1 = jnp.broadcast_to(M[:, j + 1:j + 2], (NV, 128))
        p00, p01, p11 = c0[j:j + 1], c1[j:j + 1], c1[j + 1:j + 2]
        inv = 1.0 / (p00 * p11 - p01 * p01)
        g0 = (p11 * r0 - p01 * r1) * inv
        g1 = (p00 * r1 - p01 * r0) * inv
        return jnp.where(line > j + 1, M - c0 * g0 - c1 * g1, M)

    def scaled(M):
        diag = jnp.sum(jnp.where(l32 == r32, M, 0.0), axis=1, keepdims=True)
        side = jnp.sum(jnp.where(l32 == r32 - odd, M, 0.0), axis=1, keepdims=True)
        ratio = side / pltpu.roll(jnp.broadcast_to(diag, (NV, 128)), 1, 0)
        M = jnp.where(odd == 1, M - ratio * pltpu.roll(M, 1, 0), M)
        diag = jnp.sum(jnp.where(l32 == r32, M, 0.0), axis=1, keepdims=True)
        return pltpu.roll(M * (1.0 / jnp.sqrt(diag)), 128 - NV, 1)

    def factor(k):
        cs = groups[k]
        part = pl.ds(cs[0], len(cs))
        arrived(RZ.at[pl.ds(0, span - 1), part], ra_ + k)
        both = [cleaned(c) for c in cs]
        mats = [m for m, _ in both]
        for j in range(0, NV, 2):
            mats = [eliminate(m, j) for m in mats]
        mats = [scaled(m) for m in mats]
        for i, c in enumerate(cs):
            LP[c] = jnp.where(l32 < NB, mats[i], pltpu.roll(both[i][1], 2 * NV, 1))
            send(LP.at[c], LR.at[c], sl, rl + c, yp)
        for i, c in enumerate(cs):
            LM[p * S + c] = mats[i][:, :NB]
            keep_corr(p * S + c, both[i][1])

    def keep_corr(s, wide):
        cor[s] = jnp.concatenate([wide, jnp.zeros((128 - NV, 128), F32)], 0).T[:NW, :NV]

    def take(c):
        s = q * S + c
        arrived(LR.at[c], rl + c)
        wide = LR[c]
        LM[s] = wide[:, :NB]
        keep_corr(s, pltpu.roll(wide, 128 - 2 * NV, 1))
        arrived(FA.at[s], rf + c)

    stored = []

    def store(src, dst, i):
        stored.append(load(src, dst, i))

    def finish(s, i):
        hi, lw = split(LM[s])
        left = jnp.concatenate([hi, lw], 0)
        left = jnp.concatenate([left, jnp.concatenate([hi, jnp.zeros((NV, NB), BF)], 0)], 1)

        def body(x):
            z = [jnp.concatenate([FA[s, x, r], RA[s, x, r], RA[s + 2, x, r]], 0) for r in range(Y)]
            zh, zl = split(jnp.concatenate(z, 1))
            o = lax.dot_general(left, jnp.concatenate([zh, zl], 0), NN, preferred_element_type=F32)
            o = o[:NV] + o[NV:]
            for r in range(Y):
                out[s, pl.ds(x * Y + r, NV, stride=J), :] = o[:, r * NZ:(r + 1) * NZ]

        loop(X, 8, body)
        store(out.at[s], out_h.at[s], i)

    def finish_own(c):
        finish(p * S + c, c)

    def finish_rest(c):
        take(c)
        finish(q * S + c, S + c)

    def settle():
        left(O.at[xi, rows(lo)], so)
        for k in range(2):
            left(O.at[xi, H], so + 1 + k)
            left(O.at[H, own], so + 3 + k)
        left(T, sy)
        left(RQ, sr)
        left(RA.at[pl.ds(0, 2)], sc)
        for c in range(S):
            left(E.at[c, xi, pl.ds(0, Y + 2)], sz + c)
            left(E.at[c, pl.ds(0, 4 * H), rows(0)], sx + c)
            left(E.at[c, pl.ds(0, 4), 0], sk + c)

    end = S - 1
    for c in range(S):
        got_y(c)
        send_rest_z(c)
        send_x(c, lq)
        if c == 0:
            send_own_z(end)
            early_corners(0)
        if c == 1:
            early_corners(1) if c < end else None
            early(0)
    for c in range(2, end):
        early_corners(c)
    late_corners(0)
    for c in range(1, end):
        early(c)
    gram_rest(0)
    late_near(0)
    early_corners(end)
    late_far(0)
    for c in range(1, end):
        gram_rest(c)
    early(end)
    for c in range(1, end):
        late_corners(c)
    gram_rest(end)
    for c in range(1, end):
        late_near(c)
        late_far(c)
    sum_start(0)
    late_corners(end)
    sum_more(0)
    late_near(end)
    late_far(end)
    sum_start(1)
    sum_more(1)
    settle()
    factor(0)
    for c in range(end):
        finish_own(c)
    factor(1)
    for c in range(end):
        finish_rest(c)
    finish_own(end)
    for k in range(2):
        part = pl.ds(groups[k][0], len(groups[k]))
        if not direct:
            left(RX.at[pl.ds(0, nx - 1), part], sb + k)
        left(RZ.at[pl.ds(0, span - 1), part], sa + k)
    left(FT, sf)
    take(S - 1)
    store(cor, cor_h, 2 * S)
    finish(q * S + S - 1, 2 * S - 1)
    for copy in stored:
        copy.wait()
    left(LP, sl)


def place(block, corr, block_out, corr_out, sem):
    copies = [pltpu.make_async_copy(block.at[s], block_out.at[s], sem.at[s]) for s in range(block.shape[0])]
    copies.append(pltpu.make_async_copy(corr, corr_out, sem.at[block.shape[0]]))
    for copy in copies:
        copy.start()
    for copy in copies:
        copy.wait()


def on_device(disorder, slice_bounds, start, ritz):
    nc, nx, ny = (lax.axis_size(a) for a in ("cuts", "lx", "ly"))
    count, NV, X, Y, NZ = start.shape
    NR = ritz.shape[1]
    J = X * Y
    S, R, K = count // 2, 2 * Y, ny // 2
    V = pltpu.VMEM
    D = pltpu.SemaphoreType.DMA
    dims = (nc, nx, ny, count, NV, NR, X, Y, NZ)
    hbm = pl.BlockSpec(memory_space=pl.ANY)
    sends, receives = sem_counts(nx, K, S)
    block, corr = pl.pallas_call(
        functools.partial(kernel, dims),
        out_shape=(jax.ShapeDtypeStruct((count, NV * J, NZ), F32),
                   jax.ShapeDtypeStruct((count, 2 * NR, NV), F32)),
        in_specs=[hbm] * 4,
        out_specs=(hbm, hbm),
        scratch_shapes=[
            V((count, NV * J, NZ), F32),
            V((count, 2 * NR, NV), F32),
            pltpu.SMEM((2, count), F32),
            V((J, NZ), jnp.int32),
            V((count, NV * J, NZ), F32),
            V((count, NR * J, NZ), F32),
            D((2 * S + 3,)),
            V((S, X + 2 * H, R + 2 * H, NV, NZ), F32),
            V((S, X, Y, NV, NZ), F32),
            V((X + 2 * H, R + 2 * H, 1, NZ), F32),
            V((S, X + 2 * H, R + 2 * H, NV, NZ), F32),
            V((count, X, Y, NV, NZ), F32),
            V((S, X, Y, NV, NZ), F32),
            V((count + 2, X, Y, NR, NZ), F32),
            V((S + 2, X, Y, NR, NZ), F32),
            V((S, 2 * (NV + 2 * NR), NV + 2 * NR), F32),
            V((S, 2, 8, 128), F32),
            V((nx, S, 2, 8, 128), F32),
            V((S, 2, 8, 128), F32),
            V((nx * K if direct_sum(nx, K) else K, S, 2, 8, 128), F32),
            V((count, NV, NV + 2 * NR), F32),
            V((S, NV, 128), F32),
            V((S, NV, 128), F32),
            D((sends,)), D((receives,)),
        ],
        compiler_params=pltpu.CompilerParams(collective_id=0, has_side_effects=True, vmem_limit_bytes=48 << 20),
    )(*[pltpu.with_memory_space_constraint(a, pltpu.HBM) for a in (
        disorder.reshape(J, NZ), slice_bounds.T, start.reshape(count, NV * J, NZ), ritz.reshape(count, NR * J, NZ))])
    block, corr = pl.pallas_call(
        place,
        out_shape=(jax.ShapeDtypeStruct(block.shape, F32), jax.ShapeDtypeStruct(corr.shape, F32)),
        in_specs=[hbm] * 2,
        out_specs=(hbm, hbm),
        scratch_shapes=[D((count + 1,))],
        compiler_params=pltpu.CompilerParams(vmem_limit_bytes=1 << 20),
    )(block, corr)
    return (block.reshape(start.shape), corr)


def solution(mesh):
    in_specs = (
        P("lx", "ly", None),
        P("cuts", None),
        P("cuts", None, "lx", "ly", None),
        P("cuts", None, "lx", "ly", None),
    )
    out_specs = (P("cuts", None, "lx", "ly", None), P("cuts", None, None))
    return jax.shard_map(
        on_device, mesh=mesh, in_specs=in_specs, out_specs=out_specs, check_vma=False
    )
```

```python
import functools

import jax
import jax.numpy as jnp
from jax import lax
from jax.experimental import pallas as pl
from jax.experimental.pallas import tpu as pltpu
from jax.sharding import PartitionSpec as P

LEVELS = 256
MESH = pl.DeviceIdType.MESH
HP = lax.Precision.HIGHEST
H = 2
BF = jnp.bfloat16
F32 = jnp.float32
NT = (((1,), (1,)), ((), ()))
NN = (((1,), (0,)), ((), ()))
TN = (((0,), (0,)), ((), ()))


def direct_sum(nx, K):
    return nx * K <= 16


def sem_counts(nx, K, S):
    more = 0 if direct_sum(nx, K) else 2
    return 13 + 3 * S + more, 10 + 11 * S + more


def split(z):
    hi = z.astype(BF)
    return hi, (z - hi.astype(F32)).astype(BF)


def loop(n, unroll, body):
    def step(i, carry):
        for k in range(unroll):
            body(i * unroll + k)
        return carry

    if n % unroll:
        unroll = 1
    lax.fori_loop(0, n // unroll, step, 0)


def kernel(dims, dis_h, bnd_h, start_h, ritz_h, out_h, cor_h, out, cor, bnd, dis, start, ritz, ls, E, T, O, U, FA, FT,
           RA, RQ, GS, GT, PK, RX, SM, RZ, LM, LP, LR, LC, LD, ss, rs):
    nc, nx, ny, count, NV, NR, X, Y, NZ = dims
    S = count // 2
    R = 2 * Y
    J = X * Y
    K = ny // 2
    total = float(J * NZ * nx * ny)
    NW = 2 * NR
    NB = NV + NW
    cut, mx, my = lax.axis_index("cuts"), lax.axis_index("lx"), lax.axis_index("ly")
    p = lax.rem(my, 2)
    q = 1 - p
    kz = my // 2
    yp = (cut, mx, kz * 2 + q)
    zup = (cut, mx, lax.rem(kz + 1, K) * 2 + p)
    zdown = (cut, mx, lax.rem(kz + K - 1, K) * 2 + p)
    xup = (cut, lax.rem(mx + 1, nx), my)
    xdown = (cut, lax.rem(mx + nx - 1, nx), my)
    cup = (lax.rem(cut + 1, nc), mx, my)
    cdown = (lax.rem(cut + nc - 1, nc), mx, my)

    def load(src, dst, i):
        copy = pltpu.make_async_copy(src, dst, ls.at[i])
        copy.start()
        return copy

    barrier = pltpu.get_barrier_semaphore()

    def greet(dev):
        pl.semaphore_signal(barrier, inc=1, device_id=dev, device_id_type=MESH)

    greet(yp)
    if direct_sum(nx, K):
        for o in range(1, nx * K):
            t = lax.rem(mx * K + kz + o, nx * K)
            greet((cut, t // K, lax.rem(t, K) * 2 + p))
        greeted = nx * K + 2
    else:
        for o in range(1, nx):
            greet((cut, lax.rem(mx + o, nx), my))
        for o in range(1, K):
            greet((cut, mx, lax.rem(kz + o, K) * 2 + p))
        greeted = nx + K + 1
    greet(cup)
    greet(cdown)

    away, kept = [], []
    for c in range(S):
        kept.append(load(start_h.at[p * S + c], start.at[S + c], S + c))
        if c == 0:
            level_load = load(dis_h, dis, 2 * S)
        away.append(load(start_h.at[q * S + c], start.at[c], c))
    bound_load = load(bnd_h, bnd, 2 * S + 2)
    ritz_load = load(ritz_h, ritz, 2 * S + 1)

    lo = H + Y * p
    lq = H + Y * q
    xi = pl.ds(H, X)
    mid = pl.ds(H + 1, X - 2)
    def stage_away(c):
        away[c].wait()
        for x in range(X):
            for r in range(Y):
                T[c, x, r] = start[c, pl.ds(x * Y + r, NV, stride=J), :]

    def stage_kept(c):
        kept[c].wait()
        for x in range(X):
            for r in range(Y):
                E[c, H + x, lo + r] = start[S + c, pl.ds(x * Y + r, NV, stride=J), :]

    used = [0, 0]

    def take_slots(kind, n=1):
        i = used[kind]
        used[kind] += n
        return i

    def send(src, dst, i, j, dev):
        pltpu.make_async_remote_copy(
            src_ref=src, dst_ref=dst, send_sem=ss.at[i], recv_sem=rs.at[j], device_id=dev, device_id_type=MESH).start()

    def left(src, i):
        pltpu.make_async_remote_copy(
            src_ref=src, dst_ref=src, send_sem=ss.at[i], recv_sem=ss.at[i],
            device_id=yp, device_id_type=MESH).wait_send()

    def arrived(dst, j):
        pltpu.make_async_remote_copy(
            src_ref=dst, dst_ref=dst, send_sem=rs.at[j], recv_sem=rs.at[j],
            device_id=yp, device_id_type=MESH).wait_recv()

    def rows(at):
        return pl.ds(at, Y)

    so, sy, sf, sl, sr, sc, sd = (take_slots(0, n) for n in (5, 1, 1, 1, 1, 1, 1))
    sz, sx, sk, sa = (take_slots(0, n) for n in (S, S, S, 2))
    ro, ry, rf, rl, rx, rc, rr, ra_, rd = (take_slots(1, n) for n in (5, S, S, S, S, 2, S, 2, 1))
    rz, rk = take_slots(1, 4 * S), take_slots(1, 2 * S)
    groups = [list(range(S - 1)), [S - 1]]
    direct = direct_sum(nx, K)
    span = nx * K if direct else K
    me = mx * K + kz if direct else kz
    sb, rb = (0, 0) if direct else (take_slots(0, 2), take_slots(1, 2))

    def send_y(c):
        send(T.at[c], E.at[c, xi, rows(lo)], sy, ry + c, yp)

    def z_dev(half):
        return (cut, mx, jnp.where(half == 1, zup[2], zdown[2]))

    def send_own_z(c):
        dst = jnp.where(p == 1, 0, H + R)
        send(E.at[c, xi, rows(lo)], E.at[c, xi, rows(dst)], sz + c, rz + 4 * c, z_dev(p))

    def send_rest_z(c):
        src = [jnp.where(q == 1, H + R - 1 - k, H + k) for k in range(2)]
        dst = [jnp.where(q == 1, H - 1 - k, H + R + k) for k in range(2)]
        for x in (H, H + X - 1):
            send(E.at[c, x, src[0]], E.at[c, x, dst[0]], sz + c, rz + 4 * c + 1, z_dev(q))
        send(E.at[c, mid, src[0]], E.at[c, mid, dst[0]], sz + c, rz + 4 * c + 2, z_dev(q))
        send(E.at[c, xi, src[1]], E.at[c, xi, dst[1]], sz + c, rz + 4 * c + 3, z_dev(q))

    def send_x(c, at):
        send(E.at[c, pl.ds(X, H), rows(at)], E.at[c, pl.ds(0, H), rows(at)], sx + c, rx + c, xup)
        send(E.at[c, pl.ds(H, H), rows(at)], E.at[c, pl.ds(H + X, H), rows(at)], sx + c, rx + c, xdown)

    def got_x(c):
        arrived(E.at[c, pl.ds(0, 4 * H), rows(0)], rx + c)

    def send_o(half):
        side = 1 - half
        src = jnp.where(half == 1, H + R - 1, H)
        dst = jnp.where(half == 1, 1, H + R)
        send(O.at[xi, src], O.at[xi, dst], so + 1 + side, ro + 1 + side, z_dev(half))

    own = pl.ds(H, R)

    def relay_o():
        arrived(O.at[xi, rows(lq)], ro)
        send_o(q)
        send(O.at[H + X - 1, own], O.at[H - 1, own], so + 3, ro + 3, xup)
        send(O.at[H, own], O.at[H + X, own], so + 4, ro + 4, xdown)

    level_load.wait()
    for x in range(X):
        for r in range(Y):
            row = dis[pl.ds(x * Y + r, 1), :].astype(F32)
            O[H + x, lo + r] = 16.5 * (row / F32(LEVELS - 1) - 0.5)
    stage_kept(0)
    pl.semaphore_wait(barrier, greeted)
    send(O.at[xi, rows(lo)], O.at[xi, rows(lo)], so, ro, yp)
    send_o(p)
    send_own_z(0)
    stage_away(0)
    send_y(0)
    send_x(0, lo)
    for c in range(1, S):
        stage_away(c)
        send_y(c)
        stage_kept(c)
        if c == 1:
            relay_o()
        if c < S - 1:
            send_own_z(c)
        send_x(c, lo)
    bound_load.wait()
    ritz_load.wait()
    for s in range(count):
        for x in range(X):
            for r in range(Y):
                RA[s + 1, x, r] = ritz[s, pl.ds(x * Y + r, NR, stride=J), :]
    send(RA.at[count], RA.at[0], sc, rc, cup)
    send(RA.at[1], RA.at[count + 1], sc, rc + 1, cdown)

    arrived(RA.at[0], rc)
    arrived(RA.at[count + 1], rc + 1)

    @pl.when(cut == 0)
    def _():
        RA[0] = jnp.zeros((X, Y, NR, NZ), F32)

    @pl.when(cut == nc - 1)
    def _():
        RA[count + 1] = jnp.zeros((X, Y, NR, NZ), F32)

    fresh = [[j for j in (c, c + 2) if j >= 2 or c < 2] for c in range(S)]
    fresh = [[j for j in js if j not in sum(fresh[:c], [])] for c, js in enumerate(fresh)]
    for c in range(S):
        for j in fresh[c]:
            send(RA.at[q * S + j], RQ.at[j], sr, rr + c, yp)

    def got_y(c):
        arrived(E.at[c, xi, rows(lq)], ry + c)

    last = R + 2 * H - 1
    ra = [a + p * (last - 2 * a) for a in range(last + 1)]
    near, far = H - 1, H + R

    def point(src, x, a, centre):
        v = src(x, a)
        beside = src(x + 1, a) + src(x - 1, a)
        beside = beside + src(x, a + 1) + src(x, a - 1)
        beside = beside + pltpu.roll(v, 1, 1) + pltpu.roll(v, NZ - 1, 1)
        level = jnp.broadcast_to(O[x, ra[a]] - centre, (NV, NZ))
        return level * v - beside

    def refs(c):
        s = p * S + c
        centre = (bnd[0, s] + bnd[1, s]) / 2.0

        def from_e(x, a):
            return E[c, x, ra[a]]

        def from_u(x, a):
            return U[c, x, ra[a]]

        def one(x, a):
            U[c, x, ra[a]] = point(from_e, x, a, centre)

        def two(x, a):
            return point(from_u, x, a, centre) * (2.0 / 256.0) - from_e(x, a)

        return one, two

    def corners(c, a, k):
        send(E.at[c, H + X - 1, ra[a]], E.at[c, H - 1, ra[a]], sk + c, rk + k, xup)
        send(E.at[c, H, ra[a]], E.at[c, H + X, ra[a]], sk + c, rk + k, xdown)

    def got_corners(c, k):
        arrived(E.at[c, pl.ds(0, 2), 0], rk + k)

    def early_corners(c):
        arrived(E.at[c, xi, rows(jnp.where(p == 1, 0, H + R))], rz + 4 * c)
        corners(c, far, 2 * c)

    def late_corners(c):
        arrived(E.at[c, pl.ds(0, 2), 0], rz + 4 * c + 1)
        corners(c, near, 2 * c + 1)

    def got_o():
        arrived(O.at[xi, H - 1], ro + 1)
        arrived(O.at[xi, H + R], ro + 2)
        arrived(O.at[H - 1, own], ro + 3)
        arrived(O.at[H + X, own], ro + 4)

    def early(c):
        one, two = refs(c)
        got_x(c)
        if c == 0:
            got_o()

        def inner(i):
            for a in range(H + 1, far + 1):
                one(H + 1 + i, a)

        loop(X - 2, 6, inner)
        for x in (H, H + X - 1):
            for a in range(H + 1, far):
                one(x, a)
        for x in (H - 1, H + X):
            for a in range(H + 1, far - 1):
                one(x, a)
        got_corners(c, 2 * c)
        for x in (H, H + X - 1):
            one(x, far)
        for x in (H - 1, H + X):
            one(x, far - 1)

        def outer(i):
            for a in range(H + Y, far):
                FT[c, i, ra[a] - lq] = two(H + i, a)

        loop(X, 8, outer)
        send(FT.at[c], FA.at[p * S + c], sf, rf + c, yp)

    def row_gram(c, a, two, acc, product=None):
        s, r = p * S + c, ra[a] - lo
        for i in range(0, X, 2):
            z = []
            for x in (i, i + 1):
                f = two(H + x, a)
                FA[s, x, r] = f
                z.append(jnp.concatenate([f, RA[s, x, r], RA[s + 2, x, r]], 0))
            acc = acc + (product or square)(z)
        return acc

    def late_near(c):
        one, two = refs(c)
        arrived(E.at[c, mid, ra[near]], rz + 4 * c + 2)
        for x in range(H, H + X):
            one(x, H)
        g = GS[c]
        for a in range(H + 1, H + Y):
            g = row_gram(c, a, two, g)
        g = jnp.concatenate([g, jnp.zeros((2 * NB, 128 - NB), F32)], 1)
        cross = jnp.concatenate([g[NB:], jnp.zeros((128 - NB, 128), F32)], 0)
        GT[c] = g[:NB] + (cross + cross.T)[:NB]

    def late_far(c):
        one, two = refs(c)
        arrived(E.at[c, xi, ra[near - 1]], rz + 4 * c + 3)
        for x in range(H + 1, H + X - 1):
            one(x, near)
        got_corners(c, 2 * c + 1)
        for x in (H, H + X - 1):
            one(x, near)
        for x in (H - 1, H + X):
            one(x, H)
        g = row_gram(c, H, two, jnp.zeros((NB, NB), F32), symmetric)
        gram_pack(c, GT[c] + jnp.concatenate([g, jnp.zeros((NB, 128 - NB), F32)], 1))

    def square(z):
        hi, lw = split(jnp.concatenate(z, 1))
        return lax.dot_general(jnp.concatenate([hi, lw], 0), hi, NT, preferred_element_type=F32)

    def symmetric(z):
        hi, lw = split(jnp.concatenate(z, 1))
        a = lax.dot_general(jnp.concatenate([hi, lw], 0), hi, NT, preferred_element_type=F32)
        return a[:NB] + a[NB:] + lax.dot_general(hi, lw, NT, preferred_element_type=F32)

    def product(f, w0, w1):
        def body(i, acc):
            for k in range(8):
                x = 8 * i + k
                z = [jnp.concatenate([f(x, r), w0(x, r), w1(x, r)], 0) for r in range(Y)]
                acc = acc + square(z)
            return acc

        return lax.fori_loop(0, X // 8, body, jnp.zeros((2 * NB, NB), F32))

    def gram_rest(c):
        arrived(RQ.at[pl.ds(0, len(fresh[c]))], rr + c)
        GS[c] = product(lambda x, r: FT[c, x, r], lambda x, r: RQ[c, x, r], lambda x, r: RQ[c + 2, x, r])

    def gram_pack(c, g):
        lane = lax.broadcasted_iota(jnp.int32, (8, 128), 1)
        t0 = jnp.zeros((8, 128), F32)
        t1 = jnp.zeros((8, 128), F32)
        for b_ in range(NV // 8):
            block = g[b_ * 8:b_ * 8 + 8]
            ff = jnp.where(lane < NV, block, 0.0)
            fw = jnp.where(lane >= NV, block, 0.0)
            t0 = t0 + (pltpu.roll(ff, b_ * NV, 1) if b_ else ff)
            t1 = t1 + pltpu.roll(fw, (128 - NV + b_ * NW) % 128, 1)
        for b_ in range(NW // 8):
            ww = jnp.where(lane >= NV, g[NV + b_ * 8:NV + b_ * 8 + 8], 0.0)
            t1 = t1 + pltpu.roll(ww, (128 - NV + (NV // 8 + b_) * NW) % 128, 1)
        PK[c, 0] = t0
        PK[c, 1] = t1

    def spread(k, src):
        cs = groups[k]
        part = pl.ds(cs[0], len(cs))
        for o in range(1, span):
            t = lax.rem(me + o, span)
            x, z = (t // K, lax.rem(t, K)) if direct else (mx, t)
            send(src.at[part], RZ.at[me, part], sa + k, ra_ + k, (cut, x, z * 2 + p))

    def sum_start(k):
        cs = groups[k]
        part = pl.ds(cs[0], len(cs))
        for c in cs:
            if direct:
                RZ[me, c] = PK[c]
            else:
                RX[mx, c] = PK[c]
        if direct:
            spread(k, PK)
            return
        for o in range(1, nx):
            send(PK.at[part], RX.at[mx, part], sb + k, rb + k, (cut, lax.rem(mx + o, nx), my))

    def sum_more(k):
        if direct:
            return
        cs = groups[k]
        part = pl.ds(cs[0], len(cs))
        arrived(RX.at[pl.ds(0, nx - 1), part], rb + k)
        for c in cs:
            acc = RX[0, c]
            for t in range(1, nx):
                acc = acc + RX[t, c]
            SM[c] = acc
            RZ[kz, c] = acc
        spread(k, SM)

    e16r = lax.broadcasted_iota(jnp.int32, (NW, NW), 0)
    e16l = lax.broadcasted_iota(jnp.int32, (NW, NW), 1)
    l32 = lax.broadcasted_iota(jnp.int32, (NV, 128), 1)
    r32 = lax.broadcasted_iota(jnp.int32, (NV, 128), 0)
    eye = jnp.where(l32 == r32 + NV, 1.0, 0.0)

    line = lax.broadcasted_iota(jnp.int32, (NV, 1), 0)

    def strip(t, at):
        return pltpu.roll(t, 128 - at, 1) if at else t

    def cleaned(c):
        acc = RZ[0, c]
        for t in range(1, span):
            acc = acc + RZ[t, c]
        acc = acc * (1.0 / total)
        t0, t1 = acc[0], acc[1]
        ff = jnp.concatenate([strip(t0, b * NV) for b in range(NV // 8)], 0)
        fw = jnp.concatenate([strip(t1, b * NW) for b in range(NV // 8)], 0)
        ww = jnp.concatenate([strip(t1, NV // 8 * NW + b * NW) for b in range(NW // 8)], 0)
        b = jnp.where(e16r == e16l, 2.0, 0.0) - ww[:, :NW]
        fn = fw[:, :NW]
        fb = lax.dot_general(fn, b, NN, precision=HP, preferred_element_type=F32)
        sub = lax.dot_general(fb, fn, NT, precision=HP, preferred_element_type=F32)
        sub = jnp.concatenate([sub, jnp.zeros((NV, 128 - NV), F32)], 1)
        wide = jnp.where(l32 < NW, fw, 0.0)
        return jnp.where(l32 < NV, ff - sub, eye) - pltpu.roll(wide, 2 * NV, 1), t1

    def pair(a, b, i, scale, ratio):
        p00, p01, p11 = a[i:i + 1], b[i:i + 1], b[i + 1:i + 2]
        inv = 1.0 / (p00 * p11 - p01 * p01)
        scale = jnp.where(line == i, 1.0 / jnp.sqrt(p00), jnp.where(line == i + 1, jnp.sqrt(p00 * inv), scale))
        ratio = jnp.where(line == i + 1, p01 / p00, ratio)
        return (lambda u, v: ((p11 * u - p01 * v) * inv, (p00 * v - p01 * u) * inv)), scale, ratio

    def eliminate(state, j):
        M, scale, ratio = state
        c = [jnp.broadcast_to(M[:, j + k:j + k + 1], (NV, 128)) for k in range(4)]
        r = [M[j + k:j + k + 1] for k in range(4)]
        solve, scale, ratio = pair(c[0], c[1], j, scale, ratio)
        g0, g1 = solve(r[0], r[1])
        for k in (2, 3):
            h0, h1 = solve(c[k][j:j + 1], c[k][j + 1:j + 2])
            r[k] = r[k] - c[0][j + k:j + k + 1] * g0 - c[1][j + k:j + k + 1] * g1
            c[k] = c[k] - c[0] * h0 - c[1] * h1
        solve, scale, ratio = pair(c[2], c[3], j + 2, scale, ratio)
        g2, g3 = solve(r[2], r[3])
        M = jnp.where(line > j + 1, M - c[0] * g0 - c[1] * g1, M)
        return jnp.where(line > j + 3, M - c[2] * g2 - c[3] * g3, M), scale, ratio

    def scaled(state):
        M, scale, ratio = state
        return pltpu.roll((M - ratio * pltpu.roll(M, 1, 0)) * scale, 128 - NV, 1)

    def factor(k):
        cs = groups[k]
        arrived(RZ.at[pl.ds(0, span - 1), pl.ds(cs[0], len(cs))], ra_ + k)
        both = [cleaned(c) for c in cs]
        blank = jnp.zeros((NV, 128), F32)
        mats = [(m, blank, blank) for m, _ in both]
        for j in range(0, NV, 4):
            mats = [eliminate(m, j) for m in mats]
        mats = [scaled(m) for m in mats]
        for i, c in enumerate(cs):
            low = jnp.where(l32 < NB, mats[i], 0.0)
            LP[c] = low[:NV // 2] + pltpu.roll(low[NV // 2:], 64, 1)
            send(LP.at[c], LR.at[c], sl, rl + c, yp)
        for i, c in enumerate(cs):
            LC[c] = both[i][1]
            LM[p * S + c] = mats[i][:, :NB]

    def unpacked(t1):
        return jnp.where(l32 < NW, jnp.concatenate([strip(t1, b * NW) for b in range(NV // 8)], 0), 0.0)

    def keep_corr(s, wide):
        cor[s] = jnp.concatenate([wide, jnp.zeros((128 - NV, 128), F32)], 0).T[:NW, :NV]

    def take(c):
        s = q * S + c
        arrived(LR.at[c], rl + c)
        half = LR[c]
        LM[s] = jnp.concatenate([half, pltpu.roll(half, 64, 1)], 0)[:, :NB]
        arrived(FA.at[s], rf + c)

    stored = []

    def store(src, dst, i):
        stored.append(load(src, dst, i))

    def finish(s, i):
        hi, lw = split(LM[s])
        left = jnp.concatenate([hi, lw], 0)
        left = jnp.concatenate([left, jnp.concatenate([hi, jnp.zeros((NV, NB), BF)], 0)], 1)

        def body(x):
            z = [jnp.concatenate([FA[s, x, r], RA[s, x, r], RA[s + 2, x, r]], 0) for r in range(Y)]
            zh, zl = split(jnp.concatenate(z, 1))
            o = lax.dot_general(left, jnp.concatenate([zh, zl], 0), NN, preferred_element_type=F32)
            o = o[:NV] + o[NV:]
            for r in range(Y):
                out[s, pl.ds(x * Y + r, NV, stride=J), :] = o[:, r * NZ:(r + 1) * NZ]

        loop(X, 8, body)
        store(out.at[s], out_h.at[s], i)

    def finish_own(c):
        finish(p * S + c, c)

    def finish_rest(c):
        take(c)
        finish(q * S + c, S + c)

    def settle():
        left(O.at[xi, rows(lo)], so)
        for k in range(2):
            left(O.at[xi, H], so + 1 + k)
            left(O.at[H, own], so + 3 + k)
        left(T, sy)
        left(RQ, sr)
        left(RA.at[pl.ds(0, 2)], sc)
        for c in range(S):
            left(E.at[c, xi, pl.ds(0, Y + 2)], sz + c)
            left(E.at[c, pl.ds(0, 4 * H), rows(0)], sx + c)
            left(E.at[c, pl.ds(0, 4), 0], sk + c)

    end = S - 1
    for c in range(S):
        got_y(c)
        send_rest_z(c)
        send_x(c, lq)
        if c == 0:
            send_own_z(end)
            early_corners(0)
        if c == 1:
            early_corners(1) if c < end else None
            early(0)
    for c in range(2, end):
        early_corners(c)
    late_corners(0)
    for c in range(1, end):
        early(c)
    gram_rest(0)
    late_near(0)
    early_corners(end)
    late_far(0)
    for c in range(1, end):
        gram_rest(c)
    early(end)
    for c in range(1, end):
        late_corners(c)
    gram_rest(end)
    for c in range(1, end):
        late_near(c)
        late_far(c)
    sum_start(0)
    late_corners(end)
    sum_more(0)
    late_near(end)
    late_far(end)
    sum_start(1)
    sum_more(1)
    settle()
    factor(0)
    factor(1)
    send(LC, LD, sd, rd, yp)
    for c in range(S):
        finish_own(c)
    for k in range(2):
        part = pl.ds(groups[k][0], len(groups[k]))
        if not direct:
            left(RX.at[pl.ds(0, nx - 1), part], sb + k)
        left(RZ.at[pl.ds(0, span - 1), part], sa + k)
    left(FT, sf)
    for c in range(end):
        finish_rest(c)
    for c in range(S):
        keep_corr(p * S + c, unpacked(LC[c]))
    finish_rest(end)
    arrived(LD, rd)
    for c in range(S):
        keep_corr(q * S + c, unpacked(LD[c]))
    store(cor, cor_h, 2 * S)
    for copy in stored:
        copy.wait()
    left(LP, sl)
    left(LC, sd)


def place(block, corr, block_out, corr_out, sem):
    copies = [pltpu.make_async_copy(block.at[s], block_out.at[s], sem.at[s]) for s in range(block.shape[0])]
    copies.append(pltpu.make_async_copy(corr, corr_out, sem.at[block.shape[0]]))
    for copy in copies:
        copy.start()
    for copy in copies:
        copy.wait()


def on_device(disorder, slice_bounds, start, ritz):
    nc, nx, ny = (lax.axis_size(a) for a in ("cuts", "lx", "ly"))
    count, NV, X, Y, NZ = start.shape
    NR = ritz.shape[1]
    J = X * Y
    S, R, K = count // 2, 2 * Y, ny // 2
    V = pltpu.VMEM
    D = pltpu.SemaphoreType.DMA
    dims = (nc, nx, ny, count, NV, NR, X, Y, NZ)
    hbm = pl.BlockSpec(memory_space=pl.ANY)
    sends, receives = sem_counts(nx, K, S)
    block, corr = pl.pallas_call(
        functools.partial(kernel, dims),
        out_shape=(jax.ShapeDtypeStruct((count, NV * J, NZ), F32),
                   jax.ShapeDtypeStruct((count, 2 * NR, NV), F32)),
        in_specs=[hbm] * 4,
        out_specs=(hbm, hbm),
        scratch_shapes=[
            V((count, NV * J, NZ), F32),
            V((count, 2 * NR, NV), F32),
            pltpu.SMEM((2, count), F32),
            V((J, NZ), jnp.int32),
            V((count, NV * J, NZ), F32),
            V((count, NR * J, NZ), F32),
            D((2 * S + 3,)),
            V((S, X + 2 * H, R + 2 * H, NV, NZ), F32),
            V((S, X, Y, NV, NZ), F32),
            V((X + 2 * H, R + 2 * H, 1, NZ), F32),
            V((S, X + 2 * H, R + 2 * H, NV, NZ), F32),
            V((count, X, Y, NV, NZ), F32),
            V((S, X, Y, NV, NZ), F32),
            V((count + 2, X, Y, NR, NZ), F32),
            V((S + 2, X, Y, NR, NZ), F32),
            V((S, 2 * (NV + 2 * NR), NV + 2 * NR), F32),
            V((S, NV + 2 * NR, 128), F32),
            V((S, 2, 8, 128), F32),
            V((nx, S, 2, 8, 128), F32),
            V((S, 2, 8, 128), F32),
            V((nx * K if direct_sum(nx, K) else K, S, 2, 8, 128), F32),
            V((count, NV, NV + 2 * NR), F32),
            V((S, NV // 2, 128), F32),
            V((S, NV // 2, 128), F32),
            V((S, 8, 128), F32),
            V((S, 8, 128), F32),
            D((sends,)), D((receives,)),
        ],
        compiler_params=pltpu.CompilerParams(collective_id=0, has_side_effects=True, vmem_limit_bytes=48 << 20),
    )(*[pltpu.with_memory_space_constraint(a, pltpu.HBM) for a in (
        disorder.reshape(J, NZ), slice_bounds.T, start.reshape(count, NV * J, NZ), ritz.reshape(count, NR * J, NZ))])
    block, corr = pl.pallas_call(
        place,
        out_shape=(jax.ShapeDtypeStruct(block.shape, F32), jax.ShapeDtypeStruct(corr.shape, F32)),
        in_specs=[hbm] * 2,
        out_specs=(hbm, hbm),
        scratch_shapes=[D((count + 1,))],
        compiler_params=pltpu.CompilerParams(vmem_limit_bytes=1 << 20),
    )(block, corr)
    return (block.reshape(start.shape), corr)


def solution(mesh):
    in_specs = (
        P("lx", "ly", None),
        P("cuts", None),
        P("cuts", None, "lx", "ly", None),
        P("cuts", None, "lx", "ly", None),
    )
    out_specs = (P("cuts", None, "lx", "ly", None), P("cuts", None, None))
    return jax.shard_map(
        on_device, mesh=mesh, in_specs=in_specs, out_specs=out_specs, check_vma=False
    )
```

```python
import functools

import jax
import jax.numpy as jnp
from jax import lax
from jax.experimental import pallas as pl
from jax.experimental.pallas import tpu as pltpu
from jax.sharding import PartitionSpec as P

LEVELS = 256
MESH = pl.DeviceIdType.MESH
HP = lax.Precision.HIGHEST
H = 2
BF = jnp.bfloat16
F32 = jnp.float32
NT = (((1,), (1,)), ((), ()))
NN = (((1,), (0,)), ((), ()))
TN = (((0,), (0,)), ((), ()))


def direct_sum(nx, K):
    return nx * K <= 16


def sem_counts(nx, K, S):
    more = 0 if direct_sum(nx, K) else 2
    return 13 + 3 * S + more, 10 + 11 * S + more


def split(z):
    hi = z.astype(BF)
    return hi, (z - hi.astype(F32)).astype(BF)


def loop(n, unroll, body):
    def step(i, carry):
        for k in range(unroll):
            body(i * unroll + k)
        return carry

    if n % unroll:
        unroll = 1
    lax.fori_loop(0, n // unroll, step, 0)


def kernel(dims, dis_h, bnd_h, start_h, ritz_h, out_h, cor_h, out, cor, bnd, dis, start, ritz, ls, E, T, O, U, FA, FT,
           RA, RQ, GS, GT, PK, RX, SM, RZ, LM, LP, LR, LC, LD, ss, rs):
    nc, nx, ny, count, NV, NR, X, Y, NZ = dims
    S = count // 2
    R = 2 * Y
    J = X * Y
    K = ny // 2
    total = float(J * NZ * nx * ny)
    NW = 2 * NR
    NB = NV + NW
    cut, mx, my = lax.axis_index("cuts"), lax.axis_index("lx"), lax.axis_index("ly")
    p = lax.rem(my, 2)
    q = 1 - p
    kz = my // 2
    yp = (cut, mx, kz * 2 + q)
    zup = (cut, mx, lax.rem(kz + 1, K) * 2 + p)
    zdown = (cut, mx, lax.rem(kz + K - 1, K) * 2 + p)
    xup = (cut, lax.rem(mx + 1, nx), my)
    xdown = (cut, lax.rem(mx + nx - 1, nx), my)
    cup = (lax.rem(cut + 1, nc), mx, my)
    cdown = (lax.rem(cut + nc - 1, nc), mx, my)

    def load(src, dst, i):
        copy = pltpu.make_async_copy(src, dst, ls.at[i])
        copy.start()
        return copy

    barrier = pltpu.get_barrier_semaphore()

    def greet(dev):
        pl.semaphore_signal(barrier, inc=1, device_id=dev, device_id_type=MESH)

    greet(yp)
    if direct_sum(nx, K):
        for o in range(1, nx * K):
            t = lax.rem(mx * K + kz + o, nx * K)
            greet((cut, t // K, lax.rem(t, K) * 2 + p))
        greeted = nx * K + 2
    else:
        for o in range(1, nx):
            greet((cut, lax.rem(mx + o, nx), my))
        for o in range(1, K):
            greet((cut, mx, lax.rem(kz + o, K) * 2 + p))
        greeted = nx + K + 1
    greet(cup)
    greet(cdown)

    away, kept = [], []
    for c in range(S):
        kept.append(load(start_h.at[p * S + c], start.at[S + c], S + c))
        if c == 0:
            level_load = load(dis_h, dis, 2 * S)
        away.append(load(start_h.at[q * S + c], start.at[c], c))
    bound_load = load(bnd_h, bnd, 2 * S + 2)
    ritz_load = load(ritz_h, ritz, 2 * S + 1)

    lo = H + Y * p
    lq = H + Y * q
    xi = pl.ds(H, X)
    mid = pl.ds(H + 1, X - 2)
    def stage_away(c):
        away[c].wait()
        for x in range(X):
            for r in range(Y):
                T[c, x, r] = start[c, pl.ds(x * Y + r, NV, stride=J), :]

    def stage_kept(c):
        kept[c].wait()
        for x in range(X):
            for r in range(Y):
                E[c, H + x, lo + r] = start[S + c, pl.ds(x * Y + r, NV, stride=J), :]

    used = [0, 0]

    def take_slots(kind, n=1):
        i = used[kind]
        used[kind] += n
        return i

    def send(src, dst, i, j, dev):
        pltpu.make_async_remote_copy(
            src_ref=src, dst_ref=dst, send_sem=ss.at[i], recv_sem=rs.at[j], device_id=dev, device_id_type=MESH).start()

    def left(src, i):
        pltpu.make_async_remote_copy(
            src_ref=src, dst_ref=src, send_sem=ss.at[i], recv_sem=ss.at[i],
            device_id=yp, device_id_type=MESH).wait_send()

    def arrived(dst, j):
        pltpu.make_async_remote_copy(
            src_ref=dst, dst_ref=dst, send_sem=rs.at[j], recv_sem=rs.at[j],
            device_id=yp, device_id_type=MESH).wait_recv()

    def rows(at):
        return pl.ds(at, Y)

    so, sy, sf, sl, sr, sc, sd = (take_slots(0, n) for n in (5, 1, 1, 1, 1, 1, 1))
    sz, sx, sk, sa = (take_slots(0, n) for n in (S, S, S, 2))
    ro, ry, rf, rl, rx, rc, rr, ra_, rd = (take_slots(1, n) for n in (5, S, S, S, S, 2, S, 2, 1))
    rz, rk = take_slots(1, 4 * S), take_slots(1, 2 * S)
    groups = [list(range(S - 1)), [S - 1]]
    direct = direct_sum(nx, K)
    span = nx * K if direct else K
    me = mx * K + kz if direct else kz
    sb, rb = (0, 0) if direct else (take_slots(0, 2), take_slots(1, 2))

    def send_y(c):
        send(T.at[c], E.at[c, xi, rows(lo)], sy, ry + c, yp)

    def z_dev(half):
        return (cut, mx, jnp.where(half == 1, zup[2], zdown[2]))

    def send_own_z(c):
        dst = jnp.where(p == 1, 0, H + R)
        send(E.at[c, xi, rows(lo)], E.at[c, xi, rows(dst)], sz + c, rz + 4 * c, z_dev(p))

    def send_rest_z(c):
        src = [jnp.where(q == 1, H + R - 1 - k, H + k) for k in range(2)]
        dst = [jnp.where(q == 1, H - 1 - k, H + R + k) for k in range(2)]
        for x in (H, H + X - 1):
            send(E.at[c, x, src[0]], E.at[c, x, dst[0]], sz + c, rz + 4 * c + 1, z_dev(q))
        send(E.at[c, mid, src[0]], E.at[c, mid, dst[0]], sz + c, rz + 4 * c + 2, z_dev(q))
        send(E.at[c, xi, src[1]], E.at[c, xi, dst[1]], sz + c, rz + 4 * c + 3, z_dev(q))

    def send_x(c, at):
        send(E.at[c, pl.ds(X, H), rows(at)], E.at[c, pl.ds(0, H), rows(at)], sx + c, rx + c, xup)
        send(E.at[c, pl.ds(H, H), rows(at)], E.at[c, pl.ds(H + X, H), rows(at)], sx + c, rx + c, xdown)

    def got_x(c):
        arrived(E.at[c, pl.ds(0, 4 * H), rows(0)], rx + c)

    def send_o(half):
        side = 1 - half
        src = jnp.where(half == 1, H + R - 1, H)
        dst = jnp.where(half == 1, 1, H + R)
        send(O.at[xi, src], O.at[xi, dst], so + 1 + side, ro + 1 + side, z_dev(half))

    own = pl.ds(H, R)

    def relay_o():
        arrived(O.at[xi, rows(lq)], ro)
        send_o(q)
        send(O.at[H + X - 1, own], O.at[H - 1, own], so + 3, ro + 3, xup)
        send(O.at[H, own], O.at[H + X, own], so + 4, ro + 4, xdown)

    level_load.wait()
    for x in range(X):
        for r in range(Y):
            row = dis[pl.ds(x * Y + r, 1), :].astype(F32)
            O[H + x, lo + r] = 16.5 * (row / F32(LEVELS - 1) - 0.5)
    stage_kept(0)
    pl.semaphore_wait(barrier, greeted)
    send(O.at[xi, rows(lo)], O.at[xi, rows(lo)], so, ro, yp)
    send_o(p)
    send_own_z(0)
    stage_away(0)
    send_y(0)
    send_x(0, lo)
    for c in range(1, S):
        stage_away(c)
        send_y(c)
        stage_kept(c)
        if c == 1:
            relay_o()
        if c < S - 1:
            send_own_z(c)
        send_x(c, lo)
    bound_load.wait()
    ritz_load.wait()
    for s in range(count):
        for x in range(X):
            for r in range(Y):
                RA[s + 1, x, r] = ritz[s, pl.ds(x * Y + r, NR, stride=J), :]
    send(RA.at[count], RA.at[0], sc, rc, cup)
    send(RA.at[1], RA.at[count + 1], sc, rc + 1, cdown)

    arrived(RA.at[0], rc)
    arrived(RA.at[count + 1], rc + 1)

    @pl.when(cut == 0)
    def _():
        RA[0] = jnp.zeros((X, Y, NR, NZ), F32)

    @pl.when(cut == nc - 1)
    def _():
        RA[count + 1] = jnp.zeros((X, Y, NR, NZ), F32)

    fresh = [[j for j in (c, c + 2) if j >= 2 or c < 2] for c in range(S)]
    fresh = [[j for j in js if j not in sum(fresh[:c], [])] for c, js in enumerate(fresh)]
    for c in range(S):
        for j in fresh[c]:
            send(RA.at[q * S + j], RQ.at[j], sr, rr + c, yp)

    def got_y(c):
        arrived(E.at[c, xi, rows(lq)], ry + c)

    last = R + 2 * H - 1
    ra = [a + p * (last - 2 * a) for a in range(last + 1)]
    near, far = H - 1, H + R

    def point(src, x, a, centre):
        v = src(x, a)
        beside = src(x + 1, a) + src(x - 1, a)
        beside = beside + src(x, a + 1) + src(x, a - 1)
        beside = beside + pltpu.roll(v, 1, 1) + pltpu.roll(v, NZ - 1, 1)
        level = jnp.broadcast_to(O[x, ra[a]] - centre, (NV, NZ))
        return level * v - beside

    def refs(c):
        s = p * S + c
        centre = (bnd[0, s] + bnd[1, s]) / 2.0

        def from_e(x, a):
            return E[c, x, ra[a]]

        def from_u(x, a):
            return U[c, x, ra[a]]

        def one(x, a):
            U[c, x, ra[a]] = point(from_e, x, a, centre)

        def two(x, a):
            return point(from_u, x, a, centre) * (2.0 / 256.0) - from_e(x, a)

        return one, two

    def corners(c, a, k):
        send(E.at[c, H + X - 1, ra[a]], E.at[c, H - 1, ra[a]], sk + c, rk + k, xup)
        send(E.at[c, H, ra[a]], E.at[c, H + X, ra[a]], sk + c, rk + k, xdown)

    def got_corners(c, k):
        arrived(E.at[c, pl.ds(0, 2), 0], rk + k)

    def early_corners(c):
        arrived(E.at[c, xi, rows(jnp.where(p == 1, 0, H + R))], rz + 4 * c)
        corners(c, far, 2 * c)

    def late_corners(c):
        arrived(E.at[c, pl.ds(0, 2), 0], rz + 4 * c + 1)
        corners(c, near, 2 * c + 1)

    def got_o():
        arrived(O.at[xi, H - 1], ro + 1)
        arrived(O.at[xi, H + R], ro + 2)
        arrived(O.at[H - 1, own], ro + 3)
        arrived(O.at[H + X, own], ro + 4)

    def early(c):
        one, two = refs(c)
        got_x(c)
        if c == 0:
            got_o()

        def inner(i):
            for a in range(H + 1, far + 1):
                one(H + 1 + i, a)

        loop(X - 2, 6, inner)
        for x in (H, H + X - 1):
            for a in range(H + 1, far):
                one(x, a)
        for x in (H - 1, H + X):
            for a in range(H + 1, far - 1):
                one(x, a)
        got_corners(c, 2 * c)
        for x in (H, H + X - 1):
            one(x, far)
        for x in (H - 1, H + X):
            one(x, far - 1)

        def outer(i):
            for a in range(H + Y, far):
                FT[c, i, ra[a] - lq] = two(H + i, a)

        loop(X, 8, outer)
        send(FT.at[c], FA.at[p * S + c], sf, rf + c, yp)

    def row_gram(c, a, two, acc, product=None):
        s, r = p * S + c, ra[a] - lo
        for i in range(0, X, 2):
            z = []
            for x in (i, i + 1):
                f = two(H + x, a)
                FA[s, x, r] = f
                z.append(jnp.concatenate([f, RA[s, x, r], RA[s + 2, x, r]], 0))
            acc = acc + (product or square)(z)
        return acc

    def late_near(c):
        one, two = refs(c)
        arrived(E.at[c, mid, ra[near]], rz + 4 * c + 2)
        for x in range(H, H + X):
            one(x, H)
        g = GS[c]
        for a in range(H + 1, H + Y):
            g = row_gram(c, a, two, g)
        g = jnp.concatenate([g, jnp.zeros((2 * NB, 128 - NB), F32)], 1)
        cross = jnp.concatenate([g[NB:], jnp.zeros((128 - NB, 128), F32)], 0)
        GT[c] = g[:NB] + (cross + cross.T)[:NB]

    def late_far(c):
        one, two = refs(c)
        arrived(E.at[c, xi, ra[near - 1]], rz + 4 * c + 3)
        for x in range(H + 1, H + X - 1):
            one(x, near)
        got_corners(c, 2 * c + 1)
        for x in (H, H + X - 1):
            one(x, near)
        for x in (H - 1, H + X):
            one(x, H)
        g = row_gram(c, H, two, jnp.zeros((NB, NB), F32), symmetric)
        gram_pack(c, GT[c] + jnp.concatenate([g, jnp.zeros((NB, 128 - NB), F32)], 1))

    def square(z):
        hi, lw = split(jnp.concatenate(z, 1))
        return lax.dot_general(jnp.concatenate([hi, lw], 0), hi, NT, preferred_element_type=F32)

    def symmetric(z):
        hi, lw = split(jnp.concatenate(z, 1))
        a = lax.dot_general(jnp.concatenate([hi, lw], 0), hi, NT, preferred_element_type=F32)
        return a[:NB] + a[NB:] + lax.dot_general(hi, lw, NT, preferred_element_type=F32)

    def product(f, w0, w1):
        def body(i, acc):
            for k in range(8):
                x = 8 * i + k
                z = [jnp.concatenate([f(x, r), w0(x, r), w1(x, r)], 0) for r in range(Y)]
                acc = acc + square(z)
            return acc

        return lax.fori_loop(0, X // 8, body, jnp.zeros((2 * NB, NB), F32))

    def gram_rest(c):
        arrived(RQ.at[pl.ds(0, len(fresh[c]))], rr + c)
        GS[c] = product(lambda x, r: FT[c, x, r], lambda x, r: RQ[c, x, r], lambda x, r: RQ[c + 2, x, r])

    def gram_pack(c, g):
        lane = lax.broadcasted_iota(jnp.int32, (8, 128), 1)
        t0 = jnp.zeros((8, 128), F32)
        t1 = jnp.zeros((8, 128), F32)
        for b_ in range(NV // 8):
            block = g[b_ * 8:b_ * 8 + 8]
            ff = jnp.where(lane < NV, block, 0.0)
            fw = jnp.where(lane >= NV, block, 0.0)
            t0 = t0 + (pltpu.roll(ff, b_ * NV, 1) if b_ else ff)
            t1 = t1 + pltpu.roll(fw, (128 - NV + b_ * NW) % 128, 1)
        for b_ in range(NW // 8):
            ww = jnp.where(lane >= NV, g[NV + b_ * 8:NV + b_ * 8 + 8], 0.0)
            t1 = t1 + pltpu.roll(ww, (128 - NV + (NV // 8 + b_) * NW) % 128, 1)
        PK[c, 0] = t0
        PK[c, 1] = t1

    def spread(k, src):
        cs = groups[k]
        part = pl.ds(cs[0], len(cs))
        for o in range(1, span):
            t = lax.rem(me + o, span)
            x, z = (t // K, lax.rem(t, K)) if direct else (mx, t)
            send(src.at[part], RZ.at[me, part], sa + k, ra_ + k, (cut, x, z * 2 + p))

    def sum_start(k):
        cs = groups[k]
        part = pl.ds(cs[0], len(cs))
        for c in cs:
            if direct:
                RZ[me, c] = PK[c]
            else:
                RX[mx, c] = PK[c]
        if direct:
            spread(k, PK)
            return
        for o in range(1, nx):
            send(PK.at[part], RX.at[mx, part], sb + k, rb + k, (cut, lax.rem(mx + o, nx), my))

    def sum_more(k):
        if direct:
            return
        cs = groups[k]
        part = pl.ds(cs[0], len(cs))
        arrived(RX.at[pl.ds(0, nx - 1), part], rb + k)
        for c in cs:
            acc = RX[0, c]
            for t in range(1, nx):
                acc = acc + RX[t, c]
            SM[c] = acc
            RZ[kz, c] = acc
        spread(k, SM)

    e16r = lax.broadcasted_iota(jnp.int32, (NW, NW), 0)
    e16l = lax.broadcasted_iota(jnp.int32, (NW, NW), 1)
    l32 = lax.broadcasted_iota(jnp.int32, (NV, 128), 1)
    r32 = lax.broadcasted_iota(jnp.int32, (NV, 128), 0)
    eye = jnp.where(l32 == r32 + NV, 1.0, 0.0)

    line = lax.broadcasted_iota(jnp.int32, (NV, 1), 0)

    def strip(t, at):
        return pltpu.roll(t, 128 - at, 1) if at else t

    def cleaned(c):
        acc = RZ[0, c]
        for t in range(1, span):
            acc = acc + RZ[t, c]
        acc = acc * (1.0 / total)
        t0, t1 = acc[0], acc[1]
        ff = jnp.concatenate([strip(t0, b * NV) for b in range(NV // 8)], 0)
        fw = jnp.concatenate([strip(t1, b * NW) for b in range(NV // 8)], 0)
        ww = jnp.concatenate([strip(t1, NV // 8 * NW + b * NW) for b in range(NW // 8)], 0)
        b = jnp.where(e16r == e16l, 2.0, 0.0) - ww[:, :NW]
        fn = fw[:, :NW]
        fb = lax.dot_general(fn, b, NN, precision=HP, preferred_element_type=F32)
        sub = lax.dot_general(fb, fn, NT, precision=HP, preferred_element_type=F32)
        sub = jnp.concatenate([sub, jnp.zeros((NV, 128 - NV), F32)], 1)
        wide = jnp.where(l32 < NW, fw, 0.0)
        square_of = jnp.where(l32 == r32, ff, 0.0)
        by_row = 1.0 / jnp.sqrt(jnp.sum(square_of, axis=1, keepdims=True))
        by_lane = jnp.sum(square_of, axis=0, keepdims=True)
        by_lane = jnp.where(l32[:1] < NV, 1.0 / jnp.sqrt(by_lane), 1.0)
        M = jnp.where(l32 < NV, ff - sub, eye) - pltpu.roll(wide, 2 * NV, 1)
        return M * (by_row * by_lane), t1

    def pair(a, b, i, scale, ratio):
        p00, p01, p11 = a[i:i + 1], b[i:i + 1], b[i + 1:i + 2]
        inv = 1.0 / (p00 * p11 - p01 * p01)
        scale = jnp.where(line == i, 1.0 / jnp.sqrt(p00), jnp.where(line == i + 1, jnp.sqrt(p00 * inv), scale))
        ratio = jnp.where(line == i + 1, p01 / p00, ratio)
        return (lambda u, v: ((p11 * u - p01 * v) * inv, (p00 * v - p01 * u) * inv)), scale, ratio

    def eliminate(state, j):
        M, scale, ratio = state
        c = [jnp.broadcast_to(M[:, j + k:j + k + 1], (NV, 128)) for k in range(4)]
        r = [M[j + k:j + k + 1] for k in range(4)]
        solve, scale, ratio = pair(c[0], c[1], j, scale, ratio)
        g0, g1 = solve(r[0], r[1])
        for k in (2, 3):
            h0, h1 = solve(c[k][j:j + 1], c[k][j + 1:j + 2])
            r[k] = r[k] - c[0][j + k:j + k + 1] * g0 - c[1][j + k:j + k + 1] * g1
            c[k] = c[k] - c[0] * h0 - c[1] * h1
        solve, scale, ratio = pair(c[2], c[3], j + 2, scale, ratio)
        g2, g3 = solve(r[2], r[3])
        M = jnp.where(line > j + 1, M - c[0] * g0 - c[1] * g1, M)
        return jnp.where(line > j + 3, M - c[2] * g2 - c[3] * g3, M), scale, ratio

    def scaled(state):
        M, scale, ratio = state
        return pltpu.roll((M - ratio * pltpu.roll(M, 1, 0)) * scale, 128 - NV, 1)

    def factor(k):
        cs = groups[k]
        arrived(RZ.at[pl.ds(0, span - 1), pl.ds(cs[0], len(cs))], ra_ + k)
        both = [cleaned(c) for c in cs]
        blank = jnp.zeros((NV, 128), F32)
        mats = [(m, blank, blank) for m, _ in both]
        for j in range(0, NV, 4):
            mats = [eliminate(m, j) for m in mats]
        mats = [scaled(m) for m in mats]
        for i, c in enumerate(cs):
            low = jnp.where(l32 < NB, mats[i], 0.0)
            LP[c] = low[:NV // 2] + pltpu.roll(low[NV // 2:], 64, 1)
            send(LP.at[c], LR.at[c], sl, rl + c, yp)
        for i, c in enumerate(cs):
            LC[c] = both[i][1]
            LM[p * S + c] = mats[i][:, :NB]

    def unpacked(t1):
        return jnp.where(l32 < NW, jnp.concatenate([strip(t1, b * NW) for b in range(NV // 8)], 0), 0.0)

    def keep_corr(s, wide):
        cor[s] = jnp.concatenate([wide, jnp.zeros((128 - NV, 128), F32)], 0).T[:NW, :NV]

    def take(c):
        s = q * S + c
        arrived(LR.at[c], rl + c)
        half = LR[c]
        LM[s] = jnp.concatenate([half, pltpu.roll(half, 64, 1)], 0)[:, :NB]
        arrived(FA.at[s], rf + c)

    stored = []

    def store(src, dst, i):
        stored.append(load(src, dst, i))

    def finish(s, i):
        hi, lw = split(LM[s])
        left = jnp.concatenate([hi, lw], 0)
        left = jnp.concatenate([left, jnp.concatenate([hi, jnp.zeros((NV, NB), BF)], 0)], 1)

        def body(x):
            z = [jnp.concatenate([FA[s, x, r], RA[s, x, r], RA[s + 2, x, r]], 0) for r in range(Y)]
            zh, zl = split(jnp.concatenate(z, 1))
            o = lax.dot_general(left, jnp.concatenate([zh, zl], 0), NN, preferred_element_type=F32)
            o = o[:NV] + o[NV:]
            for r in range(Y):
                out[s, pl.ds(x * Y + r, NV, stride=J), :] = o[:, r * NZ:(r + 1) * NZ]

        loop(X, 8, body)
        store(out.at[s], out_h.at[s], i)

    def finish_own(c):
        finish(p * S + c, c)

    def finish_rest(c):
        take(c)
        finish(q * S + c, S + c)

    def settle():
        left(O.at[xi, rows(lo)], so)
        for k in range(2):
            left(O.at[xi, H], so + 1 + k)
            left(O.at[H, own], so + 3 + k)
        left(T, sy)
        left(RQ, sr)
        left(RA.at[pl.ds(0, 2)], sc)
        for c in range(S):
            left(E.at[c, xi, pl.ds(0, Y + 2)], sz + c)
            left(E.at[c, pl.ds(0, 4 * H), rows(0)], sx + c)
            left(E.at[c, pl.ds(0, 4), 0], sk + c)

    end = S - 1
    for c in range(S):
        got_y(c)
        send_rest_z(c)
        send_x(c, lq)
        if c == 0:
            send_own_z(end)
            early_corners(0)
        if c == 1:
            early_corners(1) if c < end else None
            early(0)
    for c in range(2, end):
        early_corners(c)
    late_corners(0)
    for c in range(1, end):
        early(c)
    gram_rest(0)
    late_near(0)
    early_corners(end)
    late_far(0)
    for c in range(1, end):
        gram_rest(c)
    early(end)
    for c in range(1, end):
        late_corners(c)
    gram_rest(end)
    for c in range(1, end):
        late_near(c)
        late_far(c)
    sum_start(0)
    late_corners(end)
    sum_more(0)
    late_near(end)
    late_far(end)
    sum_start(1)
    sum_more(1)
    settle()
    factor(0)
    factor(1)
    send(LC, LD, sd, rd, yp)
    for c in range(S):
        finish_own(c)
    for k in range(2):
        part = pl.ds(groups[k][0], len(groups[k]))
        if not direct:
            left(RX.at[pl.ds(0, nx - 1), part], sb + k)
        left(RZ.at[pl.ds(0, span - 1), part], sa + k)
    left(FT, sf)
    for c in range(end):
        finish_rest(c)
    for c in range(S):
        keep_corr(p * S + c, unpacked(LC[c]))
    finish_rest(end)
    arrived(LD, rd)
    for c in range(S):
        keep_corr(q * S + c, unpacked(LD[c]))
    store(cor, cor_h, 2 * S)
    for copy in stored:
        copy.wait()
    left(LP, sl)
    left(LC, sd)


def place(block, corr, block_out, corr_out, sem):
    copies = [pltpu.make_async_copy(block.at[s], block_out.at[s], sem.at[s]) for s in range(block.shape[0])]
    copies.append(pltpu.make_async_copy(corr, corr_out, sem.at[block.shape[0]]))
    for copy in copies:
        copy.start()
    for copy in copies:
        copy.wait()


def on_device(disorder, slice_bounds, start, ritz):
    nc, nx, ny = (lax.axis_size(a) for a in ("cuts", "lx", "ly"))
    count, NV, X, Y, NZ = start.shape
    NR = ritz.shape[1]
    J = X * Y
    S, R, K = count // 2, 2 * Y, ny // 2
    V = pltpu.VMEM
    D = pltpu.SemaphoreType.DMA
    dims = (nc, nx, ny, count, NV, NR, X, Y, NZ)
    hbm = pl.BlockSpec(memory_space=pl.ANY)
    sends, receives = sem_counts(nx, K, S)
    block, corr = pl.pallas_call(
        functools.partial(kernel, dims),
        out_shape=(jax.ShapeDtypeStruct((count, NV * J, NZ), F32),
                   jax.ShapeDtypeStruct((count, 2 * NR, NV), F32)),
        in_specs=[hbm] * 4,
        out_specs=(hbm, hbm),
        scratch_shapes=[
            V((count, NV * J, NZ), F32),
            V((count, 2 * NR, NV), F32),
            pltpu.SMEM((2, count), F32),
            V((J, NZ), jnp.int32),
            V((count, NV * J, NZ), F32),
            V((count, NR * J, NZ), F32),
            D((2 * S + 3,)),
            V((S, X + 2 * H, R + 2 * H, NV, NZ), F32),
            V((S, X, Y, NV, NZ), F32),
            V((X + 2 * H, R + 2 * H, 1, NZ), F32),
            V((S, X + 2 * H, R + 2 * H, NV, NZ), F32),
            V((count, X, Y, NV, NZ), F32),
            V((S, X, Y, NV, NZ), F32),
            V((count + 2, X, Y, NR, NZ), F32),
            V((S + 2, X, Y, NR, NZ), F32),
            V((S, 2 * (NV + 2 * NR), NV + 2 * NR), F32),
            V((S, NV + 2 * NR, 128), F32),
            V((S, 2, 8, 128), F32),
            V((nx, S, 2, 8, 128), F32),
            V((S, 2, 8, 128), F32),
            V((nx * K if direct_sum(nx, K) else K, S, 2, 8, 128), F32),
            V((count, NV, NV + 2 * NR), F32),
            V((S, NV // 2, 128), F32),
            V((S, NV // 2, 128), F32),
            V((S, 8, 128), F32),
            V((S, 8, 128), F32),
            D((sends,)), D((receives,)),
        ],
        compiler_params=pltpu.CompilerParams(collective_id=0, has_side_effects=True, vmem_limit_bytes=48 << 20),
    )(*[pltpu.with_memory_space_constraint(a, pltpu.HBM) for a in (
        disorder.reshape(J, NZ), slice_bounds.T, start.reshape(count, NV * J, NZ), ritz.reshape(count, NR * J, NZ))])
    block, corr = pl.pallas_call(
        place,
        out_shape=(jax.ShapeDtypeStruct(block.shape, F32), jax.ShapeDtypeStruct(corr.shape, F32)),
        in_specs=[hbm] * 2,
        out_specs=(hbm, hbm),
        scratch_shapes=[D((count + 1,))],
        compiler_params=pltpu.CompilerParams(vmem_limit_bytes=1 << 20),
    )(block, corr)
    return (block.reshape(start.shape), corr)


def solution(mesh):
    in_specs = (
        P("lx", "ly", None),
        P("cuts", None),
        P("cuts", None, "lx", "ly", None),
        P("cuts", None, "lx", "ly", None),
    )
    out_specs = (P("cuts", None, "lx", "ly", None), P("cuts", None, None))
    return jax.shard_map(
        on_device, mesh=mesh, in_specs=in_specs, out_specs=out_specs, check_vma=False
    )
```

```python
import functools

import jax
import jax.numpy as jnp
from jax import lax
from jax.experimental import pallas as pl
from jax.experimental.pallas import tpu as pltpu
from jax.sharding import PartitionSpec as P

LEVELS = 256
MESH = pl.DeviceIdType.MESH
HP = lax.Precision.HIGHEST
H = 2
BF = jnp.bfloat16
F32 = jnp.float32
NT = (((1,), (1,)), ((), ()))
NN = (((1,), (0,)), ((), ()))
TN = (((0,), (0,)), ((), ()))


def direct_sum(nx, K):
    return nx * K <= 16


def sem_counts(nx, K, S):
    more = 0 if direct_sum(nx, K) else 2
    return 13 + 3 * S + more, 10 + 11 * S + more


def split(z):
    hi = z.astype(BF)
    return hi, (z - hi.astype(F32)).astype(BF)


def loop(n, unroll, body):
    def step(i, carry):
        for k in range(unroll):
            body(i * unroll + k)
        return carry

    if n % unroll:
        unroll = 1
    lax.fori_loop(0, n // unroll, step, 0)


def kernel(dims, dis_h, bnd_h, start_h, ritz_h, out_h, cor_h, out, cor, bnd, dis, start, ritz, ls, E, T, O, U, FA, FT,
           RA, RQ, GS, GT, PK, RX, SM, RZ, LM, LP, LR, LC, LD, ss, rs):
    nc, nx, ny, count, NV, NR, X, Y, NZ = dims
    S = count // 2
    R = 2 * Y
    J = X * Y
    K = ny // 2
    total = float(J * NZ * nx * ny)
    NW = 2 * NR
    NB = NV + NW
    cut, mx, my = lax.axis_index("cuts"), lax.axis_index("lx"), lax.axis_index("ly")
    p = lax.rem(my, 2)
    q = 1 - p
    kz = my // 2
    yp = (cut, mx, kz * 2 + q)
    zup = (cut, mx, lax.rem(kz + 1, K) * 2 + p)
    zdown = (cut, mx, lax.rem(kz + K - 1, K) * 2 + p)
    xup = (cut, lax.rem(mx + 1, nx), my)
    xdown = (cut, lax.rem(mx + nx - 1, nx), my)
    cup = (lax.rem(cut + 1, nc), mx, my)
    cdown = (lax.rem(cut + nc - 1, nc), mx, my)

    def load(src, dst, i):
        copy = pltpu.make_async_copy(src, dst, ls.at[i])
        copy.start()
        return copy

    barrier = pltpu.get_barrier_semaphore()

    def greet(dev):
        pl.semaphore_signal(barrier, inc=1, device_id=dev, device_id_type=MESH)

    greet(yp)
    if direct_sum(nx, K):
        for o in range(1, nx * K):
            t = lax.rem(mx * K + kz + o, nx * K)
            greet((cut, t // K, lax.rem(t, K) * 2 + p))
        greeted = nx * K + 2
    else:
        for o in range(1, nx):
            greet((cut, lax.rem(mx + o, nx), my))
        for o in range(1, K):
            greet((cut, mx, lax.rem(kz + o, K) * 2 + p))
        greeted = nx + K + 1
    greet(cup)
    greet(cdown)

    away, kept = [], []
    for c in range(S):
        kept.append(load(start_h.at[p * S + c], start.at[S + c], S + c))
        if c == 0:
            level_load = load(dis_h, dis, 2 * S)
        away.append(load(start_h.at[q * S + c], start.at[c], c))
    bound_load = load(bnd_h, bnd, 2 * S + 2)
    ritz_load = load(ritz_h, ritz, 2 * S + 1)

    lo = H + Y * p
    lq = H + Y * q
    xi = pl.ds(H, X)
    mid = pl.ds(H + 1, X - 2)
    def stage_away(c):
        away[c].wait()
        for x in range(X):
            for r in range(Y):
                T[c, x, r] = start[c, pl.ds(x * Y + r, NV, stride=J), :]

    def stage_kept(c):
        kept[c].wait()
        for x in range(X):
            for r in range(Y):
                E[c, H + x, lo + r] = start[S + c, pl.ds(x * Y + r, NV, stride=J), :]

    used = [0, 0]

    def take_slots(kind, n=1):
        i = used[kind]
        used[kind] += n
        return i

    def send(src, dst, i, j, dev):
        pltpu.make_async_remote_copy(
            src_ref=src, dst_ref=dst, send_sem=ss.at[i], recv_sem=rs.at[j], device_id=dev, device_id_type=MESH).start()

    def left(src, i):
        pltpu.make_async_remote_copy(
            src_ref=src, dst_ref=src, send_sem=ss.at[i], recv_sem=ss.at[i],
            device_id=yp, device_id_type=MESH).wait_send()

    def arrived(dst, j):
        pltpu.make_async_remote_copy(
            src_ref=dst, dst_ref=dst, send_sem=rs.at[j], recv_sem=rs.at[j],
            device_id=yp, device_id_type=MESH).wait_recv()

    def rows(at):
        return pl.ds(at, Y)

    so, sy, sf, sl, sr, sc, sd = (take_slots(0, n) for n in (5, 1, 1, 1, 1, 1, 1))
    sz, sx, sk, sa = (take_slots(0, n) for n in (S, S, S, 2))
    ro, ry, rf, rl, rx, rc, rr, ra_, rd = (take_slots(1, n) for n in (5, S, S, S, S, 2, S, 2, 1))
    rz, rk = take_slots(1, 4 * S), take_slots(1, 2 * S)
    groups = [list(range(S - 1)), [S - 1]]
    direct = direct_sum(nx, K)
    span = nx * K if direct else K
    me = mx * K + kz if direct else kz
    sb, rb = (0, 0) if direct else (take_slots(0, 2), take_slots(1, 2))

    def send_y(c):
        send(T.at[c], E.at[c, xi, rows(lo)], sy, ry + c, yp)

    def z_dev(half):
        return (cut, mx, jnp.where(half == 1, zup[2], zdown[2]))

    def send_own_z(c):
        dst = jnp.where(p == 1, 0, H + R)
        send(E.at[c, xi, rows(lo)], E.at[c, xi, rows(dst)], sz + c, rz + 4 * c, z_dev(p))

    def send_rest_z(c):
        src = [jnp.where(q == 1, H + R - 1 - k, H + k) for k in range(2)]
        dst = [jnp.where(q == 1, H - 1 - k, H + R + k) for k in range(2)]
        for x in (H, H + X - 1):
            send(E.at[c, x, src[0]], E.at[c, x, dst[0]], sz + c, rz + 4 * c + 1, z_dev(q))
        send(E.at[c, mid, src[0]], E.at[c, mid, dst[0]], sz + c, rz + 4 * c + 2, z_dev(q))
        send(E.at[c, xi, src[1]], E.at[c, xi, dst[1]], sz + c, rz + 4 * c + 3, z_dev(q))

    def send_x(c, at):
        send(E.at[c, pl.ds(X, H), rows(at)], E.at[c, pl.ds(0, H), rows(at)], sx + c, rx + c, xup)
        send(E.at[c, pl.ds(H, H), rows(at)], E.at[c, pl.ds(H + X, H), rows(at)], sx + c, rx + c, xdown)

    def got_x(c):
        arrived(E.at[c, pl.ds(0, 4 * H), rows(0)], rx + c)

    def send_o(half):
        side = 1 - half
        src = jnp.where(half == 1, H + R - 1, H)
        dst = jnp.where(half == 1, 1, H + R)
        send(O.at[xi, src], O.at[xi, dst], so + 1 + side, ro + 1 + side, z_dev(half))

    own = pl.ds(H, R)

    def relay_o():
        arrived(O.at[xi, rows(lq)], ro)
        send_o(q)
        send(O.at[H + X - 1, own], O.at[H - 1, own], so + 3, ro + 3, xup)
        send(O.at[H, own], O.at[H + X, own], so + 4, ro + 4, xdown)

    level_load.wait()
    for x in range(X):
        for r in range(Y):
            row = dis[pl.ds(x * Y + r, 1), :].astype(F32)
            O[H + x, lo + r] = 16.5 * (row / F32(LEVELS - 1) - 0.5)
    stage_kept(0)
    pl.semaphore_wait(barrier, greeted)
    send(O.at[xi, rows(lo)], O.at[xi, rows(lo)], so, ro, yp)
    send_o(p)
    send_own_z(0)
    stage_away(0)
    send_y(0)
    send_x(0, lo)
    for c in range(1, S):
        stage_away(c)
        send_y(c)
        stage_kept(c)
        if c == 1:
            relay_o()
        if c < S - 1:
            send_own_z(c)
        send_x(c, lo)
    bound_load.wait()
    ritz_load.wait()
    for s in range(count):
        for x in range(X):
            for r in range(Y):
                RA[s + 1, x, r] = ritz[s, pl.ds(x * Y + r, NR, stride=J), :]
    send(RA.at[count], RA.at[0], sc, rc, cup)
    send(RA.at[1], RA.at[count + 1], sc, rc + 1, cdown)

    arrived(RA.at[0], rc)
    arrived(RA.at[count + 1], rc + 1)

    @pl.when(cut == 0)
    def _():
        RA[0] = jnp.zeros((X, Y, NR, NZ), F32)

    @pl.when(cut == nc - 1)
    def _():
        RA[count + 1] = jnp.zeros((X, Y, NR, NZ), F32)

    fresh = [[j for j in (c, c + 2) if j >= 2 or c < 2] for c in range(S)]
    fresh = [[j for j in js if j not in sum(fresh[:c], [])] for c, js in enumerate(fresh)]
    for c in range(S):
        for j in fresh[c]:
            send(RA.at[q * S + j], RQ.at[j], sr, rr + c, yp)

    def got_y(c):
        arrived(E.at[c, xi, rows(lq)], ry + c)

    last = R + 2 * H - 1
    ra = [a + p * (last - 2 * a) for a in range(last + 1)]
    near, far = H - 1, H + R

    def point(src, x, a, centre):
        v = src(x, a)
        beside = src(x + 1, a) + src(x - 1, a)
        beside = beside + src(x, a + 1) + src(x, a - 1)
        beside = beside + pltpu.roll(v, 1, 1) + pltpu.roll(v, NZ - 1, 1)
        level = jnp.broadcast_to(O[x, ra[a]] - centre, (NV, NZ))
        return level * v - beside

    def refs(c):
        s = p * S + c
        centre = (bnd[0, s] + bnd[1, s]) / 2.0

        def from_e(x, a):
            return E[c, x, ra[a]]

        def from_u(x, a):
            return U[c, x, ra[a]]

        def one(x, a):
            U[c, x, ra[a]] = point(from_e, x, a, centre)

        def two(x, a):
            return point(from_u, x, a, centre) * (2.0 / 256.0) - from_e(x, a)

        return one, two

    def corners(c, a, k):
        send(E.at[c, H + X - 1, ra[a]], E.at[c, H - 1, ra[a]], sk + c, rk + k, xup)
        send(E.at[c, H, ra[a]], E.at[c, H + X, ra[a]], sk + c, rk + k, xdown)

    def got_corners(c, k):
        arrived(E.at[c, pl.ds(0, 2), 0], rk + k)

    def early_corners(c):
        arrived(E.at[c, xi, rows(jnp.where(p == 1, 0, H + R))], rz + 4 * c)
        corners(c, far, 2 * c)

    def late_corners(c):
        arrived(E.at[c, pl.ds(0, 2), 0], rz + 4 * c + 1)
        corners(c, near, 2 * c + 1)

    def got_o():
        arrived(O.at[xi, H - 1], ro + 1)
        arrived(O.at[xi, H + R], ro + 2)
        arrived(O.at[H - 1, own], ro + 3)
        arrived(O.at[H + X, own], ro + 4)

    def early(c):
        one, two = refs(c)
        got_x(c)
        if c == 0:
            got_o()

        def inner(i):
            for a in range(H + 1, far + 1):
                one(H + 1 + i, a)

        loop(X - 2, 6, inner)
        for x in (H, H + X - 1):
            for a in range(H + 1, far):
                one(x, a)
        for x in (H - 1, H + X):
            for a in range(H + 1, far - 1):
                one(x, a)
        got_corners(c, 2 * c)
        for x in (H, H + X - 1):
            one(x, far)
        for x in (H - 1, H + X):
            one(x, far - 1)

        def outer(i):
            for a in range(H + Y, far):
                FT[c, i, ra[a] - lq] = two(H + i, a)

        loop(X, 8, outer)
        send(FT.at[c], FA.at[p * S + c], sf, rf + c, yp)

    def row_gram(c, a, two, acc, product=None):
        s, r = p * S + c, ra[a] - lo
        for i in range(0, X, 2):
            z = []
            for x in (i, i + 1):
                f = two(H + x, a)
                FA[s, x, r] = f
                z.append(jnp.concatenate([f, RA[s, x, r], RA[s + 2, x, r]], 0))
            acc = acc + (product or square)(z)
        return acc

    def late_near(c):
        one, two = refs(c)
        arrived(E.at[c, mid, ra[near]], rz + 4 * c + 2)
        for x in range(H, H + X):
            one(x, H)
        g = GS[c]
        for a in range(H + 1, H + Y):
            g = row_gram(c, a, two, g)
        g = jnp.concatenate([g, jnp.zeros((2 * NB, 128 - NB), F32)], 1)
        cross = jnp.concatenate([g[NB:], jnp.zeros((128 - NB, 128), F32)], 0)
        GT[c] = g[:NB] + (cross + cross.T)[:NB]

    def late_far(c):
        one, two = refs(c)
        arrived(E.at[c, xi, ra[near - 1]], rz + 4 * c + 3)
        for x in range(H + 1, H + X - 1):
            one(x, near)
        got_corners(c, 2 * c + 1)
        for x in (H, H + X - 1):
            one(x, near)
        for x in (H - 1, H + X):
            one(x, H)
        g = row_gram(c, H, two, jnp.zeros((NB, NB), F32), symmetric)
        gram_pack(c, GT[c] + jnp.concatenate([g, jnp.zeros((NB, 128 - NB), F32)], 1))

    def square(z):
        hi, lw = split(jnp.concatenate(z, 1))
        return lax.dot_general(jnp.concatenate([hi, lw], 0), hi, NT, preferred_element_type=F32)

    def symmetric(z):
        hi, lw = split(jnp.concatenate(z, 1))
        a = lax.dot_general(jnp.concatenate([hi, lw], 0), hi, NT, preferred_element_type=F32)
        return a[:NB] + a[NB:] + lax.dot_general(hi, lw, NT, preferred_element_type=F32)

    def product(f, w0, w1):
        def body(i, acc):
            for k in range(8):
                x = 8 * i + k
                z = [jnp.concatenate([f(x, r), w0(x, r), w1(x, r)], 0) for r in range(Y)]
                acc = acc + square(z)
            return acc

        return lax.fori_loop(0, X // 8, body, jnp.zeros((2 * NB, NB), F32))

    def gram_rest(c):
        arrived(RQ.at[pl.ds(0, len(fresh[c]))], rr + c)
        GS[c] = product(lambda x, r: FT[c, x, r], lambda x, r: RQ[c, x, r], lambda x, r: RQ[c + 2, x, r])

    def gram_pack(c, g):
        lane = lax.broadcasted_iota(jnp.int32, (8, 128), 1)
        t0 = jnp.zeros((8, 128), F32)
        t1 = jnp.zeros((8, 128), F32)
        for b_ in range(NV // 8):
            block = g[b_ * 8:b_ * 8 + 8]
            ff = jnp.where(lane < NV, block, 0.0)
            fw = jnp.where(lane >= NV, block, 0.0)
            t0 = t0 + (pltpu.roll(ff, b_ * NV, 1) if b_ else ff)
            t1 = t1 + pltpu.roll(fw, (128 - NV + b_ * NW) % 128, 1)
        for b_ in range(NW // 8):
            ww = jnp.where(lane >= NV, g[NV + b_ * 8:NV + b_ * 8 + 8], 0.0)
            t1 = t1 + pltpu.roll(ww, (128 - NV + (NV // 8 + b_) * NW) % 128, 1)
        PK[c, 0] = t0
        PK[c, 1] = t1

    def spread(k, src):
        cs = groups[k]
        part = pl.ds(cs[0], len(cs))
        bits = K.bit_length() - 1
        flips = direct and K == 1 << bits
        steps = [(dx, dz) for dz in reversed(range(K)) for dx in reversed(range(nx)) if dx or dz]
        for o in range(1, span):
            t = lax.rem(me + o, span)
            x, z = (t // K, lax.rem(t, K)) if direct else (mx, t)
            if flips:
                dx, dz = steps[o - 1]
                x = lax.rem(mx + dx, nx)
                z = sum(lax.rem(kz // (1 << b) + (dz >> b), 2) * (1 << b) for b in range(bits))
            send(src.at[part], RZ.at[me, part], sa + k, ra_ + k, (cut, x, z * 2 + p))

    def sum_start(k):
        cs = groups[k]
        part = pl.ds(cs[0], len(cs))
        for c in cs:
            if direct:
                RZ[me, c] = PK[c]
            else:
                RX[mx, c] = PK[c]
        if direct:
            spread(k, PK)
            return
        for o in range(1, nx):
            send(PK.at[part], RX.at[mx, part], sb + k, rb + k, (cut, lax.rem(mx + o, nx), my))

    def sum_more(k):
        if direct:
            return
        cs = groups[k]
        part = pl.ds(cs[0], len(cs))
        arrived(RX.at[pl.ds(0, nx - 1), part], rb + k)
        for c in cs:
            acc = RX[0, c]
            for t in range(1, nx):
                acc = acc + RX[t, c]
            SM[c] = acc
            RZ[kz, c] = acc
        spread(k, SM)

    e16r = lax.broadcasted_iota(jnp.int32, (NW, NW), 0)
    e16l = lax.broadcasted_iota(jnp.int32, (NW, NW), 1)
    l32 = lax.broadcasted_iota(jnp.int32, (NV, 128), 1)
    r32 = lax.broadcasted_iota(jnp.int32, (NV, 128), 0)
    eye = jnp.where(l32 == r32 + NV, 1.0, 0.0)

    line = lax.broadcasted_iota(jnp.int32, (NV, 1), 0)

    def strip(t, at):
        return pltpu.roll(t, 128 - at, 1) if at else t

    def cleaned(c):
        acc = RZ[0, c]
        for t in range(1, span):
            acc = acc + RZ[t, c]
        acc = acc * (1.0 / total)
        t0, t1 = acc[0], acc[1]
        ff = jnp.concatenate([strip(t0, b * NV) for b in range(NV // 8)], 0)
        fw = jnp.concatenate([strip(t1, b * NW) for b in range(NV // 8)], 0)
        ww = jnp.concatenate([strip(t1, NV // 8 * NW + b * NW) for b in range(NW // 8)], 0)
        b = jnp.where(e16r == e16l, 2.0, 0.0) - ww[:, :NW]
        fn = fw[:, :NW]
        fb = lax.dot_general(fn, b, NN, precision=HP, preferred_element_type=F32)
        sub = lax.dot_general(fb, fn, NT, precision=HP, preferred_element_type=F32)
        sub = jnp.concatenate([sub, jnp.zeros((NV, 128 - NV), F32)], 1)
        wide = jnp.where(l32 < NW, fw, 0.0)
        square_of = jnp.where(l32 == r32, ff, 0.0)
        by_row = 1.0 / jnp.sqrt(jnp.sum(square_of, axis=1, keepdims=True))
        by_lane = jnp.sum(square_of, axis=0, keepdims=True)
        by_lane = jnp.where(l32[:1] < NV, 1.0 / jnp.sqrt(by_lane), 1.0)
        M = jnp.where(l32 < NV, ff - sub, eye) - pltpu.roll(wide, 2 * NV, 1)
        return M * (by_row * by_lane), t1

    def pair(a, b, i, scale, ratio):
        p00, p01, p11 = a[i:i + 1], b[i:i + 1], b[i + 1:i + 2]
        inv = 1.0 / (p00 * p11 - p01 * p01)
        scale = jnp.where(line == i, 1.0 / jnp.sqrt(p00), jnp.where(line == i + 1, jnp.sqrt(p00 * inv), scale))
        ratio = jnp.where(line == i + 1, p01 / p00, ratio)
        return (lambda u, v: ((p11 * u - p01 * v) * inv, (p00 * v - p01 * u) * inv)), scale, ratio

    def eliminate(state, j):
        M, scale, ratio = state
        c = [jnp.broadcast_to(M[:, j + k:j + k + 1], (NV, 128)) for k in range(4)]
        r = [M[j + k:j + k + 1] for k in range(4)]
        solve, scale, ratio = pair(c[0], c[1], j, scale, ratio)
        g0, g1 = solve(r[0], r[1])
        for k in (2, 3):
            h0, h1 = solve(c[k][j:j + 1], c[k][j + 1:j + 2])
            r[k] = r[k] - c[0][j + k:j + k + 1] * g0 - c[1][j + k:j + k + 1] * g1
            c[k] = c[k] - c[0] * h0 - c[1] * h1
        solve, scale, ratio = pair(c[2], c[3], j + 2, scale, ratio)
        g2, g3 = solve(r[2], r[3])
        M = jnp.where(line > j + 1, M - c[0] * g0 - c[1] * g1, M)
        return jnp.where(line > j + 3, M - c[2] * g2 - c[3] * g3, M), scale, ratio

    def scaled(state):
        M, scale, ratio = state
        return pltpu.roll((M - ratio * pltpu.roll(M, 1, 0)) * scale, 128 - NV, 1)

    def factor(k):
        cs = groups[k]
        arrived(RZ.at[pl.ds(0, span - 1), pl.ds(cs[0], len(cs))], ra_ + k)
        both = [cleaned(c) for c in cs]
        blank = jnp.zeros((NV, 128), F32)
        mats = [(m, blank, blank) for m, _ in both]
        for j in range(0, NV, 4):
            mats = [eliminate(m, j) for m in mats]
        mats = [scaled(m) for m in mats]
        for i, c in enumerate(cs):
            low = jnp.where(l32 < NB, mats[i], 0.0)
            LP[c] = low[:NV // 2] + pltpu.roll(low[NV // 2:], 64, 1)
            send(LP.at[c], LR.at[c], sl, rl + c, yp)
        for i, c in enumerate(cs):
            LC[c] = both[i][1]
            LM[p * S + c] = mats[i][:, :NB]

    def unpacked(t1):
        return jnp.where(l32 < NW, jnp.concatenate([strip(t1, b * NW) for b in range(NV // 8)], 0), 0.0)

    def keep_corr(s, wide):
        cor[s] = jnp.concatenate([wide, jnp.zeros((128 - NV, 128), F32)], 0).T[:NW, :NV]

    def take(c):
        s = q * S + c
        arrived(LR.at[c], rl + c)
        half = LR[c]
        LM[s] = jnp.concatenate([half, pltpu.roll(half, 64, 1)], 0)[:, :NB]
        arrived(FA.at[s], rf + c)

    stored = []

    def store(src, dst, i):
        stored.append(load(src, dst, i))

    def finish(s, i):
        hi, lw = split(LM[s])
        left = jnp.concatenate([hi, lw], 0)
        left = jnp.concatenate([left, jnp.concatenate([hi, jnp.zeros((NV, NB), BF)], 0)], 1)

        def body(x):
            z = [jnp.concatenate([FA[s, x, r], RA[s, x, r], RA[s + 2, x, r]], 0) for r in range(Y)]
            zh, zl = split(jnp.concatenate(z, 1))
            o = lax.dot_general(left, jnp.concatenate([zh, zl], 0), NN, preferred_element_type=F32)
            o = o[:NV] + o[NV:]
            for r in range(Y):
                out[s, pl.ds(x * Y + r, NV, stride=J), :] = o[:, r * NZ:(r + 1) * NZ]

        loop(X, 8, body)
        store(out.at[s], out_h.at[s], i)

    def finish_own(c):
        finish(p * S + c, c)

    def finish_rest(c):
        take(c)
        finish(q * S + c, S + c)

    def settle():
        left(O.at[xi, rows(lo)], so)
        for k in range(2):
            left(O.at[xi, H], so + 1 + k)
            left(O.at[H, own], so + 3 + k)
        left(T, sy)
        left(RQ, sr)
        left(RA.at[pl.ds(0, 2)], sc)
        for c in range(S):
            left(E.at[c, xi, pl.ds(0, Y + 2)], sz + c)
            left(E.at[c, pl.ds(0, 4 * H), rows(0)], sx + c)
            left(E.at[c, pl.ds(0, 4), 0], sk + c)

    end = S - 1
    for c in range(S):
        got_y(c)
        send_rest_z(c)
        send_x(c, lq)
        if c == 0:
            send_own_z(end)
            early_corners(0)
        if c == 1:
            early_corners(1) if c < end else None
            early(0)
    for c in range(2, end):
        early_corners(c)
    late_corners(0)
    for c in range(1, end):
        early(c)
    gram_rest(0)
    late_near(0)
    early_corners(end)
    late_far(0)
    for c in range(1, end):
        gram_rest(c)
    early(end)
    for c in range(1, end):
        late_corners(c)
    gram_rest(end)
    for c in range(1, end):
        late_near(c)
        late_far(c)
    sum_start(0)
    late_corners(end)
    sum_more(0)
    late_near(end)
    late_far(end)
    sum_start(1)
    sum_more(1)
    settle()
    factor(0)
    factor(1)
    send(LC, LD, sd, rd, yp)
    for c in range(S):
        finish_own(c)
    for k in range(2):
        part = pl.ds(groups[k][0], len(groups[k]))
        if not direct:
            left(RX.at[pl.ds(0, nx - 1), part], sb + k)
        left(RZ.at[pl.ds(0, span - 1), part], sa + k)
    left(FT, sf)
    for c in range(end):
        finish_rest(c)
    for c in range(S):
        keep_corr(p * S + c, unpacked(LC[c]))
    finish_rest(end)
    arrived(LD, rd)
    for c in range(S):
        keep_corr(q * S + c, unpacked(LD[c]))
    store(cor, cor_h, 2 * S)
    for copy in stored:
        copy.wait()
    left(LP, sl)
    left(LC, sd)


def place(block, corr, block_out, corr_out, sem):
    copies = [pltpu.make_async_copy(block.at[s], block_out.at[s], sem.at[s]) for s in range(block.shape[0])]
    copies.append(pltpu.make_async_copy(corr, corr_out, sem.at[block.shape[0]]))
    for copy in copies:
        copy.start()
    for copy in copies:
        copy.wait()


def on_device(disorder, slice_bounds, start, ritz):
    nc, nx, ny = (lax.axis_size(a) for a in ("cuts", "lx", "ly"))
    count, NV, X, Y, NZ = start.shape
    NR = ritz.shape[1]
    J = X * Y
    S, R, K = count // 2, 2 * Y, ny // 2
    V = pltpu.VMEM
    D = pltpu.SemaphoreType.DMA
    dims = (nc, nx, ny, count, NV, NR, X, Y, NZ)
    hbm = pl.BlockSpec(memory_space=pl.ANY)
    sends, receives = sem_counts(nx, K, S)
    block, corr = pl.pallas_call(
        functools.partial(kernel, dims),
        out_shape=(jax.ShapeDtypeStruct((count, NV * J, NZ), F32),
                   jax.ShapeDtypeStruct((count, 2 * NR, NV), F32)),
        in_specs=[hbm] * 4,
        out_specs=(hbm, hbm),
        scratch_shapes=[
            V((count, NV * J, NZ), F32),
            V((count, 2 * NR, NV), F32),
            pltpu.SMEM((2, count), F32),
            V((J, NZ), jnp.int32),
            V((count, NV * J, NZ), F32),
            V((count, NR * J, NZ), F32),
            D((2 * S + 3,)),
            V((S, X + 2 * H, R + 2 * H, NV, NZ), F32),
            V((S, X, Y, NV, NZ), F32),
            V((X + 2 * H, R + 2 * H, 1, NZ), F32),
            V((S, X + 2 * H, R + 2 * H, NV, NZ), F32),
            V((count, X, Y, NV, NZ), F32),
            V((S, X, Y, NV, NZ), F32),
            V((count + 2, X, Y, NR, NZ), F32),
            V((S + 2, X, Y, NR, NZ), F32),
            V((S, 2 * (NV + 2 * NR), NV + 2 * NR), F32),
            V((S, NV + 2 * NR, 128), F32),
            V((S, 2, 8, 128), F32),
            V((nx, S, 2, 8, 128), F32),
            V((S, 2, 8, 128), F32),
            V((nx * K if direct_sum(nx, K) else K, S, 2, 8, 128), F32),
            V((count, NV, NV + 2 * NR), F32),
            V((S, NV // 2, 128), F32),
            V((S, NV // 2, 128), F32),
            V((S, 8, 128), F32),
            V((S, 8, 128), F32),
            D((sends,)), D((receives,)),
        ],
        compiler_params=pltpu.CompilerParams(collective_id=0, has_side_effects=True, vmem_limit_bytes=48 << 20),
    )(*[pltpu.with_memory_space_constraint(a, pltpu.HBM) for a in (
        disorder.reshape(J, NZ), slice_bounds.T, start.reshape(count, NV * J, NZ), ritz.reshape(count, NR * J, NZ))])
    block, corr = pl.pallas_call(
        place,
        out_shape=(jax.ShapeDtypeStruct(block.shape, F32), jax.ShapeDtypeStruct(corr.shape, F32)),
        in_specs=[hbm] * 2,
        out_specs=(hbm, hbm),
        scratch_shapes=[D((count + 1,))],
        compiler_params=pltpu.CompilerParams(vmem_limit_bytes=1 << 20),
    )(block, corr)
    return (block.reshape(start.shape), corr)


def solution(mesh):
    in_specs = (
        P("lx", "ly", None),
        P("cuts", None),
        P("cuts", None, "lx", "ly", None),
        P("cuts", None, "lx", "ly", None),
    )
    out_specs = (P("cuts", None, "lx", "ly", None), P("cuts", None, None))
    return jax.shard_map(
        on_device, mesh=mesh, in_specs=in_specs, out_specs=out_specs, check_vma=False
    )
```

```python
import functools

import jax
import jax.numpy as jnp
from jax import lax
from jax.experimental import pallas as pl
from jax.experimental.pallas import tpu as pltpu
from jax.sharding import PartitionSpec as P

LEVELS = 256
MESH = pl.DeviceIdType.MESH
HP = lax.Precision.HIGHEST
H = 2
BF = jnp.bfloat16
F32 = jnp.float32
NT = (((1,), (1,)), ((), ()))
NN = (((1,), (0,)), ((), ()))
TN = (((0,), (0,)), ((), ()))


def direct_sum(nx, K):
    return nx * K <= 16


def sem_counts(nx, K, S):
    more = 0 if direct_sum(nx, K) else 2
    return 14 + 3 * S + more, 11 + 11 * S + more


def split(z):
    hi = z.astype(BF)
    return hi, (z - hi.astype(F32)).astype(BF)


def loop(n, unroll, body):
    def step(i, carry):
        for k in range(unroll):
            body(i * unroll + k)
        return carry

    if n % unroll:
        unroll = 1
    lax.fori_loop(0, n // unroll, step, 0)


def kernel(dims, dis_h, bnd_h, start_h, ritz_h, out_h, cor_h, out, cor, bnd, dis, start, ritz, ls, E, T, O, U, FA, FT,
           RA, RQ, GS, GT, PK, RX, SM, RZ, LM, LP, LR, LC, LD, ss, rs):
    nc, nx, ny, count, NV, NR, X, Y, NZ = dims
    S = count // 2
    R = 2 * Y
    J = X * Y
    K = ny // 2
    total = float(J * NZ * nx * ny)
    NW = 2 * NR
    NB = NV + NW
    cut, mx, my = lax.axis_index("cuts"), lax.axis_index("lx"), lax.axis_index("ly")
    p = lax.rem(my, 2)
    q = 1 - p
    kz = my // 2
    yp = (cut, mx, kz * 2 + q)
    zup = (cut, mx, lax.rem(kz + 1, K) * 2 + p)
    zdown = (cut, mx, lax.rem(kz + K - 1, K) * 2 + p)
    xup = (cut, lax.rem(mx + 1, nx), my)
    xdown = (cut, lax.rem(mx + nx - 1, nx), my)
    cup = (lax.rem(cut + 1, nc), mx, my)
    cdown = (lax.rem(cut + nc - 1, nc), mx, my)

    def load(src, dst, i):
        copy = pltpu.make_async_copy(src, dst, ls.at[i])
        copy.start()
        return copy

    barrier = pltpu.get_barrier_semaphore()

    def greet(dev):
        pl.semaphore_signal(barrier, inc=1, device_id=dev, device_id_type=MESH)

    greet(yp)
    if direct_sum(nx, K):
        for o in range(1, nx * K):
            t = lax.rem(mx * K + kz + o, nx * K)
            greet((cut, t // K, lax.rem(t, K) * 2 + p))
        greeted = nx * K + 2
    else:
        for o in range(1, nx):
            greet((cut, lax.rem(mx + o, nx), my))
        for o in range(1, K):
            greet((cut, mx, lax.rem(kz + o, K) * 2 + p))
        greeted = nx + K + 1
    greet(cup)
    greet(cdown)

    away, kept = [], []
    for c in range(S):
        kept.append(load(start_h.at[p * S + c], start.at[S + c], S + c))
        if c == 0:
            level_load = load(dis_h, dis, 2 * S)
        away.append(load(start_h.at[q * S + c], start.at[c], c))
    bound_load = load(bnd_h, bnd, 2 * S + 2)
    ritz_load = load(ritz_h, ritz, 2 * S + 1)

    lo = H + Y * p
    lq = H + Y * q
    xi = pl.ds(H, X)
    mid = pl.ds(H + 1, X - 2)
    def stage_away(c):
        away[c].wait()
        for x in range(X):
            for r in range(Y):
                T[c, x, r] = start[c, pl.ds(x * Y + r, NV, stride=J), :]

    def stage_kept(c):
        kept[c].wait()
        for x in range(X):
            for r in range(Y):
                E[c, H + x, lo + r] = start[S + c, pl.ds(x * Y + r, NV, stride=J), :]

    used = [0, 0]

    def take_slots(kind, n=1):
        i = used[kind]
        used[kind] += n
        return i

    def send(src, dst, i, j, dev):
        pltpu.make_async_remote_copy(
            src_ref=src, dst_ref=dst, send_sem=ss.at[i], recv_sem=rs.at[j], device_id=dev, device_id_type=MESH).start()

    def left(src, i):
        pltpu.make_async_remote_copy(
            src_ref=src, dst_ref=src, send_sem=ss.at[i], recv_sem=ss.at[i],
            device_id=yp, device_id_type=MESH).wait_send()

    def arrived(dst, j):
        pltpu.make_async_remote_copy(
            src_ref=dst, dst_ref=dst, send_sem=rs.at[j], recv_sem=rs.at[j],
            device_id=yp, device_id_type=MESH).wait_recv()

    def rows(at):
        return pl.ds(at, Y)

    so, sy, sf, sl, sr, sc, sd = (take_slots(0, n) for n in (5, 1, 1, 1, 1, 1, 2))
    sz, sx, sk, sa = (take_slots(0, n) for n in (S, S, S, 2))
    ro, ry, rf, rl, rx, rc, rr, ra_, rd = (take_slots(1, n) for n in (5, S, S, S, S, 2, S, 2, 2))
    rz, rk = take_slots(1, 4 * S), take_slots(1, 2 * S)
    groups = [list(range(S - 1)), [S - 1]]
    direct = direct_sum(nx, K)
    span = nx * K if direct else K
    me = mx * K + kz if direct else kz
    sb, rb = (0, 0) if direct else (take_slots(0, 2), take_slots(1, 2))

    def send_y(c):
        send(T.at[c], E.at[c, xi, rows(lo)], sy, ry + c, yp)

    def z_dev(half):
        return (cut, mx, jnp.where(half == 1, zup[2], zdown[2]))

    def send_own_z(c):
        dst = jnp.where(p == 1, 0, H + R)
        send(E.at[c, xi, rows(lo)], E.at[c, xi, rows(dst)], sz + c, rz + 4 * c, z_dev(p))

    def send_rest_z(c):
        src = [jnp.where(q == 1, H + R - 1 - k, H + k) for k in range(2)]
        dst = [jnp.where(q == 1, H - 1 - k, H + R + k) for k in range(2)]
        for x in (H, H + X - 1):
            send(E.at[c, x, src[0]], E.at[c, x, dst[0]], sz + c, rz + 4 * c + 1, z_dev(q))
        send(E.at[c, mid, src[0]], E.at[c, mid, dst[0]], sz + c, rz + 4 * c + 2, z_dev(q))
        send(E.at[c, xi, src[1]], E.at[c, xi, dst[1]], sz + c, rz + 4 * c + 3, z_dev(q))

    def send_x(c, at):
        send(E.at[c, pl.ds(X, H), rows(at)], E.at[c, pl.ds(0, H), rows(at)], sx + c, rx + c, xup)
        send(E.at[c, pl.ds(H, H), rows(at)], E.at[c, pl.ds(H + X, H), rows(at)], sx + c, rx + c, xdown)

    def got_x(c):
        arrived(E.at[c, pl.ds(0, 4 * H), rows(0)], rx + c)

    def send_o(half):
        side = 1 - half
        src = jnp.where(half == 1, H + R - 1, H)
        dst = jnp.where(half == 1, 1, H + R)
        send(O.at[xi, src], O.at[xi, dst], so + 1 + side, ro + 1 + side, z_dev(half))

    own = pl.ds(H, R)

    def relay_o():
        arrived(O.at[xi, rows(lq)], ro)
        send_o(q)
        send(O.at[H + X - 1, own], O.at[H - 1, own], so + 3, ro + 3, xup)
        send(O.at[H, own], O.at[H + X, own], so + 4, ro + 4, xdown)

    level_load.wait()
    for x in range(X):
        for r in range(Y):
            row = dis[pl.ds(x * Y + r, 1), :].astype(F32)
            O[H + x, lo + r] = 16.5 * (row / F32(LEVELS - 1) - 0.5)
    stage_kept(0)
    pl.semaphore_wait(barrier, greeted)
    send(O.at[xi, rows(lo)], O.at[xi, rows(lo)], so, ro, yp)
    send_o(p)
    send_own_z(0)
    stage_away(0)
    send_y(0)
    send_x(0, lo)
    for c in range(1, S):
        stage_away(c)
        send_y(c)
        stage_kept(c)
        if c == 1:
            relay_o()
        if c < S - 1:
            send_own_z(c)
        send_x(c, lo)
    bound_load.wait()
    ritz_load.wait()
    for s in range(count):
        for x in range(X):
            for r in range(Y):
                RA[s + 1, x, r] = ritz[s, pl.ds(x * Y + r, NR, stride=J), :]
    send(RA.at[count], RA.at[0], sc, rc, cup)
    send(RA.at[1], RA.at[count + 1], sc, rc + 1, cdown)

    arrived(RA.at[0], rc)
    arrived(RA.at[count + 1], rc + 1)

    @pl.when(cut == 0)
    def _():
        RA[0] = jnp.zeros((X, Y, NR, NZ), F32)

    @pl.when(cut == nc - 1)
    def _():
        RA[count + 1] = jnp.zeros((X, Y, NR, NZ), F32)

    fresh = [[j for j in (c, c + 2) if j >= 2 or c < 2] for c in range(S)]
    fresh = [[j for j in js if j not in sum(fresh[:c], [])] for c, js in enumerate(fresh)]
    for c in range(S):
        for j in fresh[c]:
            send(RA.at[q * S + j], RQ.at[j], sr, rr + c, yp)

    def got_y(c):
        arrived(E.at[c, xi, rows(lq)], ry + c)

    last = R + 2 * H - 1
    ra = [a + p * (last - 2 * a) for a in range(last + 1)]
    near, far = H - 1, H + R

    def point(src, x, a, centre):
        v = src(x, a)
        beside = src(x + 1, a) + src(x - 1, a)
        beside = beside + src(x, a + 1) + src(x, a - 1)
        beside = beside + pltpu.roll(v, 1, 1) + pltpu.roll(v, NZ - 1, 1)
        level = jnp.broadcast_to(O[x, ra[a]] - centre, (NV, NZ))
        return level * v - beside

    def refs(c):
        s = p * S + c
        centre = (bnd[0, s] + bnd[1, s]) / 2.0

        def from_e(x, a):
            return E[c, x, ra[a]]

        def from_u(x, a):
            return U[c, x, ra[a]]

        def one(x, a):
            U[c, x, ra[a]] = point(from_e, x, a, centre)

        def two(x, a):
            return point(from_u, x, a, centre) * (2.0 / 256.0) - from_e(x, a)

        return one, two

    def corners(c, a, k):
        send(E.at[c, H + X - 1, ra[a]], E.at[c, H - 1, ra[a]], sk + c, rk + k, xup)
        send(E.at[c, H, ra[a]], E.at[c, H + X, ra[a]], sk + c, rk + k, xdown)

    def got_corners(c, k):
        arrived(E.at[c, pl.ds(0, 2), 0], rk + k)

    def early_corners(c):
        arrived(E.at[c, xi, rows(jnp.where(p == 1, 0, H + R))], rz + 4 * c)
        corners(c, far, 2 * c)

    def late_corners(c):
        arrived(E.at[c, pl.ds(0, 2), 0], rz + 4 * c + 1)
        corners(c, near, 2 * c + 1)

    def got_o():
        arrived(O.at[xi, H - 1], ro + 1)
        arrived(O.at[xi, H + R], ro + 2)
        arrived(O.at[H - 1, own], ro + 3)
        arrived(O.at[H + X, own], ro + 4)

    def early(c):
        one, two = refs(c)
        got_x(c)
        if c == 0:
            got_o()

        def inner(i):
            for a in range(H + 1, far + 1):
                one(H + 1 + i, a)

        loop(X - 2, 6, inner)
        for x in (H, H + X - 1):
            for a in range(H + 1, far):
                one(x, a)
        for x in (H - 1, H + X):
            for a in range(H + 1, far - 1):
                one(x, a)
        got_corners(c, 2 * c)
        for x in (H, H + X - 1):
            one(x, far)
        for x in (H - 1, H + X):
            one(x, far - 1)

        def outer(i):
            for a in range(H + Y, far):
                FT[c, i, ra[a] - lq] = two(H + i, a)

        loop(X, 8, outer)
        send(FT.at[c], FA.at[p * S + c], sf, rf + c, yp)

    def row_gram(c, a, two, acc, product=None):
        s, r = p * S + c, ra[a] - lo
        for i in range(0, X, 2):
            z = []
            for x in (i, i + 1):
                f = two(H + x, a)
                FA[s, x, r] = f
                z.append(jnp.concatenate([f, RA[s, x, r], RA[s + 2, x, r]], 0))
            acc = acc + (product or square)(z)
        return acc

    def late_near(c):
        one, two = refs(c)
        arrived(E.at[c, mid, ra[near]], rz + 4 * c + 2)
        for x in range(H, H + X):
            one(x, H)
        g = GS[c]
        for a in range(H + 1, H + Y):
            g = row_gram(c, a, two, g)
        g = jnp.concatenate([g, jnp.zeros((2 * NB, 128 - NB), F32)], 1)
        cross = jnp.concatenate([g[NB:], jnp.zeros((128 - NB, 128), F32)], 0)
        GT[c] = g[:NB] + (cross + cross.T)[:NB]

    def late_far(c):
        one, two = refs(c)
        arrived(E.at[c, xi, ra[near - 1]], rz + 4 * c + 3)
        for x in range(H + 1, H + X - 1):
            one(x, near)
        got_corners(c, 2 * c + 1)
        for x in (H, H + X - 1):
            one(x, near)
        for x in (H - 1, H + X):
            one(x, H)
        g = row_gram(c, H, two, jnp.zeros((NB, NB), F32), symmetric)
        gram_pack(c, GT[c] + jnp.concatenate([g, jnp.zeros((NB, 128 - NB), F32)], 1))

    def square(z):
        hi, lw = split(jnp.concatenate(z, 1))
        return lax.dot_general(jnp.concatenate([hi, lw], 0), hi, NT, preferred_element_type=F32)

    def symmetric(z):
        hi, lw = split(jnp.concatenate(z, 1))
        a = lax.dot_general(jnp.concatenate([hi, lw], 0), hi, NT, preferred_element_type=F32)
        return a[:NB] + a[NB:] + lax.dot_general(hi, lw, NT, preferred_element_type=F32)

    def product(f, w0, w1):
        def body(i, acc):
            for k in range(8):
                x = 8 * i + k
                z = [jnp.concatenate([f(x, r), w0(x, r), w1(x, r)], 0) for r in range(Y)]
                acc = acc + square(z)
            return acc

        return lax.fori_loop(0, X // 8, body, jnp.zeros((2 * NB, NB), F32))

    def gram_rest(c):
        arrived(RQ.at[pl.ds(0, len(fresh[c]))], rr + c)
        GS[c] = product(lambda x, r: FT[c, x, r], lambda x, r: RQ[c, x, r], lambda x, r: RQ[c + 2, x, r])

    def gram_pack(c, g):
        lane = lax.broadcasted_iota(jnp.int32, (8, 128), 1)
        t0 = jnp.zeros((8, 128), F32)
        t1 = jnp.zeros((8, 128), F32)
        for b_ in range(NV // 8):
            block = g[b_ * 8:b_ * 8 + 8]
            ff = jnp.where(lane < NV, block, 0.0)
            fw = jnp.where(lane >= NV, block, 0.0)
            t0 = t0 + (pltpu.roll(ff, b_ * NV, 1) if b_ else ff)
            t1 = t1 + pltpu.roll(fw, (128 - NV + b_ * NW) % 128, 1)
        for b_ in range(NW // 8):
            ww = jnp.where(lane >= NV, g[NV + b_ * 8:NV + b_ * 8 + 8], 0.0)
            t1 = t1 + pltpu.roll(ww, (128 - NV + (NV // 8 + b_) * NW) % 128, 1)
        PK[c, 0] = t0
        PK[c, 1] = t1

    def spread(k, src):
        cs = groups[k]
        part = pl.ds(cs[0], len(cs))
        bits = K.bit_length() - 1
        flips = direct and K == 1 << bits
        steps = [(dx, dz) for dz in reversed(range(K)) for dx in reversed(range(nx)) if dx or dz]
        for o in range(1, span):
            t = lax.rem(me + o, span)
            x, z = (t // K, lax.rem(t, K)) if direct else (mx, t)
            if flips:
                dx, dz = steps[o - 1]
                x = lax.rem(mx + dx, nx)
                z = sum(lax.rem(kz // (1 << b) + (dz >> b), 2) * (1 << b) for b in range(bits))
            send(src.at[part], RZ.at[me, part], sa + k, ra_ + k, (cut, x, z * 2 + p))

    def sum_start(k):
        cs = groups[k]
        part = pl.ds(cs[0], len(cs))
        for c in cs:
            if direct:
                RZ[me, c] = PK[c]
            else:
                RX[mx, c] = PK[c]
        if direct:
            spread(k, PK)
            return
        for o in range(1, nx):
            send(PK.at[part], RX.at[mx, part], sb + k, rb + k, (cut, lax.rem(mx + o, nx), my))

    def sum_more(k):
        if direct:
            return
        cs = groups[k]
        part = pl.ds(cs[0], len(cs))
        arrived(RX.at[pl.ds(0, nx - 1), part], rb + k)
        for c in cs:
            acc = RX[0, c]
            for t in range(1, nx):
                acc = acc + RX[t, c]
            SM[c] = acc
            RZ[kz, c] = acc
        spread(k, SM)

    e16r = lax.broadcasted_iota(jnp.int32, (NW, NW), 0)
    e16l = lax.broadcasted_iota(jnp.int32, (NW, NW), 1)
    l32 = lax.broadcasted_iota(jnp.int32, (NV, 128), 1)
    r32 = lax.broadcasted_iota(jnp.int32, (NV, 128), 0)
    eye = jnp.where(l32 == r32 + NV, 1.0, 0.0)

    line = lax.broadcasted_iota(jnp.int32, (NV, 1), 0)

    def strip(t, at):
        return pltpu.roll(t, 128 - at, 1) if at else t

    def cleaned(c):
        acc = RZ[0, c]
        for t in range(1, span):
            acc = acc + RZ[t, c]
        acc = acc * (1.0 / total)
        t0, t1 = acc[0], acc[1]
        ff = jnp.concatenate([strip(t0, b * NV) for b in range(NV // 8)], 0)
        fw = jnp.concatenate([strip(t1, b * NW) for b in range(NV // 8)], 0)
        ww = jnp.concatenate([strip(t1, NV // 8 * NW + b * NW) for b in range(NW // 8)], 0)
        b = jnp.where(e16r == e16l, 2.0, 0.0) - ww[:, :NW]
        fn = fw[:, :NW]
        fb = lax.dot_general(fn, b, NN, precision=HP, preferred_element_type=F32)
        sub = lax.dot_general(fb, fn, NT, precision=HP, preferred_element_type=F32)
        sub = jnp.concatenate([sub, jnp.zeros((NV, 128 - NV), F32)], 1)
        wide = jnp.where(l32 < NW, fw, 0.0)
        square_of = jnp.where(l32 == r32, ff, 0.0)
        by_row = 1.0 / jnp.sqrt(jnp.sum(square_of, axis=1, keepdims=True))
        by_lane = jnp.sum(square_of, axis=0, keepdims=True)
        by_lane = jnp.where(l32[:1] < NV, 1.0 / jnp.sqrt(by_lane), 1.0)
        M = jnp.where(l32 < NV, ff - sub, eye) - pltpu.roll(wide, 2 * NV, 1)
        return M * (by_row * by_lane), t1

    def pair(a, b, i, scale, ratio):
        p00, p01, p11 = a[i:i + 1], b[i:i + 1], b[i + 1:i + 2]
        inv = 1.0 / (p00 * p11 - p01 * p01)
        scale = jnp.where(line == i, 1.0 / jnp.sqrt(p00), jnp.where(line == i + 1, jnp.sqrt(p00 * inv), scale))
        ratio = jnp.where(line == i + 1, p01 / p00, ratio)
        return (lambda u, v: ((p11 * u - p01 * v) * inv, (p00 * v - p01 * u) * inv)), scale, ratio

    def eliminate(state, j):
        M, scale, ratio = state
        c = [jnp.broadcast_to(M[:, j + k:j + k + 1], (NV, 128)) for k in range(4)]
        r = [M[j + k:j + k + 1] for k in range(4)]
        solve, scale, ratio = pair(c[0], c[1], j, scale, ratio)
        g0, g1 = solve(r[0], r[1])
        for k in (2, 3):
            h0, h1 = solve(c[k][j:j + 1], c[k][j + 1:j + 2])
            r[k] = r[k] - c[0][j + k:j + k + 1] * g0 - c[1][j + k:j + k + 1] * g1
            c[k] = c[k] - c[0] * h0 - c[1] * h1
        solve, scale, ratio = pair(c[2], c[3], j + 2, scale, ratio)
        g2, g3 = solve(r[2], r[3])
        M = jnp.where(line > j + 1, M - c[0] * g0 - c[1] * g1, M)
        return jnp.where(line > j + 3, M - c[2] * g2 - c[3] * g3, M), scale, ratio

    def scaled(state):
        M, scale, ratio = state
        return pltpu.roll((M - ratio * pltpu.roll(M, 1, 0)) * scale, 128 - NV, 1)

    def factor(k):
        cs = groups[k]
        arrived(RZ.at[pl.ds(0, span - 1), pl.ds(cs[0], len(cs))], ra_ + k)
        both = [cleaned(c) for c in cs]
        blank = jnp.zeros((NV, 128), F32)
        mats = [(m, blank, blank) for m, _ in both]
        for j in range(0, NV, 4):
            mats = [eliminate(m, j) for m in mats]
        mats = [scaled(m) for m in mats]
        for i, c in enumerate(cs):
            low = jnp.where(l32 < NB, mats[i], 0.0)
            LP[c] = low[:NV // 2] + pltpu.roll(low[NV // 2:], 64, 1)
            send(LP.at[c], LR.at[c], sl, rl + c, yp)
        for i, c in enumerate(cs):
            LC[c] = both[i][1]
            LM[p * S + c] = mats[i][:, :NB]
        part = pl.ds(cs[0], len(cs))
        send(LC.at[part], LD.at[part], sd + k, rd + k, yp)

    def unpacked(t1):
        return jnp.where(l32 < NW, jnp.concatenate([strip(t1, b * NW) for b in range(NV // 8)], 0), 0.0)

    def keep_corr(s, wide):
        cor[s] = jnp.concatenate([wide, jnp.zeros((128 - NV, 128), F32)], 0).T[:NW, :NV]

    def take(c):
        s = q * S + c
        arrived(LR.at[c], rl + c)
        half = LR[c]
        LM[s] = jnp.concatenate([half, pltpu.roll(half, 64, 1)], 0)[:, :NB]
        arrived(FA.at[s], rf + c)

    stored = []

    def store(src, dst, i):
        stored.append(load(src, dst, i))

    def finish(s, i):
        hi, lw = split(LM[s])
        left = jnp.concatenate([hi, lw], 0)
        left = jnp.concatenate([left, jnp.concatenate([hi, jnp.zeros((NV, NB), BF)], 0)], 1)

        def body(x):
            z = [jnp.concatenate([FA[s, x, r], RA[s, x, r], RA[s + 2, x, r]], 0) for r in range(Y)]
            zh, zl = split(jnp.concatenate(z, 1))
            o = lax.dot_general(left, jnp.concatenate([zh, zl], 0), NN, preferred_element_type=F32)
            o = o[:NV] + o[NV:]
            for r in range(Y):
                out[s, pl.ds(x * Y + r, NV, stride=J), :] = o[:, r * NZ:(r + 1) * NZ]

        loop(X, 8, body)
        store(out.at[s], out_h.at[s], i)

    def finish_own(c):
        finish(p * S + c, c)

    def finish_rest(c):
        take(c)
        finish(q * S + c, S + c)

    def settle():
        left(O.at[xi, rows(lo)], so)
        for k in range(2):
            left(O.at[xi, H], so + 1 + k)
            left(O.at[H, own], so + 3 + k)
        left(T, sy)
        left(RQ, sr)
        left(RA.at[pl.ds(0, 2)], sc)
        for c in range(S):
            left(E.at[c, xi, pl.ds(0, Y + 2)], sz + c)
            left(E.at[c, pl.ds(0, 4 * H), rows(0)], sx + c)
            left(E.at[c, pl.ds(0, 4), 0], sk + c)

    end = S - 1
    for c in range(S):
        got_y(c)
        send_rest_z(c)
        send_x(c, lq)
        if c == 0:
            send_own_z(end)
            early_corners(0)
        if c == 1:
            early_corners(1) if c < end else None
            early(0)
    for c in range(2, end):
        early_corners(c)
    late_corners(0)
    for c in range(1, end):
        early(c)
    gram_rest(0)
    late_near(0)
    early_corners(end)
    late_far(0)
    for c in range(1, end):
        gram_rest(c)
    early(end)
    for c in range(1, end):
        late_corners(c)
    gram_rest(end)
    for c in range(1, end):
        late_near(c)
        late_far(c)
    sum_start(0)
    late_corners(end)
    sum_more(0)
    late_near(end)
    late_far(end)
    sum_start(1)
    sum_more(1)
    settle()
    factor(0)
    factor(1)
    for c in range(S):
        finish_own(c)
    for k in range(2):
        part = pl.ds(groups[k][0], len(groups[k]))
        if not direct:
            left(RX.at[pl.ds(0, nx - 1), part], sb + k)
        left(RZ.at[pl.ds(0, span - 1), part], sa + k)
    left(FT, sf)
    for c in range(end):
        finish_rest(c)
    for c in range(S):
        keep_corr(p * S + c, unpacked(LC[c]))
    arrived(LD.at[pl.ds(0, end)], rd)
    for c in range(end):
        keep_corr(q * S + c, unpacked(LD[c]))
    finish_rest(end)
    arrived(LD.at[pl.ds(end, 1)], rd + 1)
    keep_corr(q * S + end, unpacked(LD[end]))
    store(cor, cor_h, 2 * S)
    for copy in stored:
        copy.wait()
    left(LP, sl)
    left(LC.at[pl.ds(0, end)], sd)
    left(LC.at[pl.ds(end, 1)], sd + 1)


def place(block, corr, block_out, corr_out, sem):
    copies = [pltpu.make_async_copy(block.at[s], block_out.at[s], sem.at[s]) for s in range(block.shape[0])]
    copies.append(pltpu.make_async_copy(corr, corr_out, sem.at[block.shape[0]]))
    for copy in copies:
        copy.start()
    for copy in copies:
        copy.wait()


def on_device(disorder, slice_bounds, start, ritz):
    nc, nx, ny = (lax.axis_size(a) for a in ("cuts", "lx", "ly"))
    count, NV, X, Y, NZ = start.shape
    NR = ritz.shape[1]
    J = X * Y
    S, R, K = count // 2, 2 * Y, ny // 2
    V = pltpu.VMEM
    D = pltpu.SemaphoreType.DMA
    dims = (nc, nx, ny, count, NV, NR, X, Y, NZ)
    hbm = pl.BlockSpec(memory_space=pl.ANY)
    sends, receives = sem_counts(nx, K, S)
    block, corr = pl.pallas_call(
        functools.partial(kernel, dims),
        out_shape=(jax.ShapeDtypeStruct((count, NV * J, NZ), F32),
                   jax.ShapeDtypeStruct((count, 2 * NR, NV), F32)),
        in_specs=[hbm] * 4,
        out_specs=(hbm, hbm),
        scratch_shapes=[
            V((count, NV * J, NZ), F32),
            V((count, 2 * NR, NV), F32),
            pltpu.SMEM((2, count), F32),
            V((J, NZ), jnp.int32),
            V((count, NV * J, NZ), F32),
            V((count, NR * J, NZ), F32),
            D((2 * S + 3,)),
            V((S, X + 2 * H, R + 2 * H, NV, NZ), F32),
            V((S, X, Y, NV, NZ), F32),
            V((X + 2 * H, R + 2 * H, 1, NZ), F32),
            V((S, X + 2 * H, R + 2 * H, NV, NZ), F32),
            V((count, X, Y, NV, NZ), F32),
            V((S, X, Y, NV, NZ), F32),
            V((count + 2, X, Y, NR, NZ), F32),
            V((S + 2, X, Y, NR, NZ), F32),
            V((S, 2 * (NV + 2 * NR), NV + 2 * NR), F32),
            V((S, NV + 2 * NR, 128), F32),
            V((S, 2, 8, 128), F32),
            V((nx, S, 2, 8, 128), F32),
            V((S, 2, 8, 128), F32),
            V((nx * K if direct_sum(nx, K) else K, S, 2, 8, 128), F32),
            V((count, NV, NV + 2 * NR), F32),
            V((S, NV // 2, 128), F32),
            V((S, NV // 2, 128), F32),
            V((S, 8, 128), F32),
            V((S, 8, 128), F32),
            D((sends,)), D((receives,)),
        ],
        compiler_params=pltpu.CompilerParams(collective_id=0, has_side_effects=True, vmem_limit_bytes=48 << 20),
    )(*[pltpu.with_memory_space_constraint(a, pltpu.HBM) for a in (
        disorder.reshape(J, NZ), slice_bounds.T, start.reshape(count, NV * J, NZ), ritz.reshape(count, NR * J, NZ))])
    block, corr = pl.pallas_call(
        place,
        out_shape=(jax.ShapeDtypeStruct(block.shape, F32), jax.ShapeDtypeStruct(corr.shape, F32)),
        in_specs=[hbm] * 2,
        out_specs=(hbm, hbm),
        scratch_shapes=[D((count + 1,))],
        compiler_params=pltpu.CompilerParams(vmem_limit_bytes=1 << 20),
    )(block, corr)
    return (block.reshape(start.shape), corr)


def solution(mesh):
    in_specs = (
        P("lx", "ly", None),
        P("cuts", None),
        P("cuts", None, "lx", "ly", None),
        P("cuts", None, "lx", "ly", None),
    )
    out_specs = (P("cuts", None, "lx", "ly", None), P("cuts", None, None))
    return jax.shard_map(
        on_device, mesh=mesh, in_specs=in_specs, out_specs=out_specs, check_vma=False
    )
```
